512 devices in a mesh: lat: 16 (over x, y_lo, core), lon: 32 (over y_hi, z).
Axes of the slice: x: 4, y: 4 (y_hi: 2, y_lo: 2; y = y_hi * 2 + y_lo), z: 16, core: 2. Of those that a mesh axis runs over, the one named last changes fastest.
Arguments:
- tracer: float32 [64, 1440, 864], P('lat', 'lon'), may hold values from 1 to 9
- east_courant: float32 [64, 1440, 32], P('lat', 'lon'), may hold values from -0.3 to 0.3
- north_courant: float32 [64, 1440, 32], P('lat', 'lon'), may hold values from -0.3 to 0.3
- east_limiter: int32 [64, 1440, 32], P('lat', 'lon'), may hold values from 0 to 2
- north_limiter: int32 [64, 1440, 32], P('lat', 'lon'), may hold values from 0 to 2
- filter_keep: int32 [64], P('lat'), may hold values from 1 to 721, as said below
- seed_aerosol: float32 [64, 1440, 32], P('lat', 'lon'), may hold values from 0.5 to 5
- volatility: float32 [27], replicated, may hold values from 0.01 to 1000
- cotangent: float32 [64, 1440, 864], P('lat', 'lon'), may hold values from -6 to 6
Outputs:
- particle: float32 [64, 1440, 864], P('lat', 'lon')
- tracer_adjoint: float32 [64, 1440, 864], P('lat', 'lon')
The draws below stay inside these ranges and needn't reach their ends.
Inputs may be any that keep to these rules, and one draw needn't show every extreme that they name: `filter_keep`: with d = min(i, 63 - i) for row i: rows with d < 2 keep 1 to 32 wavenumbers, and the rows with d = 1 keep exactly 32; every other row keeps 1440 // 2 + 1.
All inputs are finite; a program needn't handle non-finite values.
Results may differ from the reference program's by a relative error of at most 0.0003.
Values sent between devices are 32-bit elements; how exact they have to be, the bound alone decides.
A program may use at most 128 MiB of HBM per device.

```python
import math
import jax
import jax.numpy as jnp
from jax import lax

LON = 1440
TR = 27
LEV = 32
NEWTON = 4
KMAX = 32
POLAR = 2
LAT = 64


def draw_filter_keep(key, part):
    rows_index = jnp.arange(LAT, dtype=jnp.int32)
    distance = jnp.minimum(rows_index, LAT - 1 - rows_index)
    random_keep = jax.random.randint(key, (LAT,), 1, KMAX + 1, dtype=jnp.int32)
    polar_keep = jnp.where(distance == POLAR - 1, KMAX, random_keep)
    return jnp.where(distance < POLAR, polar_keep, LON // 2 + 1).astype(jnp.int32)


def touch_ends(entries, stream_key, least, high):
    extent = entries.shape
    spot = [jax.random.randint(jax.random.fold_in(stream_key, axis), (), 0, extent[axis]) for axis in range(len(extent))]
    entries = entries.at[tuple(spot)].set(least)
    longest = extent.index(max(extent))
    spot[longest] = (spot[longest] + 1) % extent[longest]
    return entries.at[tuple(spot)].set(high)


def level_of(stream_key, dims, split, smallest, top_value):
    def one(dim, shards_of):
        steps = jax.random.uniform(jax.random.fold_in(jax.random.fold_in(stream_key, 6), dim), (shards_of,), jnp.float32, smallest / len(split), top_value / len(split))
        return jnp.repeat(jnp.exp(steps), dims[dim] // shards_of).reshape((-1,) + (1,) * (len(dims) - dim - 1))

    level = one(*split[0])
    for cut in split[1:]:
        level = level * one(*cut)
    return level


def noise(own_key, shape, width, bound, split=(), kind=jnp.bfloat16):
    result = jax.random.normal(own_key, shape, jnp.float32) * width
    if len(split) > 0:
        result = level_of(own_key, shape, split, -0.22, 0.18) * result
    return jnp.clip(result, min=-bound, max=bound).astype(kind)


def setup_inputs(seed: int = 0) -> dict:
    seeds = jax.random.split(jax.random.key(seed), 10)
    tracer = jnp.clip(1.0 + 8.0 * jax.random.uniform(seeds[0], (LAT, LON, LEV * TR), jnp.float32) ** level_of(seeds[0], (LAT, LON, LEV * TR), ((0, 16), (1, 32)), -0.2, 0.2), 1.0, 9.0)
    east_courant = jnp.clip(jax.random.uniform(seeds[1], (LAT, LON, LEV), jnp.float32, -0.3, 0.3) * level_of(seeds[1], (LAT, LON, LEV), ((0, 16), (1, 32)), -0.4, 0.0), -0.3, 0.3)
    north_courant = jnp.clip(jax.random.uniform(seeds[2], (LAT, LON, LEV), jnp.float32, -0.3, 0.3) * level_of(seeds[2], (LAT, LON, LEV), ((0, 16), (1, 32)), -0.4, 0.0), -0.3, 0.3)
    east_limiter = touch_ends(jax.random.randint(seeds[3], (LAT, LON, LEV), 0, 3), jax.random.fold_in(seeds[3], 1), 0, 2).astype(jnp.int32)
    north_limiter = touch_ends(jax.random.randint(seeds[4], (LAT, LON, LEV), 0, 3), jax.random.fold_in(seeds[4], 1), 0, 2).astype(jnp.int32)
    filter_keep = draw_filter_keep(jax.random.fold_in(seeds[9], 71), 0)
    seed_aerosol = jnp.clip(jnp.exp(math.log(5.0) - 2.3025851 * jax.random.uniform(seeds[6], (LAT, LON, LEV), jnp.float32) ** level_of(seeds[6], (LAT, LON, LEV), ((0, 16), (1, 32)), -0.2, 0.2)), 0.5, 5.0)
    volatility = jnp.clip(jnp.exp(jax.random.uniform(seeds[7], (TR,), jnp.float32, math.log(0.01), math.log(1000.0))), 0.01, 1000.0)
    cotangent = noise(seeds[8], (LAT, LON, LEV * TR), 1.0, 6.0, ((0, 16), (1, 32)), jnp.float32)
    return dict(tracer=tracer, east_courant=east_courant, north_courant=north_courant, east_limiter=east_limiter, north_limiter=north_limiter, filter_keep=filter_keep, seed_aerosol=seed_aerosol, volatility=volatility, cotangent=cotangent)


def spread(values, copies):
    return jnp.repeat(values, copies, axis=-1)

def face_value(far_left, near_left, near_right, far_right, limiter, courant):
    fourth = (7.0 * (near_left + near_right) - (far_left + far_right)) / 12.0
    upwind = jnp.where(courant >= 0.0, near_left, near_right)
    centred = 0.5 * (near_left + near_right)
    return jnp.where(limiter == 0, fourth, jnp.where(limiter == 1, upwind, centred))

def zonal_window(window, courant, limiter, species):
    inner_count = window.shape[1] - 4
    courant_q = spread(courant[:, 2:inner_count + 3], species)
    limiter_q = spread(limiter[:, 2:inner_count + 3], species)
    fluxes = courant_q * face_value(window[:, 0:inner_count + 1], window[:, 1:inner_count + 2], window[:, 2:inner_count + 3], window[:, 3:inner_count + 4], limiter_q, courant_q)
    return window[:, 2:inner_count + 2] - (fluxes[:, 1:] - fluxes[:, :-1])

def meridional_window(window, courant, limiter, first_row, species):
    inner_count = window.shape[0] - 4
    face_rows = first_row + jnp.arange(inner_count + 1, dtype=jnp.int32)
    opened = jnp.where(face_rows[:, None, None] > 0, courant[2:inner_count + 3], 0.0)
    courant_q = spread(opened, species)
    limiter_q = spread(limiter[2:inner_count + 3], species)
    fluxes = courant_q * face_value(window[0:inner_count + 1], window[1:inner_count + 2], window[2:inner_count + 3], window[3:inner_count + 4], limiter_q, courant_q)
    return window[2:inner_count + 2] - (fluxes[1:] - fluxes[:-1])

def positive(field):
    return 0.5 * (field + jnp.sqrt(field * field + 1.0))

def partition(total_mass, seed_aerosol, volatility):
    levels = seed_aerosol.shape[-1]
    species = volatility.shape[0]
    grouped = total_mass.shape[:-1] + (levels, species)
    saturation = jnp.tile(volatility, levels)
    aerosol = seed_aerosol
    for newton_step in range(NEWTON):
        denominator = spread(aerosol, species) + saturation
        fraction = total_mass / denominator
        first_sum = lax.optimization_barrier(jnp.sum(fraction.reshape(grouped), axis=-1))
        second_sum = lax.optimization_barrier(jnp.sum((fraction / denominator).reshape(grouped), axis=-1))
        residue = 1.0 - seed_aerosol / aerosol - first_sum
        derivative = seed_aerosol / (aerosol * aerosol) + second_sum
        aerosol = aerosol - residue / derivative
    aerosol_q = spread(aerosol, species)
    return total_mass * aerosol_q / (aerosol_q + saturation)

def wrap_columns(field):
    return jnp.concatenate([field[:, -2:], field, field[:, :2]], axis=1)

def pad_rows(field):
    return jnp.pad(field, ((2, 2), (0, 0), (0, 0)))

def polar_filter(field, filter_keep):
    spectral = jnp.fft.rfft(field, axis=1)
    numbers = jnp.arange(spectral.shape[1], dtype=jnp.int32)
    kept_mask = numbers[None, :, None] < filter_keep[:, None, None]
    spectral = jnp.where(kept_mask, spectral, 0.0)
    lowpass = jnp.fft.irfft(spectral, n=field.shape[1], axis=1)
    return jnp.where((filter_keep <= KMAX)[:, None, None], lowpass, field)

def reference(tracer, east_courant, north_courant, east_limiter, north_limiter, filter_keep, seed_aerosol, volatility, cotangent):

    def transport(field):
        after_east = zonal_window(wrap_columns(field), wrap_columns(east_courant), wrap_columns(east_limiter), TR)
        after_north = meridional_window(pad_rows(after_east), pad_rows(north_courant), pad_rows(north_limiter), 0, TR)
        return polar_filter(after_north, filter_keep)
    filtered, transport_back = jax.vjp(transport, tracer)

    def column_step(inputs):
        field_row, seed_row, cotangent_row = inputs

        def chemistry(values):
            return partition(positive(values), seed_row, volatility)
        particle_row, chem_back = jax.vjp(chemistry, field_row)
        return (particle_row, chem_back(cotangent_row)[0])
    particle, adjoint_filtered = lax.map(column_step, (filtered, seed_aerosol, cotangent))
    tracer_adjoint = transport_back(adjoint_filtered)[0]
    return (particle, tracer_adjoint)
```

```python
import math

import jax
import jax.numpy as jnp
from jax import lax
from jax.sharding import PartitionSpec as P
from jax.experimental import pallas as pl
from jax.experimental.pallas import tpu as pltpu

NEWTON = 4
KMAX = 32
POLAR = 2


def with_halo(cells, sides, width, closed):
    for axis, dim in sides:
        count = lax.axis_size(axis)
        ends = count if closed else count - 1
        head = lax.slice_in_dim(cells, 0, width, axis=dim)
        tail = lax.slice_in_dim(cells, cells.shape[dim] - width, cells.shape[dim], axis=dim)
        cells = jnp.concatenate(
            [
                lax.ppermute(tail, axis, [(i, (i + 1) % count) for i in range(ends)]),
                cells,
                lax.ppermute(head, axis, [((i + 1) % count, i) for i in range(ends)]),
            ],
            axis=dim,
        )
    return cells


def spread(values, copies):
    return jnp.repeat(values, copies, axis=-1)


def face_value(far_left, near_left, near_right, far_right, limiter, courant):
    fourth = (7.0 * (near_left + near_right) - (far_left + far_right)) / 12.0
    upwind = jnp.where(courant >= 0.0, near_left, near_right)
    centred = 0.5 * (near_left + near_right)
    return jnp.where(limiter == 0, fourth, jnp.where(limiter == 1, upwind, centred))


def zonal_window(window, courant, limiter, species):
    inner_count = window.shape[1] - 4
    courant_q = spread(courant[:, 2 : inner_count + 3], species)
    limiter_q = spread(limiter[:, 2 : inner_count + 3], species)
    fluxes = courant_q * face_value(
        window[:, 0 : inner_count + 1],
        window[:, 1 : inner_count + 2],
        window[:, 2 : inner_count + 3],
        window[:, 3 : inner_count + 4],
        limiter_q,
        courant_q,
    )
    return window[:, 2 : inner_count + 2] - (fluxes[:, 1:] - fluxes[:, :-1])


def meridional_window(window, courant, limiter, first_row, species):
    inner_count = window.shape[0] - 4
    face_rows = first_row + jnp.arange(inner_count + 1, dtype=jnp.int32)
    opened = jnp.where(face_rows[:, None, None] > 0, courant[2 : inner_count + 3], 0.0)
    courant_q = spread(opened, species)
    limiter_q = spread(limiter[2 : inner_count + 3], species)
    fluxes = courant_q * face_value(
        window[0 : inner_count + 1],
        window[1 : inner_count + 2],
        window[2 : inner_count + 3],
        window[3 : inner_count + 4],
        limiter_q,
        courant_q,
    )
    return window[2 : inner_count + 2] - (fluxes[1:] - fluxes[:-1])


def positive(field):
    return 0.5 * (field + jnp.sqrt(field * field + 1.0))


def level_table(levels, species):
    channel_level = jnp.arange(levels * species, dtype=jnp.int32) // species
    return (channel_level[:, None] == jnp.arange(levels, dtype=jnp.int32)[None, :]).astype(
        jnp.float32
    )


def partition(total_mass, seed_aerosol, volatility):
    levels = seed_aerosol.shape[-1]
    species = volatility.shape[0]
    grouping = level_table(levels, species)
    saturation = jnp.tile(volatility, levels)
    aerosol = seed_aerosol
    for newton_step in range(NEWTON):
        denominator = spread(aerosol, species) + saturation
        fraction = total_mass / denominator
        first_sum = jnp.dot(fraction, grouping, precision=lax.Precision.HIGHEST)
        second_sum = jnp.dot(fraction / denominator, grouping, precision=lax.Precision.HIGHEST)
        residue = 1.0 - seed_aerosol / aerosol - first_sum
        derivative = seed_aerosol / (aerosol * aerosol) + second_sum
        aerosol = aerosol - residue / derivative
    aerosol_q = spread(aerosol, species)
    return total_mass * aerosol_q / (aerosol_q + saturation)


def east_west(field):
    return with_halo(field, (("lon", 1),), 2, True)


def north_south(field):
    return with_halo(field, (("lat", 0),), 2, False)


def fold_rows(gradient):
    inner_rows = gradient.shape[0] - 4
    rim_cells = jnp.concatenate([gradient[:2], gradient[inner_rows + 2 :]], axis=0)
    arrived = north_south(rim_cells)
    middle = gradient[2 : inner_rows + 2]
    return jnp.concatenate(
        [
            middle[:2] + arrived[:2],
            middle[2 : inner_rows - 2],
            middle[inner_rows - 2 :] + arrived[6:],
        ],
        axis=0,
    )


def fold_columns(gradient):
    inner_cols = gradient.shape[1] - 4
    rim_cells = jnp.concatenate([gradient[:, :2], gradient[:, inner_cols + 2 :]], axis=1)
    arrived = east_west(rim_cells)
    middle = gradient[:, 2 : inner_cols + 2]
    return jnp.concatenate(
        [
            middle[:, :2] + arrived[:, :2],
            middle[:, 2 : inner_cols - 2],
            middle[:, inner_cols - 2 :] + arrived[:, 6:],
        ],
        axis=1,
    )


def wave_table(positions, length):
    numbers = jnp.arange(KMAX, dtype=jnp.int32)
    phases = positions[:, None] * numbers[None, :] % length
    angles = phases.astype(jnp.float32) * (2.0 * math.pi / length)
    return jnp.concatenate([jnp.cos(angles), jnp.sin(angles)], axis=1)


def wave_weights(keep_values, length):
    numbers = jnp.arange(2 * KMAX, dtype=jnp.int32) % KMAX
    scaling = jnp.where(numbers == 0, 1.0, 2.0) / length
    kept_mask = numbers[None, :] < keep_values[:, None]
    return jnp.where(kept_mask, scaling[None, :], 0.0)


def filter_field(field, filter_keep):
    row_count, col_count = field.shape[0], field.shape[1]
    length = col_count * lax.axis_size("lon")
    polar_count = POLAR
    at_north_end = lax.axis_index("lat") == 0
    top_rows = field[:polar_count]
    bottom_rows = field[row_count - polar_count :]
    end_rows = jnp.where(at_north_end, top_rows, bottom_rows)
    end_keep = jnp.where(
        at_north_end, filter_keep[:polar_count], filter_keep[row_count - polar_count :]
    )
    positions = lax.axis_index("lon") * col_count + jnp.arange(col_count, dtype=jnp.int32)
    table = wave_table(positions, length)
    hi = lax.Precision.HIGHEST
    partial = jnp.einsum("rjq,jk->rkq", end_rows, table, precision=hi)
    coefficient = lax.psum(partial, "lon")
    coefficient = coefficient * wave_weights(end_keep, length)[:, :, None]
    lowpass = jnp.einsum("jk,rkq->rjq", table, coefficient, precision=hi)
    smoothed = jnp.where((end_keep <= KMAX)[:, None, None], lowpass, end_rows)
    new_top = jnp.where(at_north_end, smoothed, top_rows)
    new_bottom = jnp.where(at_north_end, bottom_rows, smoothed)
    return jnp.concatenate(
        [new_top, field[polar_count : row_count - polar_count], new_bottom], axis=0
    )


def chem_kernel(x_ref, seed_ref, cot_ref, sat_ref, spread_ref, group_ref, p_ref, g_ref):
    hi = lax.Precision.HIGHEST
    x = x_ref[0]
    seed = seed_ref[0]
    cot = cot_ref[0]
    sat = sat_ref[...]
    spread_m = spread_ref[...]
    group_m = group_ref[...]

    def up(v):
        return jnp.dot(v, spread_m, precision=hi, preferred_element_type=jnp.float32)

    def down(v):
        return jnp.dot(v, group_m, precision=hi, preferred_element_type=jnp.float32)

    root = jnp.sqrt(x * x + 1.0)
    mass = 0.5 * (x + root)
    aerosol = seed
    history = []
    for newton_step in range(NEWTON):
        denominator = up(aerosol) + sat
        fraction = mass / denominator
        first_sum = down(fraction)
        second_sum = down(fraction / denominator)
        residue = 1.0 - seed / aerosol - first_sum
        derivative = seed / (aerosol * aerosol) + second_sum
        history.append((aerosol, residue, derivative))
        aerosol = aerosol - residue / derivative
    aerosol_q = up(aerosol)
    final_den = aerosol_q + sat
    p_ref[0] = mass * aerosol_q / final_den
    mass_bar = cot * aerosol_q / final_den
    aerosol_bar = down(cot * mass * sat / (final_den * final_den))
    for newton_step in reversed(range(NEWTON)):
        a_n, residue, derivative = history[newton_step]
        inverse = 1.0 / (up(a_n) + sat)
        third_sum = down(mass * inverse * inverse * inverse)
        slope = -2.0 * (seed / (a_n * a_n * a_n) + third_sum)
        over_g = aerosol_bar / derivative
        over_g2 = over_g * residue / derivative
        mass_bar = mass_bar + up(over_g) * inverse + up(over_g2) * inverse * inverse
        aerosol_bar = over_g2 * slope
    g_ref[0] = mass_bar * 0.5 * (1.0 + x / root)


def chemistry_step(filtered, seed_aerosol, volatility, cotangent):
    rows, cols, channels = filtered.shape
    levels = seed_aerosol.shape[-1]
    species = volatility.shape[0]
    group_m = level_table(levels, species)
    spread_m = group_m.T
    sat = jnp.tile(volatility, levels)[None, :]
    big = pl.BlockSpec((1, cols, channels), lambda i: (i, 0, 0))
    small = pl.BlockSpec((1, cols, levels), lambda i: (i, 0, 0))
    return pl.pallas_call(
        chem_kernel,
        grid=(rows,),
        in_specs=[
            big,
            small,
            big,
            pl.BlockSpec((1, channels), lambda i: (0, 0)),
            pl.BlockSpec((levels, channels), lambda i: (0, 0)),
            pl.BlockSpec((channels, levels), lambda i: (0, 0)),
        ],
        out_specs=[big, big],
        out_shape=[
            jax.ShapeDtypeStruct(filtered.shape, jnp.float32),
            jax.ShapeDtypeStruct(filtered.shape, jnp.float32),
        ],
    )(filtered, seed_aerosol, cotangent, sat, spread_m, group_m)


def local(
    tracer,
    east_courant,
    north_courant,
    east_limiter,
    north_limiter,
    filter_keep,
    seed_aerosol,
    volatility,
    cotangent,
):
    row_count = tracer.shape[0]
    channels = tracer.shape[2]
    levels = east_courant.shape[2]
    species = volatility.shape[0]
    first_row = lax.axis_index("lat") * row_count
    packed = jnp.concatenate([tracer, east_courant, east_limiter.astype(jnp.float32)], axis=2)
    widened = east_west(packed)
    east_speed = widened[:, :, channels : channels + levels]
    east_choice = widened[:, :, channels + levels :].astype(jnp.int32)

    def zonal_only(window):
        return zonal_window(window, east_speed, east_choice, species)

    after_east, east_back = jax.vjp(zonal_only, widened[:, :, :channels])
    stacked = jnp.concatenate(
        [after_east, north_courant, north_limiter.astype(jnp.float32)], axis=2
    )
    tall_window = north_south(stacked)
    north_speed = tall_window[:, :, channels : channels + levels]
    north_choice = tall_window[:, :, channels + levels :].astype(jnp.int32)

    def meridional_only(window):
        return meridional_window(window, north_speed, north_choice, first_row, species)

    after_north, north_back = jax.vjp(meridional_only, tall_window[:, :, :channels])
    filtered = filter_field(after_north, filter_keep)

    particle, chem_grad = chemistry_step(filtered, seed_aerosol, volatility, cotangent)
    adjoint_filtered = filter_field(chem_grad, filter_keep)
    return (particle, fold_columns(east_back(fold_rows(north_back(adjoint_filtered)[0]))[0]))


def solution(mesh):
    in_specs = (
        P("lat", "lon", None),
        P("lat", "lon", None),
        P("lat", "lon", None),
        P("lat", "lon", None),
        P("lat", "lon", None),
        P("lat"),
        P("lat", "lon", None),
        P(),
        P("lat", "lon", None),
    )
    out_specs = (P("lat", "lon", None), P("lat", "lon", None))
    return jax.shard_map(local, mesh=mesh, in_specs=in_specs, out_specs=out_specs, check_vma=False)
```

```python
import math

import jax
import jax.numpy as jnp
from jax import lax
from jax.sharding import PartitionSpec as P
from jax.experimental import pallas as pl
from jax.experimental.pallas import tpu as pltpu

NEWTON = 4
KMAX = 32
POLAR = 2


def with_halo(cells, sides, width, closed):
    for axis, dim in sides:
        count = lax.axis_size(axis)
        ends = count if closed else count - 1
        head = lax.slice_in_dim(cells, 0, width, axis=dim)
        tail = lax.slice_in_dim(cells, cells.shape[dim] - width, cells.shape[dim], axis=dim)
        cells = jnp.concatenate(
            [
                lax.ppermute(tail, axis, [(i, (i + 1) % count) for i in range(ends)]),
                cells,
                lax.ppermute(head, axis, [((i + 1) % count, i) for i in range(ends)]),
            ],
            axis=dim,
        )
    return cells


def spread(values, copies):
    return jnp.repeat(values, copies, axis=-1)


def face_value(far_left, near_left, near_right, far_right, limiter, courant):
    fourth = (7.0 * (near_left + near_right) - (far_left + far_right)) / 12.0
    upwind = jnp.where(courant >= 0.0, near_left, near_right)
    centred = 0.5 * (near_left + near_right)
    return jnp.where(limiter == 0, fourth, jnp.where(limiter == 1, upwind, centred))


def zonal_window(window, courant, limiter, species):
    inner_count = window.shape[1] - 4
    courant_q = spread(courant[:, 2 : inner_count + 3], species)
    limiter_q = spread(limiter[:, 2 : inner_count + 3], species)
    fluxes = courant_q * face_value(
        window[:, 0 : inner_count + 1],
        window[:, 1 : inner_count + 2],
        window[:, 2 : inner_count + 3],
        window[:, 3 : inner_count + 4],
        limiter_q,
        courant_q,
    )
    return window[:, 2 : inner_count + 2] - (fluxes[:, 1:] - fluxes[:, :-1])


def meridional_window(window, courant, limiter, first_row, species):
    inner_count = window.shape[0] - 4
    face_rows = first_row + jnp.arange(inner_count + 1, dtype=jnp.int32)
    opened = jnp.where(face_rows[:, None, None] > 0, courant[2 : inner_count + 3], 0.0)
    courant_q = spread(opened, species)
    limiter_q = spread(limiter[2 : inner_count + 3], species)
    fluxes = courant_q * face_value(
        window[0 : inner_count + 1],
        window[1 : inner_count + 2],
        window[2 : inner_count + 3],
        window[3 : inner_count + 4],
        limiter_q,
        courant_q,
    )
    return window[2 : inner_count + 2] - (fluxes[1:] - fluxes[:-1])


def positive(field):
    return 0.5 * (field + jnp.sqrt(field * field + 1.0))


def level_table(levels, species):
    channel_level = jnp.arange(levels * species, dtype=jnp.int32) // species
    return (channel_level[:, None] == jnp.arange(levels, dtype=jnp.int32)[None, :]).astype(
        jnp.float32
    )


def partition(total_mass, seed_aerosol, volatility):
    levels = seed_aerosol.shape[-1]
    species = volatility.shape[0]
    grouping = level_table(levels, species)
    saturation = jnp.tile(volatility, levels)
    aerosol = seed_aerosol
    for newton_step in range(NEWTON):
        denominator = spread(aerosol, species) + saturation
        fraction = total_mass / denominator
        first_sum = jnp.dot(fraction, grouping, precision=lax.Precision.HIGHEST)
        second_sum = jnp.dot(fraction / denominator, grouping, precision=lax.Precision.HIGHEST)
        residue = 1.0 - seed_aerosol / aerosol - first_sum
        derivative = seed_aerosol / (aerosol * aerosol) + second_sum
        aerosol = aerosol - residue / derivative
    aerosol_q = spread(aerosol, species)
    return total_mass * aerosol_q / (aerosol_q + saturation)


def east_west(field):
    return with_halo(field, (("lon", 1),), 2, True)


def north_south(field):
    return with_halo(field, (("lat", 0),), 2, False)


def fold_rows(gradient):
    inner_rows = gradient.shape[0] - 4
    rim_cells = jnp.concatenate([gradient[:2], gradient[inner_rows + 2 :]], axis=0)
    arrived = north_south(rim_cells)
    middle = gradient[2 : inner_rows + 2]
    return jnp.concatenate(
        [
            middle[:2] + arrived[:2],
            middle[2 : inner_rows - 2],
            middle[inner_rows - 2 :] + arrived[6:],
        ],
        axis=0,
    )


def fold_columns(gradient):
    inner_cols = gradient.shape[1] - 4
    rim_cells = jnp.concatenate([gradient[:, :2], gradient[:, inner_cols + 2 :]], axis=1)
    arrived = east_west(rim_cells)
    middle = gradient[:, 2 : inner_cols + 2]
    return jnp.concatenate(
        [
            middle[:, :2] + arrived[:, :2],
            middle[:, 2 : inner_cols - 2],
            middle[:, inner_cols - 2 :] + arrived[:, 6:],
        ],
        axis=1,
    )


def wave_table(column_count, length):
    position = jnp.arange(column_count, dtype=jnp.int32)
    numbers = jnp.arange(KMAX, dtype=jnp.int32)
    phases = position[:, None] * numbers[None, :] % length
    angles = phases.astype(jnp.float32) * (2.0 * math.pi / length)
    return jnp.concatenate([jnp.cos(angles), jnp.sin(angles)], axis=1)


def wave_weights(keep_values, length):
    numbers = jnp.arange(2 * KMAX, dtype=jnp.int32) % KMAX
    scaling = jnp.where(numbers == 0, 1.0, 2.0) / length
    kept_mask = numbers[None, :] < keep_values[:, None]
    return jnp.where(kept_mask, scaling[None, :], 0.0)


def lowpass_circles(circles, keep_values):
    length = circles.shape[2]
    table_full = wave_table(length, length)
    coefficient = jnp.einsum("rqn,nk->rqk", circles, table_full, precision=lax.Precision.HIGHEST)
    coefficient = coefficient * wave_weights(keep_values, length)[:, None, :]
    lowpass = jnp.einsum("rqk,nk->rqn", coefficient, table_full, precision=lax.Precision.HIGHEST)
    return jnp.where((keep_values <= KMAX)[:, None, None], lowpass, circles)


def filter_field(field, filter_keep):
    row_count = field.shape[0]
    polar_count = POLAR
    at_north_end = lax.axis_index("lat") == 0
    top_rows = field[:polar_count]
    bottom_rows = field[row_count - polar_count :]
    end_rows = jnp.where(at_north_end, top_rows, bottom_rows)
    end_keep = jnp.where(
        at_north_end, filter_keep[:polar_count], filter_keep[row_count - polar_count :]
    )
    reordered = jnp.transpose(end_rows, (0, 2, 1))
    circles = lax.all_to_all(reordered, "lon", split_axis=1, concat_axis=2, tiled=True)
    lowpass = lowpass_circles(circles, end_keep)
    smoothed = lax.all_to_all(lowpass, "lon", split_axis=2, concat_axis=1, tiled=True)
    smoothed = jnp.transpose(smoothed, (0, 2, 1))
    new_top = jnp.where(at_north_end, smoothed, top_rows)
    new_bottom = jnp.where(at_north_end, bottom_rows, smoothed)
    return jnp.concatenate(
        [new_top, field[polar_count : row_count - polar_count], new_bottom], axis=0
    )


def chem_kernel(x_ref, seed_ref, cot_ref, sat_ref, spread_ref, group_ref, p_ref, g_ref):
    hi = lax.Precision.HIGHEST
    x = x_ref[0]
    seed = seed_ref[0]
    cot = cot_ref[0]
    sat = sat_ref[...]
    spread_m = spread_ref[...]
    group_m = group_ref[...]

    def up(v):
        return jnp.dot(v, spread_m, precision=hi, preferred_element_type=jnp.float32)

    def down(v):
        return jnp.dot(v, group_m, precision=hi, preferred_element_type=jnp.float32)

    root = jnp.sqrt(x * x + 1.0)
    mass = 0.5 * (x + root)
    aerosol = seed
    history = []
    for newton_step in range(NEWTON):
        denominator = up(aerosol) + sat
        fraction = mass / denominator
        first_sum = down(fraction)
        second_sum = down(fraction / denominator)
        residue = 1.0 - seed / aerosol - first_sum
        derivative = seed / (aerosol * aerosol) + second_sum
        history.append((aerosol, residue, derivative))
        aerosol = aerosol - residue / derivative
    aerosol_q = up(aerosol)
    final_den = aerosol_q + sat
    p_ref[0] = mass * aerosol_q / final_den
    mass_bar = cot * aerosol_q / final_den
    aerosol_bar = down(cot * mass * sat / (final_den * final_den))
    for newton_step in reversed(range(NEWTON)):
        a_n, residue, derivative = history[newton_step]
        inverse = 1.0 / (up(a_n) + sat)
        third_sum = down(mass * inverse * inverse * inverse)
        slope = -2.0 * (seed / (a_n * a_n * a_n) + third_sum)
        over_g = aerosol_bar / derivative
        over_g2 = over_g * residue / derivative
        mass_bar = mass_bar + up(over_g) * inverse + up(over_g2) * inverse * inverse
        aerosol_bar = over_g2 * slope
    g_ref[0] = mass_bar * 0.5 * (1.0 + x / root)


def chemistry_step(filtered, seed_aerosol, volatility, cotangent):
    rows, cols, channels = filtered.shape
    levels = seed_aerosol.shape[-1]
    species = volatility.shape[0]
    group_m = level_table(levels, species)
    spread_m = group_m.T
    sat = jnp.tile(volatility, levels)[None, :]
    big = pl.BlockSpec((1, cols, channels), lambda i: (i, 0, 0))
    small = pl.BlockSpec((1, cols, levels), lambda i: (i, 0, 0))
    return pl.pallas_call(
        chem_kernel,
        grid=(rows,),
        in_specs=[
            big,
            small,
            big,
            pl.BlockSpec((1, channels), lambda i: (0, 0)),
            pl.BlockSpec((levels, channels), lambda i: (0, 0)),
            pl.BlockSpec((channels, levels), lambda i: (0, 0)),
        ],
        out_specs=[big, big],
        out_shape=[
            jax.ShapeDtypeStruct(filtered.shape, jnp.float32),
            jax.ShapeDtypeStruct(filtered.shape, jnp.float32),
        ],
    )(filtered, seed_aerosol, cotangent, sat, spread_m, group_m)


def local(
    tracer,
    east_courant,
    north_courant,
    east_limiter,
    north_limiter,
    filter_keep,
    seed_aerosol,
    volatility,
    cotangent,
):
    row_count = tracer.shape[0]
    channels = tracer.shape[2]
    levels = east_courant.shape[2]
    species = volatility.shape[0]
    first_row = lax.axis_index("lat") * row_count
    packed = jnp.concatenate([tracer, east_courant, east_limiter.astype(jnp.float32)], axis=2)
    widened = east_west(packed)
    east_speed = widened[:, :, channels : channels + levels]
    east_choice = widened[:, :, channels + levels :].astype(jnp.int32)

    def zonal_only(window):
        return zonal_window(window, east_speed, east_choice, species)

    after_east, east_back = jax.vjp(zonal_only, widened[:, :, :channels])
    stacked = jnp.concatenate(
        [after_east, north_courant, north_limiter.astype(jnp.float32)], axis=2
    )
    tall_window = north_south(stacked)
    north_speed = tall_window[:, :, channels : channels + levels]
    north_choice = tall_window[:, :, channels + levels :].astype(jnp.int32)

    def meridional_only(window):
        return meridional_window(window, north_speed, north_choice, first_row, species)

    after_north, north_back = jax.vjp(meridional_only, tall_window[:, :, :channels])
    filtered = filter_field(after_north, filter_keep)

    particle, chem_grad = chemistry_step(filtered, seed_aerosol, volatility, cotangent)
    adjoint_filtered = filter_field(chem_grad, filter_keep)
    return (particle, fold_columns(east_back(fold_rows(north_back(adjoint_filtered)[0]))[0]))


def solution(mesh):
    in_specs = (
        P("lat", "lon", None),
        P("lat", "lon", None),
        P("lat", "lon", None),
        P("lat", "lon", None),
        P("lat", "lon", None),
        P("lat"),
        P("lat", "lon", None),
        P(),
        P("lat", "lon", None),
    )
    out_specs = (P("lat", "lon", None), P("lat", "lon", None))
    return jax.shard_map(local, mesh=mesh, in_specs=in_specs, out_specs=out_specs, check_vma=False)
```

```python
import math

import jax
import jax.numpy as jnp
from jax import lax
from jax.sharding import PartitionSpec as P
from jax.experimental import pallas as pl
from jax.experimental.pallas import tpu as pltpu

NEWTON = 4
KMAX = 32
POLAR = 2


def with_halo(cells, sides, width, closed):
    for axis, dim in sides:
        count = lax.axis_size(axis)
        ends = count if closed else count - 1
        head = lax.slice_in_dim(cells, 0, width, axis=dim)
        tail = lax.slice_in_dim(cells, cells.shape[dim] - width, cells.shape[dim], axis=dim)
        cells = jnp.concatenate(
            [
                lax.ppermute(tail, axis, [(i, (i + 1) % count) for i in range(ends)]),
                cells,
                lax.ppermute(head, axis, [((i + 1) % count, i) for i in range(ends)]),
            ],
            axis=dim,
        )
    return cells


def spread(values, copies):
    return jnp.repeat(values, copies, axis=-1)


def face_value(far_left, near_left, near_right, far_right, limiter, courant):
    fourth = (7.0 * (near_left + near_right) - (far_left + far_right)) / 12.0
    upwind = jnp.where(courant >= 0.0, near_left, near_right)
    centred = 0.5 * (near_left + near_right)
    return jnp.where(limiter == 0, fourth, jnp.where(limiter == 1, upwind, centred))


def zonal_window(window, courant, limiter, species):
    inner_count = window.shape[1] - 4
    courant_q = spread(courant[:, 2 : inner_count + 3], species)
    limiter_q = spread(limiter[:, 2 : inner_count + 3], species)
    fluxes = courant_q * face_value(
        window[:, 0 : inner_count + 1],
        window[:, 1 : inner_count + 2],
        window[:, 2 : inner_count + 3],
        window[:, 3 : inner_count + 4],
        limiter_q,
        courant_q,
    )
    return window[:, 2 : inner_count + 2] - (fluxes[:, 1:] - fluxes[:, :-1])


def meridional_window(window, courant, limiter, first_row, species):
    inner_count = window.shape[0] - 4
    face_rows = first_row + jnp.arange(inner_count + 1, dtype=jnp.int32)
    opened = jnp.where(face_rows[:, None, None] > 0, courant[2 : inner_count + 3], 0.0)
    courant_q = spread(opened, species)
    limiter_q = spread(limiter[2 : inner_count + 3], species)
    fluxes = courant_q * face_value(
        window[0 : inner_count + 1],
        window[1 : inner_count + 2],
        window[2 : inner_count + 3],
        window[3 : inner_count + 4],
        limiter_q,
        courant_q,
    )
    return window[2 : inner_count + 2] - (fluxes[1:] - fluxes[:-1])


def positive(field):
    return 0.5 * (field + jnp.sqrt(field * field + 1.0))


def level_table(levels, species):
    channel_level = jnp.arange(levels * species, dtype=jnp.int32) // species
    return (channel_level[:, None] == jnp.arange(levels, dtype=jnp.int32)[None, :]).astype(
        jnp.float32
    )


def partition(total_mass, seed_aerosol, volatility):
    levels = seed_aerosol.shape[-1]
    species = volatility.shape[0]
    grouping = level_table(levels, species)
    saturation = jnp.tile(volatility, levels)
    aerosol = seed_aerosol
    for newton_step in range(NEWTON):
        denominator = spread(aerosol, species) + saturation
        fraction = total_mass / denominator
        first_sum = jnp.dot(fraction, grouping, precision=lax.Precision.HIGHEST)
        second_sum = jnp.dot(fraction / denominator, grouping, precision=lax.Precision.HIGHEST)
        residue = 1.0 - seed_aerosol / aerosol - first_sum
        derivative = seed_aerosol / (aerosol * aerosol) + second_sum
        aerosol = aerosol - residue / derivative
    aerosol_q = spread(aerosol, species)
    return total_mass * aerosol_q / (aerosol_q + saturation)


def east_west(field):
    return with_halo(field, (("lon", 1),), 2, True)


def north_south(field):
    return with_halo(field, (("lat", 0),), 2, False)


def fold_rows(gradient):
    inner_rows = gradient.shape[0] - 4
    rim_cells = jnp.concatenate([gradient[:2], gradient[inner_rows + 2 :]], axis=0)
    arrived = north_south(rim_cells)
    middle = gradient[2 : inner_rows + 2]
    return jnp.concatenate(
        [
            middle[:2] + arrived[:2],
            middle[2 : inner_rows - 2],
            middle[inner_rows - 2 :] + arrived[6:],
        ],
        axis=0,
    )


def fold_columns(gradient):
    inner_cols = gradient.shape[1] - 4
    rim_cells = jnp.concatenate([gradient[:, :2], gradient[:, inner_cols + 2 :]], axis=1)
    arrived = east_west(rim_cells)
    middle = gradient[:, 2 : inner_cols + 2]
    return jnp.concatenate(
        [
            middle[:, :2] + arrived[:, :2],
            middle[:, 2 : inner_cols - 2],
            middle[:, inner_cols - 2 :] + arrived[:, 6:],
        ],
        axis=1,
    )


def wave_table(column_count, length):
    position = jnp.arange(column_count, dtype=jnp.int32)
    numbers = jnp.arange(KMAX, dtype=jnp.int32)
    phases = position[:, None] * numbers[None, :] % length
    angles = phases.astype(jnp.float32) * (2.0 * math.pi / length)
    return jnp.concatenate([jnp.cos(angles), jnp.sin(angles)], axis=1)


def wave_weights(keep_values, length):
    numbers = jnp.arange(2 * KMAX, dtype=jnp.int32) % KMAX
    scaling = jnp.where(numbers == 0, 1.0, 2.0) / length
    kept_mask = numbers[None, :] < keep_values[:, None]
    return jnp.where(kept_mask, scaling[None, :], 0.0)


def lowpass_circles(circles, keep_values):
    length = circles.shape[2]
    table_full = wave_table(length, length)
    coefficient = jnp.einsum("rqn,nk->rqk", circles, table_full, precision=lax.Precision.HIGHEST)
    coefficient = coefficient * wave_weights(keep_values, length)[:, None, :]
    lowpass = jnp.einsum("rqk,nk->rqn", coefficient, table_full, precision=lax.Precision.HIGHEST)
    return jnp.where((keep_values <= KMAX)[:, None, None], lowpass, circles)


def exchange_kernel(x_ref, o_ref, landing, send_sems, recv_sems):
    count = x_ref.shape[0]
    me = lax.axis_index("lon")
    band = lax.axis_index("lat")
    bands = lax.axis_size("lat")
    active = jnp.logical_or(band == 0, band == bands - 1)

    def copy_to(offset):
        peer = lax.rem(me + offset, count)
        return pltpu.make_async_remote_copy(
            src_ref=x_ref.at[peer],
            dst_ref=landing.at[me],
            send_sem=send_sems.at[offset],
            recv_sem=recv_sems.at[me],
            device_id=(band, peer),
            device_id_type=pl.DeviceIdType.MESH,
        )

    def copy_from(offset):
        peer = lax.rem(me + count - offset, count)
        return pltpu.make_async_remote_copy(
            src_ref=x_ref.at[peer],
            dst_ref=landing.at[peer],
            send_sem=send_sems.at[offset],
            recv_sem=recv_sems.at[peer],
            device_id=(band, peer),
            device_id_type=pl.DeviceIdType.MESH,
        )

    @pl.when(active)
    def _():
        barrier = pltpu.get_barrier_semaphore()
        for offset in range(1, count):
            peer = lax.rem(me + offset, count)
            pl.semaphore_signal(
                barrier, 1, device_id=(band, peer), device_id_type=pl.DeviceIdType.MESH
            )
        pl.semaphore_wait(barrier, count - 1)
        for offset in range(1, count):
            copy_to(offset).start()
        for offset in range(1, count):
            copy_to(offset).wait_send()
        for offset in range(1, count):
            copy_from(offset).wait_recv()
        for offset in range(1, count):
            peer = lax.rem(me + count - offset, count)
            o_ref[pl.ds(peer, 1)] = landing[pl.ds(peer, 1)]

    o_ref[pl.ds(me, 1)] = x_ref[pl.ds(me, 1)]

    @pl.when(jnp.logical_not(active))
    def _():
        o_ref[...] = x_ref[...]


def exchange(slabs, call_id):
    return pl.pallas_call(
        exchange_kernel,
        out_shape=jax.ShapeDtypeStruct(slabs.shape, slabs.dtype),
        in_specs=[pl.BlockSpec(memory_space=pltpu.VMEM)],
        out_specs=pl.BlockSpec(memory_space=pltpu.VMEM),
        scratch_shapes=[
            pltpu.VMEM(slabs.shape, slabs.dtype),
            pltpu.SemaphoreType.DMA((slabs.shape[0],)),
            pltpu.SemaphoreType.DMA((slabs.shape[0],)),
        ],
        compiler_params=pltpu.CompilerParams(collective_id=call_id, has_side_effects=True),
    )(slabs)


def slab_rows(piece):
    return -(-piece // 1024) * 8


def pack_slabs(pieces):
    count = pieces.shape[0]
    piece = math.prod(pieces.shape[1:])
    rows = slab_rows(piece)
    flat = jnp.pad(pieces.reshape(count, piece), ((0, 0), (0, rows * 128 - piece)))
    return flat.reshape(count, rows, 128)


def unpack_slabs(slabs, shape):
    count = slabs.shape[0]
    piece = math.prod(shape)
    return slabs.reshape(count, -1)[:, :piece].reshape((count,) + tuple(shape))


def filter_field(field, filter_keep, call_id):
    row_count, col_count, channels = field.shape
    count = lax.axis_size("lon")
    chunk = channels // count
    polar_count = POLAR
    band = lax.axis_index("lat")
    at_north_end = band == 0
    at_south_end = band == lax.axis_size("lat") - 1
    top_rows = field[:polar_count]
    bottom_rows = field[row_count - polar_count :]
    end_rows = jnp.where(at_north_end, top_rows, bottom_rows)
    end_keep = jnp.where(
        at_north_end, filter_keep[:polar_count], filter_keep[row_count - polar_count :]
    )
    pieces = end_rows.reshape(polar_count, col_count, count, chunk).transpose(2, 0, 1, 3)
    arrived = unpack_slabs(
        exchange(pack_slabs(pieces), call_id), (polar_count, col_count, chunk)
    )
    circles = arrived.transpose(1, 3, 0, 2).reshape(polar_count, chunk, count * col_count)
    lowpass = lowpass_circles(circles, end_keep)
    going = lowpass.reshape(polar_count, chunk, count, col_count).transpose(2, 0, 3, 1)
    returned = unpack_slabs(
        exchange(pack_slabs(going), call_id + 1), (polar_count, col_count, chunk)
    )
    smoothed = returned.transpose(1, 2, 0, 3).reshape(polar_count, col_count, channels)
    new_top = jnp.where(at_north_end, smoothed, top_rows)
    new_bottom = jnp.where(at_south_end, smoothed, bottom_rows)
    return jnp.concatenate(
        [new_top, field[polar_count : row_count - polar_count], new_bottom], axis=0
    )


def chem_kernel(x_ref, seed_ref, cot_ref, sat_ref, spread_ref, group_ref, p_ref, g_ref):
    hi = lax.Precision.HIGHEST
    x = x_ref[0]
    seed = seed_ref[0]
    cot = cot_ref[0]
    sat = sat_ref[...]
    spread_m = spread_ref[...]
    group_m = group_ref[...]

    def up(v):
        return jnp.dot(v, spread_m, precision=hi, preferred_element_type=jnp.float32)

    def down(v):
        return jnp.dot(v, group_m, precision=hi, preferred_element_type=jnp.float32)

    root = jnp.sqrt(x * x + 1.0)
    mass = 0.5 * (x + root)
    aerosol = seed
    history = []
    for newton_step in range(NEWTON):
        denominator = up(aerosol) + sat
        fraction = mass / denominator
        first_sum = down(fraction)
        second_sum = down(fraction / denominator)
        residue = 1.0 - seed / aerosol - first_sum
        derivative = seed / (aerosol * aerosol) + second_sum
        history.append((aerosol, residue, derivative))
        aerosol = aerosol - residue / derivative
    aerosol_q = up(aerosol)
    final_den = aerosol_q + sat
    p_ref[0] = mass * aerosol_q / final_den
    mass_bar = cot * aerosol_q / final_den
    aerosol_bar = down(cot * mass * sat / (final_den * final_den))
    for newton_step in reversed(range(NEWTON)):
        a_n, residue, derivative = history[newton_step]
        inverse = 1.0 / (up(a_n) + sat)
        third_sum = down(mass * inverse * inverse * inverse)
        slope = -2.0 * (seed / (a_n * a_n * a_n) + third_sum)
        over_g = aerosol_bar / derivative
        over_g2 = over_g * residue / derivative
        mass_bar = mass_bar + up(over_g) * inverse + up(over_g2) * inverse * inverse
        aerosol_bar = over_g2 * slope
    g_ref[0] = mass_bar * 0.5 * (1.0 + x / root)


def chemistry_step(filtered, seed_aerosol, volatility, cotangent):
    rows, cols, channels = filtered.shape
    levels = seed_aerosol.shape[-1]
    species = volatility.shape[0]
    group_m = level_table(levels, species)
    spread_m = group_m.T
    sat = jnp.tile(volatility, levels)[None, :]
    big = pl.BlockSpec((1, cols, channels), lambda i: (i, 0, 0))
    small = pl.BlockSpec((1, cols, levels), lambda i: (i, 0, 0))
    return pl.pallas_call(
        chem_kernel,
        grid=(rows,),
        in_specs=[
            big,
            small,
            big,
            pl.BlockSpec((1, channels), lambda i: (0, 0)),
            pl.BlockSpec((levels, channels), lambda i: (0, 0)),
            pl.BlockSpec((channels, levels), lambda i: (0, 0)),
        ],
        out_specs=[big, big],
        out_shape=[
            jax.ShapeDtypeStruct(filtered.shape, jnp.float32),
            jax.ShapeDtypeStruct(filtered.shape, jnp.float32),
        ],
    )(filtered, seed_aerosol, cotangent, sat, spread_m, group_m)


def local(
    tracer,
    east_courant,
    north_courant,
    east_limiter,
    north_limiter,
    filter_keep,
    seed_aerosol,
    volatility,
    cotangent,
):
    row_count = tracer.shape[0]
    channels = tracer.shape[2]
    levels = east_courant.shape[2]
    species = volatility.shape[0]
    first_row = lax.axis_index("lat") * row_count
    packed = jnp.concatenate([tracer, east_courant, east_limiter.astype(jnp.float32)], axis=2)
    widened = east_west(packed)
    east_speed = widened[:, :, channels : channels + levels]
    east_choice = widened[:, :, channels + levels :].astype(jnp.int32)

    def zonal_only(window):
        return zonal_window(window, east_speed, east_choice, species)

    after_east, east_back = jax.vjp(zonal_only, widened[:, :, :channels])
    stacked = jnp.concatenate(
        [after_east, north_courant, north_limiter.astype(jnp.float32)], axis=2
    )
    tall_window = north_south(stacked)
    north_speed = tall_window[:, :, channels : channels + levels]
    north_choice = tall_window[:, :, channels + levels :].astype(jnp.int32)

    def meridional_only(window):
        return meridional_window(window, north_speed, north_choice, first_row, species)

    after_north, north_back = jax.vjp(meridional_only, tall_window[:, :, :channels])
    filtered = filter_field(after_north, filter_keep, 0)

    particle, chem_grad = chemistry_step(filtered, seed_aerosol, volatility, cotangent)
    adjoint_filtered = filter_field(chem_grad, filter_keep, 2)
    return (particle, fold_columns(east_back(fold_rows(north_back(adjoint_filtered)[0]))[0]))


def solution(mesh):
    in_specs = (
        P("lat", "lon", None),
        P("lat", "lon", None),
        P("lat", "lon", None),
        P("lat", "lon", None),
        P("lat", "lon", None),
        P("lat"),
        P("lat", "lon", None),
        P(),
        P("lat", "lon", None),
    )
    out_specs = (P("lat", "lon", None), P("lat", "lon", None))
    return jax.shard_map(local, mesh=mesh, in_specs=in_specs, out_specs=out_specs, check_vma=False)
```

```python
import math

import jax
import jax.numpy as jnp
from jax import lax
from jax.sharding import PartitionSpec as P
from jax.experimental import pallas as pl
from jax.experimental.pallas import tpu as pltpu

NEWTON = 4
KMAX = 32
POLAR = 2


def with_halo(cells, sides, width, closed):
    for axis, dim in sides:
        count = lax.axis_size(axis)
        ends = count if closed else count - 1
        head = lax.slice_in_dim(cells, 0, width, axis=dim)
        tail = lax.slice_in_dim(cells, cells.shape[dim] - width, cells.shape[dim], axis=dim)
        cells = jnp.concatenate(
            [
                lax.ppermute(tail, axis, [(i, (i + 1) % count) for i in range(ends)]),
                cells,
                lax.ppermute(head, axis, [((i + 1) % count, i) for i in range(ends)]),
            ],
            axis=dim,
        )
    return cells


def spread(values, copies):
    return jnp.repeat(values, copies, axis=-1)


def face_weights(courant, limiter):
    upwind = courant >= 0.0
    half = 0.5 * courant
    inner = courant * (7.0 / 12.0)
    outer = jnp.where(limiter == 0, courant * (-1.0 / 12.0), 0.0)
    near_left = jnp.where(
        limiter == 0, inner, jnp.where(limiter == 1, jnp.where(upwind, courant, 0.0), half)
    )
    near_right = jnp.where(
        limiter == 0, inner, jnp.where(limiter == 1, jnp.where(upwind, 0.0, courant), half)
    )
    return jnp.stack([outer, near_left, near_right], axis=0)


def spread_weights(weights, species):
    levels = weights.shape[-1]
    spread_m = level_table(levels, species).T
    return jnp.einsum("...l,lq->...q", weights, spread_m, precision=lax.Precision.HIGHEST)


def zonal_window(window, courant, limiter, species):
    inner_count = window.shape[1] - 4
    weights = spread_weights(
        face_weights(courant[:, 2 : inner_count + 3], limiter[:, 2 : inner_count + 3]), species
    )
    fluxes = (
        weights[0] * (window[:, 0 : inner_count + 1] + window[:, 3 : inner_count + 4])
        + weights[1] * window[:, 1 : inner_count + 2]
        + weights[2] * window[:, 2 : inner_count + 3]
    )
    return window[:, 2 : inner_count + 2] - (fluxes[:, 1:] - fluxes[:, :-1])


def meridional_window(window, courant, limiter, first_row, species):
    inner_count = window.shape[0] - 4
    face_rows = first_row + jnp.arange(inner_count + 1, dtype=jnp.int32)
    opened = jnp.where(face_rows[:, None, None] > 0, courant[2 : inner_count + 3], 0.0)
    weights = spread_weights(face_weights(opened, limiter[2 : inner_count + 3]), species)
    fluxes = (
        weights[0] * (window[0 : inner_count + 1] + window[3 : inner_count + 4])
        + weights[1] * window[1 : inner_count + 2]
        + weights[2] * window[2 : inner_count + 3]
    )
    return window[2 : inner_count + 2] - (fluxes[1:] - fluxes[:-1])


def positive(field):
    return 0.5 * (field + jnp.sqrt(field * field + 1.0))


def level_table(levels, species):
    channel_level = jnp.arange(levels * species, dtype=jnp.int32) // species
    return (channel_level[:, None] == jnp.arange(levels, dtype=jnp.int32)[None, :]).astype(
        jnp.float32
    )


def partition(total_mass, seed_aerosol, volatility):
    levels = seed_aerosol.shape[-1]
    species = volatility.shape[0]
    grouping = level_table(levels, species)
    saturation = jnp.tile(volatility, levels)
    aerosol = seed_aerosol
    for newton_step in range(NEWTON):
        denominator = spread(aerosol, species) + saturation
        fraction = total_mass / denominator
        first_sum = jnp.dot(fraction, grouping, precision=lax.Precision.HIGHEST)
        second_sum = jnp.dot(fraction / denominator, grouping, precision=lax.Precision.HIGHEST)
        residue = 1.0 - seed_aerosol / aerosol - first_sum
        derivative = seed_aerosol / (aerosol * aerosol) + second_sum
        aerosol = aerosol - residue / derivative
    aerosol_q = spread(aerosol, species)
    return total_mass * aerosol_q / (aerosol_q + saturation)


def east_west(field):
    return with_halo(field, (("lon", 1),), 2, True)


def north_south(field):
    return with_halo(field, (("lat", 0),), 2, False)


def fold_rows(gradient):
    inner_rows = gradient.shape[0] - 4
    rim_cells = jnp.concatenate([gradient[:2], gradient[inner_rows + 2 :]], axis=0)
    arrived = north_south(rim_cells)
    middle = gradient[2 : inner_rows + 2]
    return jnp.concatenate(
        [
            middle[:2] + arrived[:2],
            middle[2 : inner_rows - 2],
            middle[inner_rows - 2 :] + arrived[6:],
        ],
        axis=0,
    )


def fold_columns(gradient):
    inner_cols = gradient.shape[1] - 4
    rim_cells = jnp.concatenate([gradient[:, :2], gradient[:, inner_cols + 2 :]], axis=1)
    arrived = east_west(rim_cells)
    middle = gradient[:, 2 : inner_cols + 2]
    return jnp.concatenate(
        [
            middle[:, :2] + arrived[:, :2],
            middle[:, 2 : inner_cols - 2],
            middle[:, inner_cols - 2 :] + arrived[:, 6:],
        ],
        axis=1,
    )


def wave_table(column_count, length):
    position = jnp.arange(column_count, dtype=jnp.int32)
    numbers = jnp.arange(KMAX, dtype=jnp.int32)
    phases = position[:, None] * numbers[None, :] % length
    angles = phases.astype(jnp.float32) * (2.0 * math.pi / length)
    return jnp.concatenate([jnp.cos(angles), jnp.sin(angles)], axis=1)


def wave_weights(keep_values, length):
    numbers = jnp.arange(2 * KMAX, dtype=jnp.int32) % KMAX
    scaling = jnp.where(numbers == 0, 1.0, 2.0) / length
    kept_mask = numbers[None, :] < keep_values[:, None]
    return jnp.where(kept_mask, scaling[None, :], 0.0)


def lowpass_circles(circles, keep_values):
    length = circles.shape[2]
    table_full = wave_table(length, length)
    coefficient = jnp.einsum("rqn,nk->rqk", circles, table_full, precision=lax.Precision.HIGHEST)
    coefficient = coefficient * wave_weights(keep_values, length)[:, None, :]
    lowpass = jnp.einsum("rqk,nk->rqn", coefficient, table_full, precision=lax.Precision.HIGHEST)
    return jnp.where((keep_values <= KMAX)[:, None, None], lowpass, circles)


def exchange_kernel(x_ref, o_ref, landing, send_sems, recv_sems):
    count = x_ref.shape[0]
    me = lax.axis_index("lon")
    band = lax.axis_index("lat")
    bands = lax.axis_size("lat")
    active = jnp.logical_or(band == 0, band == bands - 1)

    def copy_to(offset):
        peer = lax.rem(me + offset, count)
        return pltpu.make_async_remote_copy(
            src_ref=x_ref.at[peer],
            dst_ref=landing.at[me],
            send_sem=send_sems.at[offset],
            recv_sem=recv_sems.at[me],
            device_id=(band, peer),
            device_id_type=pl.DeviceIdType.MESH,
        )

    def copy_from(offset):
        peer = lax.rem(me + count - offset, count)
        return pltpu.make_async_remote_copy(
            src_ref=x_ref.at[peer],
            dst_ref=landing.at[peer],
            send_sem=send_sems.at[offset],
            recv_sem=recv_sems.at[peer],
            device_id=(band, peer),
            device_id_type=pl.DeviceIdType.MESH,
        )

    @pl.when(active)
    def _():
        barrier = pltpu.get_barrier_semaphore()
        for offset in range(1, count):
            peer = lax.rem(me + offset, count)
            pl.semaphore_signal(
                barrier, 1, device_id=(band, peer), device_id_type=pl.DeviceIdType.MESH
            )
        pl.semaphore_wait(barrier, count - 1)
        for offset in range(1, count):
            copy_to(offset).start()
        for offset in range(1, count):
            copy_to(offset).wait_send()
        for offset in range(1, count):
            copy_from(offset).wait_recv()
        for offset in range(1, count):
            peer = lax.rem(me + count - offset, count)
            o_ref[pl.ds(peer, 1)] = landing[pl.ds(peer, 1)]

    o_ref[pl.ds(me, 1)] = x_ref[pl.ds(me, 1)]

    @pl.when(jnp.logical_not(active))
    def _():
        o_ref[...] = x_ref[...]


def exchange(slabs, call_id):
    return pl.pallas_call(
        exchange_kernel,
        out_shape=jax.ShapeDtypeStruct(slabs.shape, slabs.dtype),
        in_specs=[pl.BlockSpec(memory_space=pltpu.VMEM)],
        out_specs=pl.BlockSpec(memory_space=pltpu.VMEM),
        scratch_shapes=[
            pltpu.VMEM(slabs.shape, slabs.dtype),
            pltpu.SemaphoreType.DMA((slabs.shape[0],)),
            pltpu.SemaphoreType.DMA((slabs.shape[0],)),
        ],
        compiler_params=pltpu.CompilerParams(collective_id=call_id, has_side_effects=True),
    )(slabs)


def slab_rows(piece):
    return -(-piece // 1024) * 8


def pack_slabs(pieces):
    count = pieces.shape[0]
    piece = math.prod(pieces.shape[1:])
    rows = slab_rows(piece)
    flat = jnp.pad(pieces.reshape(count, piece), ((0, 0), (0, rows * 128 - piece)))
    return flat.reshape(count, rows, 128)


def unpack_slabs(slabs, shape):
    count = slabs.shape[0]
    piece = math.prod(shape)
    return slabs.reshape(count, -1)[:, :piece].reshape((count,) + tuple(shape))


def filter_field(field, filter_keep, call_id):
    row_count, col_count, channels = field.shape
    count = lax.axis_size("lon")
    chunk = channels // count
    polar_count = POLAR
    band = lax.axis_index("lat")
    at_north_end = band == 0
    at_south_end = band == lax.axis_size("lat") - 1
    top_rows = field[:polar_count]
    bottom_rows = field[row_count - polar_count :]
    end_rows = jnp.where(at_north_end, top_rows, bottom_rows)
    end_keep = jnp.where(
        at_north_end, filter_keep[:polar_count], filter_keep[row_count - polar_count :]
    )
    pieces = end_rows.reshape(polar_count, col_count, count, chunk).transpose(2, 0, 1, 3)
    arrived = unpack_slabs(
        exchange(pack_slabs(pieces), call_id), (polar_count, col_count, chunk)
    )
    circles = arrived.transpose(1, 3, 0, 2).reshape(polar_count, chunk, count * col_count)
    lowpass = lowpass_circles(circles, end_keep)
    going = lowpass.reshape(polar_count, chunk, count, col_count).transpose(2, 0, 3, 1)
    returned = unpack_slabs(
        exchange(pack_slabs(going), call_id + 1), (polar_count, col_count, chunk)
    )
    smoothed = returned.transpose(1, 2, 0, 3).reshape(polar_count, col_count, channels)
    new_top = jnp.where(at_north_end, smoothed, top_rows)
    new_bottom = jnp.where(at_south_end, smoothed, bottom_rows)
    return jnp.concatenate(
        [new_top, field[polar_count : row_count - polar_count], new_bottom], axis=0
    )


def chem_kernel(x_ref, seed_ref, cot_ref, sat_ref, spread_ref, group_ref, p_ref, g_ref):
    hi = lax.Precision.HIGHEST
    x = x_ref[0]
    seed = seed_ref[0]
    cot = cot_ref[0]
    sat = sat_ref[...]
    spread_m = spread_ref[...]
    group_m = group_ref[...]

    def up(v):
        return jnp.dot(v, spread_m, precision=hi, preferred_element_type=jnp.float32)

    def down(v):
        return jnp.dot(v, group_m, precision=hi, preferred_element_type=jnp.float32)

    root = jnp.sqrt(x * x + 1.0)
    mass = 0.5 * (x + root)
    aerosol = seed
    history = []
    for newton_step in range(NEWTON):
        denominator = up(aerosol) + sat
        fraction = mass / denominator
        first_sum = down(fraction)
        second_sum = down(fraction / denominator)
        residue = 1.0 - seed / aerosol - first_sum
        derivative = seed / (aerosol * aerosol) + second_sum
        history.append((aerosol, residue, derivative))
        aerosol = aerosol - residue / derivative
    aerosol_q = up(aerosol)
    final_den = aerosol_q + sat
    p_ref[0] = mass * aerosol_q / final_den
    mass_bar = cot * aerosol_q / final_den
    aerosol_bar = down(cot * mass * sat / (final_den * final_den))
    for newton_step in reversed(range(NEWTON)):
        a_n, residue, derivative = history[newton_step]
        inverse = 1.0 / (up(a_n) + sat)
        third_sum = down(mass * inverse * inverse * inverse)
        slope = -2.0 * (seed / (a_n * a_n * a_n) + third_sum)
        over_g = aerosol_bar / derivative
        over_g2 = over_g * residue / derivative
        mass_bar = mass_bar + up(over_g) * inverse + up(over_g2) * inverse * inverse
        aerosol_bar = over_g2 * slope
    g_ref[0] = mass_bar * 0.5 * (1.0 + x / root)


def chemistry_step(filtered, seed_aerosol, volatility, cotangent):
    rows, cols, channels = filtered.shape
    levels = seed_aerosol.shape[-1]
    species = volatility.shape[0]
    group_m = level_table(levels, species)
    spread_m = group_m.T
    sat = jnp.tile(volatility, levels)[None, :]
    big = pl.BlockSpec((1, cols, channels), lambda i: (i, 0, 0))
    small = pl.BlockSpec((1, cols, levels), lambda i: (i, 0, 0))
    return pl.pallas_call(
        chem_kernel,
        grid=(rows,),
        in_specs=[
            big,
            small,
            big,
            pl.BlockSpec((1, channels), lambda i: (0, 0)),
            pl.BlockSpec((levels, channels), lambda i: (0, 0)),
            pl.BlockSpec((channels, levels), lambda i: (0, 0)),
        ],
        out_specs=[big, big],
        out_shape=[
            jax.ShapeDtypeStruct(filtered.shape, jnp.float32),
            jax.ShapeDtypeStruct(filtered.shape, jnp.float32),
        ],
    )(filtered, seed_aerosol, cotangent, sat, spread_m, group_m)


def local(
    tracer,
    east_courant,
    north_courant,
    east_limiter,
    north_limiter,
    filter_keep,
    seed_aerosol,
    volatility,
    cotangent,
):
    row_count = tracer.shape[0]
    channels = tracer.shape[2]
    levels = east_courant.shape[2]
    species = volatility.shape[0]
    first_row = lax.axis_index("lat") * row_count
    packed = jnp.concatenate([tracer, east_courant, east_limiter.astype(jnp.float32)], axis=2)
    widened = east_west(packed)
    east_speed = widened[:, :, channels : channels + levels]
    east_choice = widened[:, :, channels + levels :].astype(jnp.int32)

    def zonal_only(window):
        return zonal_window(window, east_speed, east_choice, species)

    after_east, east_back = jax.vjp(zonal_only, widened[:, :, :channels])
    stacked = jnp.concatenate(
        [after_east, north_courant, north_limiter.astype(jnp.float32)], axis=2
    )
    tall_window = north_south(stacked)
    north_speed = tall_window[:, :, channels : channels + levels]
    north_choice = tall_window[:, :, channels + levels :].astype(jnp.int32)

    def meridional_only(window):
        return meridional_window(window, north_speed, north_choice, first_row, species)

    after_north, north_back = jax.vjp(meridional_only, tall_window[:, :, :channels])
    filtered = filter_field(after_north, filter_keep, 0)

    particle, chem_grad = chemistry_step(filtered, seed_aerosol, volatility, cotangent)
    adjoint_filtered = filter_field(chem_grad, filter_keep, 2)
    return (particle, fold_columns(east_back(fold_rows(north_back(adjoint_filtered)[0]))[0]))


def solution(mesh):
    in_specs = (
        P("lat", "lon", None),
        P("lat", "lon", None),
        P("lat", "lon", None),
        P("lat", "lon", None),
        P("lat", "lon", None),
        P("lat"),
        P("lat", "lon", None),
        P(),
        P("lat", "lon", None),
    )
    out_specs = (P("lat", "lon", None), P("lat", "lon", None))
    return jax.shard_map(local, mesh=mesh, in_specs=in_specs, out_specs=out_specs, check_vma=False)
```

```python
import math

import jax
import jax.numpy as jnp
from jax import lax
from jax.sharding import PartitionSpec as P
from jax.experimental import pallas as pl
from jax.experimental.pallas import tpu as pltpu

NEWTON = 4
KMAX = 32
POLAR = 2


def with_halo(cells, sides, width, closed):
    for axis, dim in sides:
        count = lax.axis_size(axis)
        ends = count if closed else count - 1
        head = lax.slice_in_dim(cells, 0, width, axis=dim)
        tail = lax.slice_in_dim(cells, cells.shape[dim] - width, cells.shape[dim], axis=dim)
        cells = jnp.concatenate(
            [
                lax.ppermute(tail, axis, [(i, (i + 1) % count) for i in range(ends)]),
                cells,
                lax.ppermute(head, axis, [((i + 1) % count, i) for i in range(ends)]),
            ],
            axis=dim,
        )
    return cells


def spread(values, copies):
    return jnp.repeat(values, copies, axis=-1)


def face_weights(courant, limiter):
    upwind = courant >= 0.0
    half = 0.5 * courant
    inner = courant * (7.0 / 12.0)
    outer = jnp.where(limiter == 0, courant * (-1.0 / 12.0), 0.0)
    near_left = jnp.where(
        limiter == 0, inner, jnp.where(limiter == 1, jnp.where(upwind, courant, 0.0), half)
    )
    near_right = jnp.where(
        limiter == 0, inner, jnp.where(limiter == 1, jnp.where(upwind, 0.0, courant), half)
    )
    return jnp.stack([outer, near_left, near_right], axis=0)


def spread_weights(weights, species):
    levels = weights.shape[-1]
    spread_m = level_table(levels, species).T
    return jnp.einsum("...l,lq->...q", weights, spread_m, precision=lax.Precision.HIGHEST)


def zonal_window(window, courant, limiter, species):
    inner_count = window.shape[1] - 4
    weights = spread_weights(
        face_weights(courant[:, 2 : inner_count + 3], limiter[:, 2 : inner_count + 3]), species
    )
    fluxes = (
        weights[0] * (window[:, 0 : inner_count + 1] + window[:, 3 : inner_count + 4])
        + weights[1] * window[:, 1 : inner_count + 2]
        + weights[2] * window[:, 2 : inner_count + 3]
    )
    return window[:, 2 : inner_count + 2] - (fluxes[:, 1:] - fluxes[:, :-1])


def meridional_window(window, courant, limiter, first_row, species):
    inner_count = window.shape[0] - 4
    face_rows = first_row + jnp.arange(inner_count + 1, dtype=jnp.int32)
    opened = jnp.where(face_rows[:, None, None] > 0, courant[2 : inner_count + 3], 0.0)
    weights = spread_weights(face_weights(opened, limiter[2 : inner_count + 3]), species)
    fluxes = (
        weights[0] * (window[0 : inner_count + 1] + window[3 : inner_count + 4])
        + weights[1] * window[1 : inner_count + 2]
        + weights[2] * window[2 : inner_count + 3]
    )
    return window[2 : inner_count + 2] - (fluxes[1:] - fluxes[:-1])


def positive(field):
    return 0.5 * (field + jnp.sqrt(field * field + 1.0))


def level_table(levels, species):
    channel_level = jnp.arange(levels * species, dtype=jnp.int32) // species
    return (channel_level[:, None] == jnp.arange(levels, dtype=jnp.int32)[None, :]).astype(
        jnp.float32
    )


def partition(total_mass, seed_aerosol, volatility):
    levels = seed_aerosol.shape[-1]
    species = volatility.shape[0]
    grouping = level_table(levels, species)
    saturation = jnp.tile(volatility, levels)
    aerosol = seed_aerosol
    for newton_step in range(NEWTON):
        denominator = spread(aerosol, species) + saturation
        fraction = total_mass / denominator
        first_sum = jnp.dot(fraction, grouping, precision=lax.Precision.HIGHEST)
        second_sum = jnp.dot(fraction / denominator, grouping, precision=lax.Precision.HIGHEST)
        residue = 1.0 - seed_aerosol / aerosol - first_sum
        derivative = seed_aerosol / (aerosol * aerosol) + second_sum
        aerosol = aerosol - residue / derivative
    aerosol_q = spread(aerosol, species)
    return total_mass * aerosol_q / (aerosol_q + saturation)


def east_west(field):
    return with_halo(field, (("lon", 1),), 2, True)


def north_south(field):
    return with_halo(field, (("lat", 0),), 2, False)


def fold_rows(gradient):
    inner_rows = gradient.shape[0] - 4
    rim_cells = jnp.concatenate([gradient[:2], gradient[inner_rows + 2 :]], axis=0)
    arrived = north_south(rim_cells)
    middle = gradient[2 : inner_rows + 2]
    return jnp.concatenate(
        [
            middle[:2] + arrived[:2],
            middle[2 : inner_rows - 2],
            middle[inner_rows - 2 :] + arrived[6:],
        ],
        axis=0,
    )


def fold_columns(gradient):
    inner_cols = gradient.shape[1] - 4
    rim_cells = jnp.concatenate([gradient[:, :2], gradient[:, inner_cols + 2 :]], axis=1)
    arrived = east_west(rim_cells)
    middle = gradient[:, 2 : inner_cols + 2]
    return jnp.concatenate(
        [
            middle[:, :2] + arrived[:, :2],
            middle[:, 2 : inner_cols - 2],
            middle[:, inner_cols - 2 :] + arrived[:, 6:],
        ],
        axis=1,
    )


def wave_table(column_count, length):
    position = jnp.arange(column_count, dtype=jnp.int32)
    numbers = jnp.arange(KMAX, dtype=jnp.int32)
    phases = position[:, None] * numbers[None, :] % length
    angles = phases.astype(jnp.float32) * (2.0 * math.pi / length)
    return jnp.concatenate([jnp.cos(angles), jnp.sin(angles)], axis=1)


def wave_weights(keep_values, length):
    numbers = jnp.arange(2 * KMAX, dtype=jnp.int32) % KMAX
    scaling = jnp.where(numbers == 0, 1.0, 2.0) / length
    kept_mask = numbers[None, :] < keep_values[:, None]
    return jnp.where(kept_mask, scaling[None, :], 0.0)


def lowpass_circles(circles, keep_values):
    length = circles.shape[2]
    table_full = wave_table(length, length)
    coefficient = jnp.einsum("rqn,nk->rqk", circles, table_full, precision=lax.Precision.HIGHEST)
    coefficient = coefficient * wave_weights(keep_values, length)[:, None, :]
    lowpass = jnp.einsum("rqk,nk->rqn", coefficient, table_full, precision=lax.Precision.HIGHEST)
    return jnp.where((keep_values <= KMAX)[:, None, None], lowpass, circles)


def polar_kernel(x_ref, w_ref, t_ref, y_ref, out_go, land_go, out_back, land_back,
                 sem_a, sem_b, sem_c, sem_d):
    count = t_ref.shape[0]
    polar_count, col_count, channels = x_ref.shape
    chunk = channels // count
    padded = out_go.shape[1]
    me = lax.axis_index("lon")
    band = lax.axis_index("lat")
    bands = lax.axis_size("lat")
    active = jnp.logical_or(band == 0, band == bands - 1)
    hi = lax.Precision.HIGHEST
    mesh_id = pl.DeviceIdType.MESH

    def remote(src, dst, send_sem, recv_sem, peer):
        return pltpu.make_async_remote_copy(
            src_ref=src, dst_ref=dst, send_sem=send_sem, recv_sem=recv_sem,
            device_id=(band, peer), device_id_type=mesh_id,
        )

    def round_trip(outbox, inbox, send_sems, recv_sems):
        for offset in range(1, count):
            peer = lax.rem(me + offset, count)
            remote(outbox.at[peer], inbox.at[me], send_sems.at[offset], recv_sems.at[me], peer).start()
        inbox[pl.ds(me, 1)] = outbox[pl.ds(me, 1)]
        for offset in range(1, count):
            peer = lax.rem(me + offset, count)
            remote(outbox.at[peer], inbox.at[me], send_sems.at[offset], recv_sems.at[me], peer).wait_send()
        for offset in range(1, count):
            peer = lax.rem(me + count - offset, count)
            remote(outbox.at[peer], inbox.at[peer], send_sems.at[offset], recv_sems.at[peer], peer).wait_recv()

    @pl.when(active)
    def _():
        barrier = pltpu.get_barrier_semaphore()
        for offset in range(1, count):
            peer = lax.rem(me + offset, count)
            pl.semaphore_signal(barrier, 1, device_id=(band, peer), device_id_type=mesh_id)
        pl.semaphore_wait(barrier, count - 1)
        rows = jnp.concatenate([x_ref[r] for r in range(polar_count)], axis=0)
        slot = lax.broadcasted_iota(jnp.int32, (count * padded, channels), 0)
        channel = lax.broadcasted_iota(jnp.int32, (count * padded, channels), 1)
        target = (channel // chunk) * padded + channel % chunk
        packer = jnp.where(slot == target, 1.0, 0.0).astype(jnp.float32)
        packed = lax.dot_general(packer, rows, (((1,), (1,)), ((), ())), precision=hi,
                                 preferred_element_type=jnp.float32)
        out_go[...] = packed.reshape(count, padded, polar_count * col_count)
        round_trip(out_go, land_go, sem_a, sem_b)

        def analyse(s, acc):
            return acc + jnp.dot(land_go[s], t_ref[s], precision=hi,
                                 preferred_element_type=jnp.float32)

        coefficient = lax.fori_loop(
            0, count, analyse, jnp.zeros((padded, t_ref.shape[2]), jnp.float32)
        )
        coefficient = coefficient * w_ref[...]

        def synthesise(s, carry):
            out_back[s] = lax.dot_general(coefficient, t_ref[s], (((1,), (1,)), ((), ())),
                                          precision=hi, preferred_element_type=jnp.float32)
            return carry

        lax.fori_loop(0, count, synthesise, 0)
        round_trip(out_back, land_back, sem_c, sem_d)
        back = land_back[...].reshape(count * padded, polar_count * col_count)
        result = lax.dot_general(back, packer, (((0,), (0,)), ((), ())), precision=hi,
                                 preferred_element_type=jnp.float32)
        for r in range(polar_count):
            y_ref[r] = result[r * col_count : (r + 1) * col_count]

    @pl.when(jnp.logical_not(active))
    def _():
        y_ref[...] = x_ref[...]


def polar_lowpass(end_rows, weights, blocks, call_id):
    polar_count, col_count, channels = end_rows.shape
    count = blocks.shape[0]
    padded = -(-(channels // count) // 8) * 8
    slab = (count, padded, polar_count * col_count)
    vmem = pl.BlockSpec(memory_space=pltpu.VMEM)
    return pl.pallas_call(
        polar_kernel,
        out_shape=jax.ShapeDtypeStruct(end_rows.shape, end_rows.dtype),
        in_specs=[vmem, vmem, vmem],
        out_specs=vmem,
        scratch_shapes=[
            pltpu.VMEM(slab, jnp.float32),
            pltpu.VMEM(slab, jnp.float32),
            pltpu.VMEM(slab, jnp.float32),
            pltpu.VMEM(slab, jnp.float32),
            pltpu.SemaphoreType.DMA((count,)),
            pltpu.SemaphoreType.DMA((count,)),
            pltpu.SemaphoreType.DMA((count,)),
            pltpu.SemaphoreType.DMA((count,)),
        ],
        compiler_params=pltpu.CompilerParams(collective_id=call_id, has_side_effects=True),
    )(end_rows, weights, blocks)


def filter_field(field, filter_keep, call_id):
    row_count, col_count, channels = field.shape
    count = lax.axis_size("lon")
    length = col_count * count
    polar_count = POLAR
    band = lax.axis_index("lat")
    at_north_end = band == 0
    at_south_end = band == lax.axis_size("lat") - 1
    top_rows = field[:polar_count]
    bottom_rows = field[row_count - polar_count :]
    end_rows = jnp.where(at_north_end, top_rows, bottom_rows)
    end_keep = jnp.where(
        at_north_end, filter_keep[:polar_count], filter_keep[row_count - polar_count :]
    )
    table = wave_table(length, length).reshape(count, col_count, 2 * KMAX)
    blocks = jnp.einsum(
        "sjk,rR->srjRk", table, jnp.eye(polar_count, dtype=jnp.float32)
    ).reshape(count, polar_count * col_count, polar_count * 2 * KMAX)
    weights = wave_weights(end_keep, length).reshape(1, polar_count * 2 * KMAX)
    lowpass = polar_lowpass(end_rows, weights, blocks, call_id)
    smoothed = jnp.where((end_keep <= KMAX)[:, None, None], lowpass, end_rows)
    new_top = jnp.where(at_north_end, smoothed, top_rows)
    new_bottom = jnp.where(at_south_end, smoothed, bottom_rows)
    return jnp.concatenate(
        [new_top, field[polar_count : row_count - polar_count], new_bottom], axis=0
    )


def chem_kernel(x_ref, seed_ref, cot_ref, sat_ref, spread_ref, group_ref, p_ref, g_ref):
    hi = lax.Precision.HIGHEST
    x = x_ref[0]
    seed = seed_ref[0]
    cot = cot_ref[0]
    sat = sat_ref[...]
    spread_m = spread_ref[...]
    group_m = group_ref[...]

    def up(v):
        return jnp.dot(v, spread_m, precision=hi, preferred_element_type=jnp.float32)

    def down(v):
        return jnp.dot(v, group_m, precision=hi, preferred_element_type=jnp.float32)

    root = jnp.sqrt(x * x + 1.0)
    mass = 0.5 * (x + root)
    aerosol = seed
    history = []
    for newton_step in range(NEWTON):
        denominator = up(aerosol) + sat
        fraction = mass / denominator
        first_sum = down(fraction)
        second_sum = down(fraction / denominator)
        residue = 1.0 - seed / aerosol - first_sum
        derivative = seed / (aerosol * aerosol) + second_sum
        history.append((aerosol, residue, derivative))
        aerosol = aerosol - residue / derivative
    aerosol_q = up(aerosol)
    final_den = aerosol_q + sat
    p_ref[0] = mass * aerosol_q / final_den
    mass_bar = cot * aerosol_q / final_den
    aerosol_bar = down(cot * mass * sat / (final_den * final_den))
    for newton_step in reversed(range(NEWTON)):
        a_n, residue, derivative = history[newton_step]
        inverse = 1.0 / (up(a_n) + sat)
        third_sum = down(mass * inverse * inverse * inverse)
        slope = -2.0 * (seed / (a_n * a_n * a_n) + third_sum)
        over_g = aerosol_bar / derivative
        over_g2 = over_g * residue / derivative
        mass_bar = mass_bar + up(over_g) * inverse + up(over_g2) * inverse * inverse
        aerosol_bar = over_g2 * slope
    g_ref[0] = mass_bar * 0.5 * (1.0 + x / root)


def chemistry_step(filtered, seed_aerosol, volatility, cotangent):
    rows, cols, channels = filtered.shape
    levels = seed_aerosol.shape[-1]
    species = volatility.shape[0]
    group_m = level_table(levels, species)
    spread_m = group_m.T
    sat = jnp.tile(volatility, levels)[None, :]
    big = pl.BlockSpec((1, cols, channels), lambda i: (i, 0, 0))
    small = pl.BlockSpec((1, cols, levels), lambda i: (i, 0, 0))
    return pl.pallas_call(
        chem_kernel,
        grid=(rows,),
        in_specs=[
            big,
            small,
            big,
            pl.BlockSpec((1, channels), lambda i: (0, 0)),
            pl.BlockSpec((levels, channels), lambda i: (0, 0)),
            pl.BlockSpec((channels, levels), lambda i: (0, 0)),
        ],
        out_specs=[big, big],
        out_shape=[
            jax.ShapeDtypeStruct(filtered.shape, jnp.float32),
            jax.ShapeDtypeStruct(filtered.shape, jnp.float32),
        ],
    )(filtered, seed_aerosol, cotangent, sat, spread_m, group_m)


def local(
    tracer,
    east_courant,
    north_courant,
    east_limiter,
    north_limiter,
    filter_keep,
    seed_aerosol,
    volatility,
    cotangent,
):
    row_count = tracer.shape[0]
    channels = tracer.shape[2]
    levels = east_courant.shape[2]
    species = volatility.shape[0]
    first_row = lax.axis_index("lat") * row_count
    packed = jnp.concatenate([tracer, east_courant, east_limiter.astype(jnp.float32)], axis=2)
    widened = east_west(packed)
    east_speed = widened[:, :, channels : channels + levels]
    east_choice = widened[:, :, channels + levels :].astype(jnp.int32)

    def zonal_only(window):
        return zonal_window(window, east_speed, east_choice, species)

    after_east, east_back = jax.vjp(zonal_only, widened[:, :, :channels])
    stacked = jnp.concatenate(
        [after_east, north_courant, north_limiter.astype(jnp.float32)], axis=2
    )
    tall_window = north_south(stacked)
    north_speed = tall_window[:, :, channels : channels + levels]
    north_choice = tall_window[:, :, channels + levels :].astype(jnp.int32)

    def meridional_only(window):
        return meridional_window(window, north_speed, north_choice, first_row, species)

    after_north, north_back = jax.vjp(meridional_only, tall_window[:, :, :channels])
    filtered = filter_field(after_north, filter_keep, 0)

    particle, chem_grad = chemistry_step(filtered, seed_aerosol, volatility, cotangent)
    adjoint_filtered = filter_field(chem_grad, filter_keep, 1)
    return (particle, fold_columns(east_back(fold_rows(north_back(adjoint_filtered)[0]))[0]))


def solution(mesh):
    in_specs = (
        P("lat", "lon", None),
        P("lat", "lon", None),
        P("lat", "lon", None),
        P("lat", "lon", None),
        P("lat", "lon", None),
        P("lat"),
        P("lat", "lon", None),
        P(),
        P("lat", "lon", None),
    )
    out_specs = (P("lat", "lon", None), P("lat", "lon", None))
    return jax.shard_map(local, mesh=mesh, in_specs=in_specs, out_specs=out_specs, check_vma=False)
```

```python
import math

import jax
import jax.numpy as jnp
from jax import lax
from jax.sharding import PartitionSpec as P
from jax.experimental import pallas as pl
from jax.experimental.pallas import tpu as pltpu

NEWTON = 4
KMAX = 32
POLAR = 2


def with_halo(cells, sides, width, closed):
    for axis, dim in sides:
        count = lax.axis_size(axis)
        ends = count if closed else count - 1
        head = lax.slice_in_dim(cells, 0, width, axis=dim)
        tail = lax.slice_in_dim(cells, cells.shape[dim] - width, cells.shape[dim], axis=dim)
        cells = jnp.concatenate(
            [
                lax.ppermute(tail, axis, [(i, (i + 1) % count) for i in range(ends)]),
                cells,
                lax.ppermute(head, axis, [((i + 1) % count, i) for i in range(ends)]),
            ],
            axis=dim,
        )
    return cells


def spread(values, copies):
    return jnp.repeat(values, copies, axis=-1)


def face_weights(courant, limiter):
    upwind = courant >= 0.0
    half = 0.5 * courant
    inner = courant * (7.0 / 12.0)
    outer = jnp.where(limiter == 0, courant * (-1.0 / 12.0), 0.0)
    near_left = jnp.where(
        limiter == 0, inner, jnp.where(limiter == 1, jnp.where(upwind, courant, 0.0), half)
    )
    near_right = jnp.where(
        limiter == 0, inner, jnp.where(limiter == 1, jnp.where(upwind, 0.0, courant), half)
    )
    return jnp.stack([outer, near_left, near_right], axis=0)


def spread_weights(weights, species):
    levels = weights.shape[-1]
    spread_m = level_table(levels, species).T
    return jnp.einsum("...l,lq->...q", weights, spread_m, precision=lax.Precision.HIGHEST)


def zonal_window(window, courant, limiter, species):
    inner_count = window.shape[1] - 4
    weights = spread_weights(
        face_weights(courant[:, 2 : inner_count + 3], limiter[:, 2 : inner_count + 3]), species
    )
    fluxes = (
        weights[0] * (window[:, 0 : inner_count + 1] + window[:, 3 : inner_count + 4])
        + weights[1] * window[:, 1 : inner_count + 2]
        + weights[2] * window[:, 2 : inner_count + 3]
    )
    return window[:, 2 : inner_count + 2] - (fluxes[:, 1:] - fluxes[:, :-1])


def meridional_window(window, courant, limiter, first_row, species):
    inner_count = window.shape[0] - 4
    face_rows = first_row + jnp.arange(inner_count + 1, dtype=jnp.int32)
    opened = jnp.where(face_rows[:, None, None] > 0, courant[2 : inner_count + 3], 0.0)
    weights = spread_weights(face_weights(opened, limiter[2 : inner_count + 3]), species)
    fluxes = (
        weights[0] * (window[0 : inner_count + 1] + window[3 : inner_count + 4])
        + weights[1] * window[1 : inner_count + 2]
        + weights[2] * window[2 : inner_count + 3]
    )
    return window[2 : inner_count + 2] - (fluxes[1:] - fluxes[:-1])


def positive(field):
    return 0.5 * (field + jnp.sqrt(field * field + 1.0))


def level_table(levels, species):
    channel_level = jnp.arange(levels * species, dtype=jnp.int32) // species
    return (channel_level[:, None] == jnp.arange(levels, dtype=jnp.int32)[None, :]).astype(
        jnp.float32
    )


def partition(total_mass, seed_aerosol, volatility):
    levels = seed_aerosol.shape[-1]
    species = volatility.shape[0]
    grouping = level_table(levels, species)
    saturation = jnp.tile(volatility, levels)
    aerosol = seed_aerosol
    for newton_step in range(NEWTON):
        denominator = spread(aerosol, species) + saturation
        fraction = total_mass / denominator
        first_sum = jnp.dot(fraction, grouping, precision=lax.Precision.HIGHEST)
        second_sum = jnp.dot(fraction / denominator, grouping, precision=lax.Precision.HIGHEST)
        residue = 1.0 - seed_aerosol / aerosol - first_sum
        derivative = seed_aerosol / (aerosol * aerosol) + second_sum
        aerosol = aerosol - residue / derivative
    aerosol_q = spread(aerosol, species)
    return total_mass * aerosol_q / (aerosol_q + saturation)


def east_west(field):
    return with_halo(field, (("lon", 1),), 2, True)


def north_south(field):
    return with_halo(field, (("lat", 0),), 2, False)


def fold_rows(gradient):
    inner_rows = gradient.shape[0] - 4
    rim_cells = jnp.concatenate([gradient[:2], gradient[inner_rows + 2 :]], axis=0)
    arrived = north_south(rim_cells)
    middle = gradient[2 : inner_rows + 2]
    return jnp.concatenate(
        [
            middle[:2] + arrived[:2],
            middle[2 : inner_rows - 2],
            middle[inner_rows - 2 :] + arrived[6:],
        ],
        axis=0,
    )


def fold_columns(gradient):
    inner_cols = gradient.shape[1] - 4
    rim_cells = jnp.concatenate([gradient[:, :2], gradient[:, inner_cols + 2 :]], axis=1)
    arrived = east_west(rim_cells)
    middle = gradient[:, 2 : inner_cols + 2]
    return jnp.concatenate(
        [
            middle[:, :2] + arrived[:, :2],
            middle[:, 2 : inner_cols - 2],
            middle[:, inner_cols - 2 :] + arrived[:, 6:],
        ],
        axis=1,
    )


def wave_table(column_count, length):
    position = jnp.arange(column_count, dtype=jnp.int32)
    numbers = jnp.arange(KMAX, dtype=jnp.int32)
    phases = position[:, None] * numbers[None, :] % length
    angles = phases.astype(jnp.float32) * (2.0 * math.pi / length)
    return jnp.concatenate([jnp.cos(angles), jnp.sin(angles)], axis=1)


def wave_weights(keep_values, length):
    numbers = jnp.arange(2 * KMAX, dtype=jnp.int32) % KMAX
    scaling = jnp.where(numbers == 0, 1.0, 2.0) / length
    kept_mask = numbers[None, :] < keep_values[:, None]
    return jnp.where(kept_mask, scaling[None, :], 0.0)


def lowpass_circles(circles, keep_values):
    length = circles.shape[2]
    table_full = wave_table(length, length)
    coefficient = jnp.einsum("rqn,nk->rqk", circles, table_full, precision=lax.Precision.HIGHEST)
    coefficient = coefficient * wave_weights(keep_values, length)[:, None, :]
    lowpass = jnp.einsum("rqk,nk->rqn", coefficient, table_full, precision=lax.Precision.HIGHEST)
    return jnp.where((keep_values <= KMAX)[:, None, None], lowpass, circles)


def split_three(values):
    high = values.astype(jnp.bfloat16)
    rest = values - high.astype(jnp.float32)
    middle = rest.astype(jnp.bfloat16)
    low = (rest - middle.astype(jnp.float32)).astype(jnp.bfloat16)
    return high, middle, low


def select_dot(values, selector, dims):
    total = None
    for piece in split_three(values):
        term = lax.dot_general(piece, selector, dims, preferred_element_type=jnp.float32)
        total = term if total is None else total + term
    return total


def select_dot_left(selector, values, dims):
    total = None
    for piece in split_three(values):
        term = lax.dot_general(selector, piece, dims, preferred_element_type=jnp.float32)
        total = term if total is None else total + term
    return total


def polar_kernel(x_ref, w_ref, t_ref, y_ref, out_go, land_go, out_back, land_back,
                 sem_a, sem_b, sem_c, sem_d):
    count = t_ref.shape[0]
    polar_count, col_count, channels = x_ref.shape
    chunk = channels // count
    padded = out_go.shape[1]
    me = lax.axis_index("lon")
    band = lax.axis_index("lat")
    bands = lax.axis_size("lat")
    active = jnp.logical_or(band == 0, band == bands - 1)
    hi = lax.Precision.HIGHEST
    mesh_id = pl.DeviceIdType.MESH

    def remote(src, dst, send_sem, recv_sem, peer):
        return pltpu.make_async_remote_copy(
            src_ref=src, dst_ref=dst, send_sem=send_sem, recv_sem=recv_sem,
            device_id=(band, peer), device_id_type=mesh_id,
        )

    def round_trip(outbox, inbox, send_sems, recv_sems):
        for offset in range(1, count):
            peer = lax.rem(me + offset, count)
            remote(outbox.at[peer], inbox.at[me], send_sems.at[offset], recv_sems.at[me], peer).start()
        inbox[pl.ds(me, 1)] = outbox[pl.ds(me, 1)]
        for offset in range(1, count):
            peer = lax.rem(me + offset, count)
            remote(outbox.at[peer], inbox.at[me], send_sems.at[offset], recv_sems.at[me], peer).wait_send()
        for offset in range(1, count):
            peer = lax.rem(me + count - offset, count)
            remote(outbox.at[peer], inbox.at[peer], send_sems.at[offset], recv_sems.at[peer], peer).wait_recv()

    @pl.when(active)
    def _():
        barrier = pltpu.get_barrier_semaphore()
        for offset in range(1, count):
            peer = lax.rem(me + offset, count)
            pl.semaphore_signal(barrier, 1, device_id=(band, peer), device_id_type=mesh_id)
        pl.semaphore_wait(barrier, count - 1)
        rows = jnp.concatenate([x_ref[r] for r in range(polar_count)], axis=0)
        slot = lax.broadcasted_iota(jnp.int32, (count * padded, channels), 0)
        channel = lax.broadcasted_iota(jnp.int32, (count * padded, channels), 1)
        target = (channel // chunk) * padded + channel % chunk
        packer = jnp.where(slot == target, 1.0, 0.0).astype(jnp.bfloat16)
        packed = select_dot_left(packer, rows, (((1,), (1,)), ((), ())))
        out_go[...] = packed.reshape(count, padded, polar_count * col_count)
        round_trip(out_go, land_go, sem_a, sem_b)

        def analyse(s, acc):
            return acc + jnp.dot(land_go[s], t_ref[s], precision=hi,
                                 preferred_element_type=jnp.float32)

        coefficient = lax.fori_loop(
            0, count, analyse, jnp.zeros((padded, t_ref.shape[2]), jnp.float32)
        )
        coefficient = coefficient * w_ref[...]

        def synthesise(s, carry):
            out_back[s] = lax.dot_general(coefficient, t_ref[s], (((1,), (1,)), ((), ())),
                                          precision=hi, preferred_element_type=jnp.float32)
            return carry

        lax.fori_loop(0, count, synthesise, 0)
        round_trip(out_back, land_back, sem_c, sem_d)
        back = land_back[...].reshape(count * padded, polar_count * col_count)
        result = select_dot(back, packer, (((0,), (0,)), ((), ())))
        for r in range(polar_count):
            y_ref[r] = result[r * col_count : (r + 1) * col_count]

    @pl.when(jnp.logical_not(active))
    def _():
        y_ref[...] = x_ref[...]


def polar_lowpass(end_rows, weights, blocks, call_id):
    polar_count, col_count, channels = end_rows.shape
    count = blocks.shape[0]
    padded = -(-(channels // count) // 8) * 8
    slab = (count, padded, polar_count * col_count)
    vmem = pl.BlockSpec(memory_space=pltpu.VMEM)
    return pl.pallas_call(
        polar_kernel,
        out_shape=jax.ShapeDtypeStruct(end_rows.shape, end_rows.dtype),
        in_specs=[vmem, vmem, vmem],
        out_specs=vmem,
        scratch_shapes=[
            pltpu.VMEM(slab, jnp.float32),
            pltpu.VMEM(slab, jnp.float32),
            pltpu.VMEM(slab, jnp.float32),
            pltpu.VMEM(slab, jnp.float32),
            pltpu.SemaphoreType.DMA((count,)),
            pltpu.SemaphoreType.DMA((count,)),
            pltpu.SemaphoreType.DMA((count,)),
            pltpu.SemaphoreType.DMA((count,)),
        ],
        compiler_params=pltpu.CompilerParams(collective_id=call_id, has_side_effects=True),
    )(end_rows, weights, blocks)


def filter_field(field, filter_keep, call_id):
    row_count, col_count, channels = field.shape
    count = lax.axis_size("lon")
    length = col_count * count
    polar_count = POLAR
    band = lax.axis_index("lat")
    at_north_end = band == 0
    at_south_end = band == lax.axis_size("lat") - 1
    top_rows = field[:polar_count]
    bottom_rows = field[row_count - polar_count :]
    end_rows = jnp.where(at_north_end, top_rows, bottom_rows)
    end_keep = jnp.where(
        at_north_end, filter_keep[:polar_count], filter_keep[row_count - polar_count :]
    )
    table = wave_table(length, length).reshape(count, col_count, 2 * KMAX)
    blocks = jnp.einsum(
        "sjk,rR->srjRk", table, jnp.eye(polar_count, dtype=jnp.float32)
    ).reshape(count, polar_count * col_count, polar_count * 2 * KMAX)
    weights = wave_weights(end_keep, length).reshape(1, polar_count * 2 * KMAX)
    lowpass = polar_lowpass(end_rows, weights, blocks, call_id)
    smoothed = jnp.where((end_keep <= KMAX)[:, None, None], lowpass, end_rows)
    new_top = jnp.where(at_north_end, smoothed, top_rows)
    new_bottom = jnp.where(at_south_end, smoothed, bottom_rows)
    return jnp.concatenate(
        [new_top, field[polar_count : row_count - polar_count], new_bottom], axis=0
    )


def chem_kernel(x_ref, seed_ref, cot_ref, sat_ref, spread_ref, group_ref, p_ref, g_ref):
    hi = lax.Precision.HIGHEST
    x = x_ref[0]
    seed = seed_ref[0]
    cot = cot_ref[0]
    sat = sat_ref[...]
    spread_m = spread_ref[...].astype(jnp.bfloat16)
    group_m = group_ref[...].astype(jnp.bfloat16)

    plain = (((1,), (0,)), ((), ()))

    def up(v):
        return select_dot(v, spread_m, plain)

    def down(v):
        return select_dot(v, group_m, plain)

    root = jnp.sqrt(x * x + 1.0)
    mass = 0.5 * (x + root)
    aerosol = seed
    history = []
    for newton_step in range(NEWTON):
        denominator = up(aerosol) + sat
        fraction = mass / denominator
        first_sum = down(fraction)
        second_sum = down(fraction / denominator)
        residue = 1.0 - seed / aerosol - first_sum
        derivative = seed / (aerosol * aerosol) + second_sum
        history.append((aerosol, residue, derivative))
        aerosol = aerosol - residue / derivative
    aerosol_q = up(aerosol)
    final_den = aerosol_q + sat
    p_ref[0] = mass * aerosol_q / final_den
    mass_bar = cot * aerosol_q / final_den
    aerosol_bar = down(cot * mass * sat / (final_den * final_den))
    for newton_step in reversed(range(NEWTON)):
        a_n, residue, derivative = history[newton_step]
        inverse = 1.0 / (up(a_n) + sat)
        third_sum = down(mass * inverse * inverse * inverse)
        slope = -2.0 * (seed / (a_n * a_n * a_n) + third_sum)
        over_g = aerosol_bar / derivative
        over_g2 = over_g * residue / derivative
        mass_bar = mass_bar + up(over_g) * inverse + up(over_g2) * inverse * inverse
        aerosol_bar = over_g2 * slope
    g_ref[0] = mass_bar * 0.5 * (1.0 + x / root)


def chemistry_step(filtered, seed_aerosol, volatility, cotangent):
    rows, cols, channels = filtered.shape
    levels = seed_aerosol.shape[-1]
    species = volatility.shape[0]
    group_m = level_table(levels, species)
    spread_m = group_m.T
    sat = jnp.tile(volatility, levels)[None, :]
    big = pl.BlockSpec((1, cols, channels), lambda i: (i, 0, 0))
    small = pl.BlockSpec((1, cols, levels), lambda i: (i, 0, 0))
    return pl.pallas_call(
        chem_kernel,
        grid=(rows,),
        in_specs=[
            big,
            small,
            big,
            pl.BlockSpec((1, channels), lambda i: (0, 0)),
            pl.BlockSpec((levels, channels), lambda i: (0, 0)),
            pl.BlockSpec((channels, levels), lambda i: (0, 0)),
        ],
        out_specs=[big, big],
        out_shape=[
            jax.ShapeDtypeStruct(filtered.shape, jnp.float32),
            jax.ShapeDtypeStruct(filtered.shape, jnp.float32),
        ],
    )(filtered, seed_aerosol, cotangent, sat, spread_m, group_m)


def local(
    tracer,
    east_courant,
    north_courant,
    east_limiter,
    north_limiter,
    filter_keep,
    seed_aerosol,
    volatility,
    cotangent,
):
    row_count = tracer.shape[0]
    channels = tracer.shape[2]
    levels = east_courant.shape[2]
    species = volatility.shape[0]
    first_row = lax.axis_index("lat") * row_count
    packed = jnp.concatenate([tracer, east_courant, east_limiter.astype(jnp.float32)], axis=2)
    widened = east_west(packed)
    east_speed = widened[:, :, channels : channels + levels]
    east_choice = widened[:, :, channels + levels :].astype(jnp.int32)

    def zonal_only(window):
        return zonal_window(window, east_speed, east_choice, species)

    after_east, east_back = jax.vjp(zonal_only, widened[:, :, :channels])
    stacked = jnp.concatenate(
        [after_east, north_courant, north_limiter.astype(jnp.float32)], axis=2
    )
    tall_window = north_south(stacked)
    north_speed = tall_window[:, :, channels : channels + levels]
    north_choice = tall_window[:, :, channels + levels :].astype(jnp.int32)

    def meridional_only(window):
        return meridional_window(window, north_speed, north_choice, first_row, species)

    after_north, north_back = jax.vjp(meridional_only, tall_window[:, :, :channels])
    filtered = filter_field(after_north, filter_keep, 0)

    particle, chem_grad = chemistry_step(filtered, seed_aerosol, volatility, cotangent)
    adjoint_filtered = filter_field(chem_grad, filter_keep, 1)
    return (particle, fold_columns(east_back(fold_rows(north_back(adjoint_filtered)[0]))[0]))


def solution(mesh):
    in_specs = (
        P("lat", "lon", None),
        P("lat", "lon", None),
        P("lat", "lon", None),
        P("lat", "lon", None),
        P("lat", "lon", None),
        P("lat"),
        P("lat", "lon", None),
        P(),
        P("lat", "lon", None),
    )
    out_specs = (P("lat", "lon", None), P("lat", "lon", None))
    return jax.shard_map(local, mesh=mesh, in_specs=in_specs, out_specs=out_specs, check_vma=False)
```

```python
import math

import jax
import jax.numpy as jnp
from jax import lax
from jax.sharding import PartitionSpec as P
from jax.experimental import pallas as pl
from jax.experimental.pallas import tpu as pltpu

NEWTON = 4
KMAX = 32
POLAR = 2


def with_halo(cells, sides, width, closed):
    for axis, dim in sides:
        count = lax.axis_size(axis)
        ends = count if closed else count - 1
        head = lax.slice_in_dim(cells, 0, width, axis=dim)
        tail = lax.slice_in_dim(cells, cells.shape[dim] - width, cells.shape[dim], axis=dim)
        cells = jnp.concatenate(
            [
                lax.ppermute(tail, axis, [(i, (i + 1) % count) for i in range(ends)]),
                cells,
                lax.ppermute(head, axis, [((i + 1) % count, i) for i in range(ends)]),
            ],
            axis=dim,
        )
    return cells


def spread(values, copies):
    return jnp.repeat(values, copies, axis=-1)


def face_weights(courant, limiter):
    upwind = courant >= 0.0
    half = 0.5 * courant
    inner = courant * (7.0 / 12.0)
    outer = jnp.where(limiter == 0, courant * (-1.0 / 12.0), 0.0)
    near_left = jnp.where(
        limiter == 0, inner, jnp.where(limiter == 1, jnp.where(upwind, courant, 0.0), half)
    )
    near_right = jnp.where(
        limiter == 0, inner, jnp.where(limiter == 1, jnp.where(upwind, 0.0, courant), half)
    )
    return jnp.stack([outer, near_left, near_right], axis=0)


def spread_weights(weights, species):
    levels = weights.shape[-1]
    spread_m = level_table(levels, species).T
    return jnp.einsum("...l,lq->...q", weights, spread_m, precision=lax.Precision.HIGHEST)


def zonal_window(window, courant, limiter, species):
    inner_count = window.shape[1] - 4
    weights = spread_weights(
        face_weights(courant[:, 2 : inner_count + 3], limiter[:, 2 : inner_count + 3]), species
    )
    fluxes = (
        weights[0] * (window[:, 0 : inner_count + 1] + window[:, 3 : inner_count + 4])
        + weights[1] * window[:, 1 : inner_count + 2]
        + weights[2] * window[:, 2 : inner_count + 3]
    )
    return window[:, 2 : inner_count + 2] - (fluxes[:, 1:] - fluxes[:, :-1])


def meridional_window(window, courant, limiter, first_row, species):
    inner_count = window.shape[0] - 4
    face_rows = first_row + jnp.arange(inner_count + 1, dtype=jnp.int32)
    opened = jnp.where(face_rows[:, None, None] > 0, courant[2 : inner_count + 3], 0.0)
    weights = spread_weights(face_weights(opened, limiter[2 : inner_count + 3]), species)
    fluxes = (
        weights[0] * (window[0 : inner_count + 1] + window[3 : inner_count + 4])
        + weights[1] * window[1 : inner_count + 2]
        + weights[2] * window[2 : inner_count + 3]
    )
    return window[2 : inner_count + 2] - (fluxes[1:] - fluxes[:-1])


def positive(field):
    return 0.5 * (field + jnp.sqrt(field * field + 1.0))


def level_table(levels, species):
    channel_level = jnp.arange(levels * species, dtype=jnp.int32) // species
    return (channel_level[:, None] == jnp.arange(levels, dtype=jnp.int32)[None, :]).astype(
        jnp.float32
    )


def partition(total_mass, seed_aerosol, volatility):
    levels = seed_aerosol.shape[-1]
    species = volatility.shape[0]
    grouping = level_table(levels, species)
    saturation = jnp.tile(volatility, levels)
    aerosol = seed_aerosol
    for newton_step in range(NEWTON):
        denominator = spread(aerosol, species) + saturation
        fraction = total_mass / denominator
        first_sum = jnp.dot(fraction, grouping, precision=lax.Precision.HIGHEST)
        second_sum = jnp.dot(fraction / denominator, grouping, precision=lax.Precision.HIGHEST)
        residue = 1.0 - seed_aerosol / aerosol - first_sum
        derivative = seed_aerosol / (aerosol * aerosol) + second_sum
        aerosol = aerosol - residue / derivative
    aerosol_q = spread(aerosol, species)
    return total_mass * aerosol_q / (aerosol_q + saturation)


def east_west(field):
    return with_halo(field, (("lon", 1),), 2, True)


def north_south(field):
    return with_halo(field, (("lat", 0),), 2, False)


def fold_rows(gradient):
    inner_rows = gradient.shape[0] - 4
    rim_cells = jnp.concatenate([gradient[:2], gradient[inner_rows + 2 :]], axis=0)
    arrived = north_south(rim_cells)
    middle = gradient[2 : inner_rows + 2]
    return jnp.concatenate(
        [
            middle[:2] + arrived[:2],
            middle[2 : inner_rows - 2],
            middle[inner_rows - 2 :] + arrived[6:],
        ],
        axis=0,
    )


def fold_columns(gradient):
    inner_cols = gradient.shape[1] - 4
    rim_cells = jnp.concatenate([gradient[:, :2], gradient[:, inner_cols + 2 :]], axis=1)
    arrived = east_west(rim_cells)
    middle = gradient[:, 2 : inner_cols + 2]
    return jnp.concatenate(
        [
            middle[:, :2] + arrived[:, :2],
            middle[:, 2 : inner_cols - 2],
            middle[:, inner_cols - 2 :] + arrived[:, 6:],
        ],
        axis=1,
    )


def wave_table(column_count, length):
    position = jnp.arange(column_count, dtype=jnp.int32)
    numbers = jnp.arange(KMAX, dtype=jnp.int32)
    phases = position[:, None] * numbers[None, :] % length
    angles = phases.astype(jnp.float32) * (2.0 * math.pi / length)
    return jnp.concatenate([jnp.cos(angles), jnp.sin(angles)], axis=1)


def wave_weights(keep_values, length):
    numbers = jnp.arange(2 * KMAX, dtype=jnp.int32) % KMAX
    scaling = jnp.where(numbers == 0, 1.0, 2.0) / length
    kept_mask = numbers[None, :] < keep_values[:, None]
    return jnp.where(kept_mask, scaling[None, :], 0.0)


def lowpass_circles(circles, keep_values):
    length = circles.shape[2]
    table_full = wave_table(length, length)
    coefficient = jnp.einsum("rqn,nk->rqk", circles, table_full, precision=lax.Precision.HIGHEST)
    coefficient = coefficient * wave_weights(keep_values, length)[:, None, :]
    lowpass = jnp.einsum("rqk,nk->rqn", coefficient, table_full, precision=lax.Precision.HIGHEST)
    return jnp.where((keep_values <= KMAX)[:, None, None], lowpass, circles)


def split_three(values):
    high = values.astype(jnp.bfloat16)
    rest = values - high.astype(jnp.float32)
    middle = rest.astype(jnp.bfloat16)
    low = (rest - middle.astype(jnp.float32)).astype(jnp.bfloat16)
    return high, middle, low


def select_dot(values, selector, dims):
    total = None
    for piece in split_three(values):
        term = lax.dot_general(piece, selector, dims, preferred_element_type=jnp.float32)
        total = term if total is None else total + term
    return total


def select_dot_left(selector, values, dims):
    total = None
    for piece in split_three(values):
        term = lax.dot_general(selector, piece, dims, preferred_element_type=jnp.float32)
        total = term if total is None else total + term
    return total


def polar_kernel(x_ref, w_ref, t_ref, y_ref, out_go, land_go, out_back, land_back,
                 sem_a, sem_b, sem_c, sem_d):
    count = t_ref.shape[0]
    polar_count, col_count, channels = x_ref.shape
    chunk = channels // count
    padded = out_go.shape[1]
    me = lax.axis_index("lon")
    band = lax.axis_index("lat")
    bands = lax.axis_size("lat")
    active = jnp.logical_or(band == 0, band == bands - 1)
    hi = lax.Precision.HIGHEST
    mesh_id = pl.DeviceIdType.MESH

    def remote(src, dst, send_sem, recv_sem, peer):
        return pltpu.make_async_remote_copy(
            src_ref=src, dst_ref=dst, send_sem=send_sem, recv_sem=recv_sem,
            device_id=(band, peer), device_id_type=mesh_id,
        )

    def round_trip(outbox, inbox, send_sems, recv_sems):
        for offset in range(1, count):
            peer = lax.rem(me + offset, count)
            remote(outbox.at[peer], inbox.at[me], send_sems.at[offset], recv_sems.at[me], peer).start()
        inbox[pl.ds(me, 1)] = outbox[pl.ds(me, 1)]
        for offset in range(1, count):
            peer = lax.rem(me + offset, count)
            remote(outbox.at[peer], inbox.at[me], send_sems.at[offset], recv_sems.at[me], peer).wait_send()
        for offset in range(1, count):
            peer = lax.rem(me + count - offset, count)
            remote(outbox.at[peer], inbox.at[peer], send_sems.at[offset], recv_sems.at[peer], peer).wait_recv()

    @pl.when(active)
    def _():
        barrier = pltpu.get_barrier_semaphore()
        for offset in range(1, count):
            peer = lax.rem(me + offset, count)
            pl.semaphore_signal(barrier, 1, device_id=(band, peer), device_id_type=mesh_id)
        pl.semaphore_wait(barrier, count - 1)
        rows = jnp.concatenate([x_ref[r] for r in range(polar_count)], axis=0)
        slot = lax.broadcasted_iota(jnp.int32, (count * padded, channels), 0)
        channel = lax.broadcasted_iota(jnp.int32, (count * padded, channels), 1)
        target = (channel // chunk) * padded + channel % chunk
        packer = jnp.where(slot == target, 1.0, 0.0).astype(jnp.bfloat16)
        packed = select_dot_left(packer, rows, (((1,), (1,)), ((), ())))
        out_go[...] = packed.reshape(count, padded, polar_count * col_count)
        round_trip(out_go, land_go, sem_a, sem_b)

        def analyse(s, acc):
            return acc + jnp.dot(land_go[s], t_ref[s], precision=hi,
                                 preferred_element_type=jnp.float32)

        coefficient = lax.fori_loop(
            0, count, analyse, jnp.zeros((padded, t_ref.shape[2]), jnp.float32)
        )
        coefficient = coefficient * w_ref[...]

        def synthesise(s, carry):
            out_back[s] = lax.dot_general(coefficient, t_ref[s], (((1,), (1,)), ((), ())),
                                          precision=hi, preferred_element_type=jnp.float32)
            return carry

        lax.fori_loop(0, count, synthesise, 0)
        round_trip(out_back, land_back, sem_c, sem_d)
        back = land_back[...].reshape(count * padded, polar_count * col_count)
        result = select_dot(back, packer, (((0,), (0,)), ((), ())))
        for r in range(polar_count):
            y_ref[r] = result[r * col_count : (r + 1) * col_count]

    @pl.when(jnp.logical_not(active))
    def _():
        y_ref[...] = x_ref[...]


def polar_lowpass(end_rows, weights, blocks, call_id):
    polar_count, col_count, channels = end_rows.shape
    count = blocks.shape[0]
    padded = -(-(channels // count) // 8) * 8
    slab = (count, padded, polar_count * col_count)
    vmem = pl.BlockSpec(memory_space=pltpu.VMEM)
    return pl.pallas_call(
        polar_kernel,
        out_shape=jax.ShapeDtypeStruct(end_rows.shape, end_rows.dtype),
        in_specs=[vmem, vmem, vmem],
        out_specs=vmem,
        scratch_shapes=[
            pltpu.VMEM(slab, jnp.float32),
            pltpu.VMEM(slab, jnp.float32),
            pltpu.VMEM(slab, jnp.float32),
            pltpu.VMEM(slab, jnp.float32),
            pltpu.SemaphoreType.DMA((count,)),
            pltpu.SemaphoreType.DMA((count,)),
            pltpu.SemaphoreType.DMA((count,)),
            pltpu.SemaphoreType.DMA((count,)),
        ],
        compiler_params=pltpu.CompilerParams(collective_id=call_id, has_side_effects=True),
    )(end_rows, weights, blocks)


def column_chemistry(x, seed, cot, sat, valid):
    root = jnp.sqrt(x * x + 1.0)
    mass = jnp.where(valid, 0.5 * (x + root), 0.0)
    cot = jnp.where(valid, cot, 0.0)
    aerosol = seed
    history = []
    for newton_step in range(NEWTON):
        denominator = aerosol + sat
        fraction = mass / denominator
        first_sum = jnp.sum(fraction, axis=0, keepdims=True)
        second_sum = jnp.sum(fraction / denominator, axis=0, keepdims=True)
        residue = 1.0 - seed / aerosol - first_sum
        derivative = seed / (aerosol * aerosol) + second_sum
        history.append((aerosol, residue, derivative))
        aerosol = aerosol - residue / derivative
    final_den = aerosol + sat
    particle = mass * aerosol / final_den
    mass_bar = cot * aerosol / final_den
    aerosol_bar = jnp.sum(cot * mass * sat / (final_den * final_den), axis=0, keepdims=True)
    for newton_step in reversed(range(NEWTON)):
        a_n, residue, derivative = history[newton_step]
        inverse = 1.0 / (a_n + sat)
        third_sum = jnp.sum(mass * inverse * inverse * inverse, axis=0, keepdims=True)
        slope = -2.0 * (seed / (a_n * a_n * a_n) + third_sum)
        over_g = aerosol_bar / derivative
        over_g2 = over_g * residue / derivative
        mass_bar = mass_bar + over_g * inverse + over_g2 * inverse * inverse
        aerosol_bar = over_g2 * slope
    gradient = mass_bar * 0.5 * (1.0 + x / root)
    return jnp.where(valid, particle, 0.0), jnp.where(valid, gradient, 0.0)


def owner_kernel(x_ref, c_ref, s_ref, w_ref, m_ref, v_ref, t_ref, p_ref, g_ref,
                 out_go, land_go, out_back, land_back, field_s, sem_a, sem_b, sem_c, sem_d):
    count = t_ref.shape[0]
    polar_count, col_count, channels = x_ref.shape
    levels = s_ref.shape[2]
    chunk = channels // count
    padded = out_go.shape[1] // 2
    me = lax.axis_index("lon")
    band = lax.axis_index("lat")
    bands = lax.axis_size("lat")
    active = jnp.logical_or(band == 0, band == bands - 1)
    hi = lax.Precision.HIGHEST
    mesh_id = pl.DeviceIdType.MESH
    nt = (((1,), (1,)), ((), ()))

    def remote(src, dst, send_sem, recv_sem, peer):
        return pltpu.make_async_remote_copy(
            src_ref=src, dst_ref=dst, send_sem=send_sem, recv_sem=recv_sem,
            device_id=(band, peer), device_id_type=mesh_id,
        )

    def round_trip(outbox, inbox, send_sems, recv_sems):
        for offset in range(1, count):
            peer = lax.rem(me + offset, count)
            remote(outbox.at[peer], inbox.at[me], send_sems.at[offset], recv_sems.at[me], peer).start()
        inbox[pl.ds(me, 1)] = outbox[pl.ds(me, 1)]
        for offset in range(1, count):
            peer = lax.rem(me + offset, count)
            remote(outbox.at[peer], inbox.at[me], send_sems.at[offset], recv_sems.at[me], peer).wait_send()
        for offset in range(1, count):
            peer = lax.rem(me + count - offset, count)
            remote(outbox.at[peer], inbox.at[peer], send_sems.at[offset], recv_sems.at[peer], peer).wait_recv()

    @pl.when(active)
    def _():
        barrier = pltpu.get_barrier_semaphore()
        for offset in range(1, count):
            peer = lax.rem(me + offset, count)
            pl.semaphore_signal(barrier, 1, device_id=(band, peer), device_id_type=mesh_id)
        pl.semaphore_wait(barrier, count - 1)
        wide = channels + levels
        slot = lax.broadcasted_iota(jnp.int32, (count * padded, wide), 0)
        channel = lax.broadcasted_iota(jnp.int32, (count * padded, wide), 1)
        target = jnp.where(
            channel < channels,
            (channel // chunk) * padded + channel % chunk,
            (channel - channels) * padded + chunk,
        )
        packer_wide = jnp.where(slot == target, 1.0, 0.0).astype(jnp.bfloat16)
        packer = packer_wide[:, :channels]
        rows = jnp.concatenate(
            [jnp.concatenate([x_ref[r], s_ref[r]], axis=1) for r in range(polar_count)], axis=0
        )
        cots = jnp.concatenate([c_ref[r] for r in range(polar_count)], axis=0)
        lanes = polar_count * col_count
        out_go[:, 0:padded, :] = select_dot_left(packer_wide, rows, nt).reshape(count, padded, lanes)
        out_go[:, padded:, :] = select_dot_left(packer, cots, nt).reshape(count, padded, lanes)
        round_trip(out_go, land_go, sem_a, sem_b)

        def analyse(s, acc):
            return acc + jnp.dot(land_go[s, 0:padded, :], t_ref[s], precision=hi,
                                 preferred_element_type=jnp.float32)

        zero = jnp.zeros((padded, t_ref.shape[2]), jnp.float32)
        coefficient = lax.fori_loop(0, count, analyse, zero) * w_ref[...]
        keep_lane = m_ref[...] > 0.5
        species_row = lax.broadcasted_iota(jnp.int32, (padded, lanes), 0)
        valid = species_row < chunk
        sat = v_ref[...]

        def chemistry(s, acc):
            values = land_go[s, 0:padded, :]
            smooth = lax.dot_general(coefficient, t_ref[s], nt, precision=hi,
                                     preferred_element_type=jnp.float32)
            smooth = jnp.where(keep_lane, smooth, values)
            seed = land_go[s, pl.ds(chunk, 1), :]
            particle, gradient = column_chemistry(
                smooth, seed, land_go[s, padded:, :], sat, valid
            )
            out_back[s, 0:padded, :] = particle
            field_s[s] = gradient
            return acc + jnp.dot(gradient, t_ref[s], precision=hi,
                                 preferred_element_type=jnp.float32)

        adjoint_coef = lax.fori_loop(0, count, chemistry, zero) * w_ref[...]

        def synthesise(s, carry):
            smooth = lax.dot_general(adjoint_coef, t_ref[s], nt, precision=hi,
                                     preferred_element_type=jnp.float32)
            out_back[s, padded:, :] = jnp.where(keep_lane, smooth, field_s[s])
            return carry

        lax.fori_loop(0, count, synthesise, 0)
        round_trip(out_back, land_back, sem_c, sem_d)
        particle_back = land_back[:, 0:padded, :].reshape(count * padded, lanes)
        gradient_back = land_back[:, padded:, :].reshape(count * padded, lanes)
        particle_rows = select_dot(particle_back, packer, (((0,), (0,)), ((), ())))
        gradient_rows = select_dot(gradient_back, packer, (((0,), (0,)), ((), ())))
        for r in range(polar_count):
            p_ref[r] = particle_rows[r * col_count : (r + 1) * col_count]
            g_ref[r] = gradient_rows[r * col_count : (r + 1) * col_count]

    @pl.when(jnp.logical_not(active))
    def _():
        p_ref[...] = jnp.zeros_like(p_ref)
        g_ref[...] = jnp.zeros_like(g_ref)


def polar_step(field, seed_aerosol, volatility, cotangent, filter_keep, particle, gradient):
    row_count, col_count, channels = field.shape
    count = lax.axis_size("lon")
    length = col_count * count
    species = volatility.shape[0]
    polar_count = POLAR
    band = lax.axis_index("lat")
    at_north_end = band == 0
    at_south_end = band == lax.axis_size("lat") - 1

    def ends(values):
        return jnp.where(at_north_end, values[:polar_count], values[row_count - polar_count :])

    end_keep = ends(filter_keep)
    table = wave_table(length, length).reshape(count, col_count, 2 * KMAX)
    blocks = jnp.einsum(
        "sjk,rR->srjRk", table, jnp.eye(polar_count, dtype=jnp.float32)
    ).reshape(count, polar_count * col_count, polar_count * 2 * KMAX)
    weights = wave_weights(end_keep, length).reshape(1, polar_count * 2 * KMAX)
    lane_mask = jnp.repeat((end_keep <= KMAX).astype(jnp.float32), col_count)[None, :]
    padded = -(-(channels // count + 1) // 8) * 8
    sat = jnp.concatenate(
        [volatility, jnp.ones((padded - species,), jnp.float32)]
    )[:, None]
    slab = (count, 2 * padded, polar_count * col_count)
    vmem = pl.BlockSpec(memory_space=pltpu.VMEM)
    end_shape = jax.ShapeDtypeStruct((polar_count, col_count, channels), jnp.float32)
    polar_particle, polar_gradient = pl.pallas_call(
        owner_kernel,
        out_shape=[end_shape, end_shape],
        in_specs=[vmem] * 7,
        out_specs=[vmem, vmem],
        scratch_shapes=[
            pltpu.VMEM(slab, jnp.float32),
            pltpu.VMEM(slab, jnp.float32),
            pltpu.VMEM(slab, jnp.float32),
            pltpu.VMEM(slab, jnp.float32),
            pltpu.VMEM((count, padded, polar_count * col_count), jnp.float32),
            pltpu.SemaphoreType.DMA((count,)),
            pltpu.SemaphoreType.DMA((count,)),
            pltpu.SemaphoreType.DMA((count,)),
            pltpu.SemaphoreType.DMA((count,)),
        ],
        compiler_params=pltpu.CompilerParams(collective_id=0, has_side_effects=True),
    )(ends(field), ends(cotangent), ends(seed_aerosol), weights, lane_mask, sat, blocks)

    def merge(values, polar):
        top = jnp.where(at_north_end, polar, values[:polar_count])
        bottom = jnp.where(at_south_end, polar, values[row_count - polar_count :])
        return jnp.concatenate(
            [top, values[polar_count : row_count - polar_count], bottom], axis=0
        )

    return merge(particle, polar_particle), merge(gradient, polar_gradient)


def filter_field(field, filter_keep, call_id):
    row_count, col_count, channels = field.shape
    count = lax.axis_size("lon")
    length = col_count * count
    polar_count = POLAR
    band = lax.axis_index("lat")
    at_north_end = band == 0
    at_south_end = band == lax.axis_size("lat") - 1
    top_rows = field[:polar_count]
    bottom_rows = field[row_count - polar_count :]
    end_rows = jnp.where(at_north_end, top_rows, bottom_rows)
    end_keep = jnp.where(
        at_north_end, filter_keep[:polar_count], filter_keep[row_count - polar_count :]
    )
    table = wave_table(length, length).reshape(count, col_count, 2 * KMAX)
    blocks = jnp.einsum(
        "sjk,rR->srjRk", table, jnp.eye(polar_count, dtype=jnp.float32)
    ).reshape(count, polar_count * col_count, polar_count * 2 * KMAX)
    weights = wave_weights(end_keep, length).reshape(1, polar_count * 2 * KMAX)
    lowpass = polar_lowpass(end_rows, weights, blocks, call_id)
    smoothed = jnp.where((end_keep <= KMAX)[:, None, None], lowpass, end_rows)
    new_top = jnp.where(at_north_end, smoothed, top_rows)
    new_bottom = jnp.where(at_south_end, smoothed, bottom_rows)
    return jnp.concatenate(
        [new_top, field[polar_count : row_count - polar_count], new_bottom], axis=0
    )


def chem_kernel(x_ref, seed_ref, cot_ref, sat_ref, spread_ref, group_ref, p_ref, g_ref):
    hi = lax.Precision.HIGHEST
    x = x_ref[0]
    seed = seed_ref[0]
    cot = cot_ref[0]
    sat = sat_ref[...]
    spread_m = spread_ref[...].astype(jnp.bfloat16)
    group_m = group_ref[...].astype(jnp.bfloat16)

    plain = (((1,), (0,)), ((), ()))

    def up(v):
        return select_dot(v, spread_m, plain)

    def down(v):
        return select_dot(v, group_m, plain)

    root = jnp.sqrt(x * x + 1.0)
    mass = 0.5 * (x + root)
    aerosol = seed
    history = []
    for newton_step in range(NEWTON):
        denominator = up(aerosol) + sat
        fraction = mass / denominator
        first_sum = down(fraction)
        second_sum = down(fraction / denominator)
        residue = 1.0 - seed / aerosol - first_sum
        derivative = seed / (aerosol * aerosol) + second_sum
        history.append((aerosol, residue, derivative))
        aerosol = aerosol - residue / derivative
    aerosol_q = up(aerosol)
    final_den = aerosol_q + sat
    p_ref[0] = mass * aerosol_q / final_den
    mass_bar = cot * aerosol_q / final_den
    aerosol_bar = down(cot * mass * sat / (final_den * final_den))
    for newton_step in reversed(range(NEWTON)):
        a_n, residue, derivative = history[newton_step]
        inverse = 1.0 / (up(a_n) + sat)
        third_sum = down(mass * inverse * inverse * inverse)
        slope = -2.0 * (seed / (a_n * a_n * a_n) + third_sum)
        over_g = aerosol_bar / derivative
        over_g2 = over_g * residue / derivative
        mass_bar = mass_bar + up(over_g) * inverse + up(over_g2) * inverse * inverse
        aerosol_bar = over_g2 * slope
    g_ref[0] = mass_bar * 0.5 * (1.0 + x / root)


def chemistry_step(filtered, seed_aerosol, volatility, cotangent):
    rows, cols, channels = filtered.shape
    levels = seed_aerosol.shape[-1]
    species = volatility.shape[0]
    group_m = level_table(levels, species)
    spread_m = group_m.T
    sat = jnp.tile(volatility, levels)[None, :]
    big = pl.BlockSpec((1, cols, channels), lambda i: (i, 0, 0))
    small = pl.BlockSpec((1, cols, levels), lambda i: (i, 0, 0))
    return pl.pallas_call(
        chem_kernel,
        grid=(rows,),
        in_specs=[
            big,
            small,
            big,
            pl.BlockSpec((1, channels), lambda i: (0, 0)),
            pl.BlockSpec((levels, channels), lambda i: (0, 0)),
            pl.BlockSpec((channels, levels), lambda i: (0, 0)),
        ],
        out_specs=[big, big],
        out_shape=[
            jax.ShapeDtypeStruct(filtered.shape, jnp.float32),
            jax.ShapeDtypeStruct(filtered.shape, jnp.float32),
        ],
    )(filtered, seed_aerosol, cotangent, sat, spread_m, group_m)


def local(
    tracer,
    east_courant,
    north_courant,
    east_limiter,
    north_limiter,
    filter_keep,
    seed_aerosol,
    volatility,
    cotangent,
):
    row_count = tracer.shape[0]
    channels = tracer.shape[2]
    levels = east_courant.shape[2]
    species = volatility.shape[0]
    first_row = lax.axis_index("lat") * row_count
    packed = jnp.concatenate([tracer, east_courant, east_limiter.astype(jnp.float32)], axis=2)
    widened = east_west(packed)
    east_speed = widened[:, :, channels : channels + levels]
    east_choice = widened[:, :, channels + levels :].astype(jnp.int32)

    def zonal_only(window):
        return zonal_window(window, east_speed, east_choice, species)

    after_east, east_back = jax.vjp(zonal_only, widened[:, :, :channels])
    stacked = jnp.concatenate(
        [after_east, north_courant, north_limiter.astype(jnp.float32)], axis=2
    )
    tall_window = north_south(stacked)
    north_speed = tall_window[:, :, channels : channels + levels]
    north_choice = tall_window[:, :, channels + levels :].astype(jnp.int32)

    def meridional_only(window):
        return meridional_window(window, north_speed, north_choice, first_row, species)

    after_north, north_back = jax.vjp(meridional_only, tall_window[:, :, :channels])
    particle, chem_grad = chemistry_step(after_north, seed_aerosol, volatility, cotangent)
    particle, adjoint_filtered = polar_step(
        after_north, seed_aerosol, volatility, cotangent, filter_keep, particle, chem_grad
    )
    return (particle, fold_columns(east_back(fold_rows(north_back(adjoint_filtered)[0]))[0]))


def solution(mesh):
    in_specs = (
        P("lat", "lon", None),
        P("lat", "lon", None),
        P("lat", "lon", None),
        P("lat", "lon", None),
        P("lat", "lon", None),
        P("lat"),
        P("lat", "lon", None),
        P(),
        P("lat", "lon", None),
    )
    out_specs = (P("lat", "lon", None), P("lat", "lon", None))
    return jax.shard_map(local, mesh=mesh, in_specs=in_specs, out_specs=out_specs, check_vma=False)
```

```python
import math

import jax
import jax.numpy as jnp
from jax import lax
from jax.sharding import PartitionSpec as P
from jax.experimental import pallas as pl
from jax.experimental.pallas import tpu as pltpu

NEWTON = 4
KMAX = 32
POLAR = 2


def with_halo(cells, sides, width, closed):
    for axis, dim in sides:
        count = lax.axis_size(axis)
        ends = count if closed else count - 1
        head = lax.slice_in_dim(cells, 0, width, axis=dim)
        tail = lax.slice_in_dim(cells, cells.shape[dim] - width, cells.shape[dim], axis=dim)
        cells = jnp.concatenate(
            [
                lax.ppermute(tail, axis, [(i, (i + 1) % count) for i in range(ends)]),
                cells,
                lax.ppermute(head, axis, [((i + 1) % count, i) for i in range(ends)]),
            ],
            axis=dim,
        )
    return cells


def spread(values, copies):
    return jnp.repeat(values, copies, axis=-1)


def face_weights(courant, limiter):
    upwind = courant >= 0.0
    half = 0.5 * courant
    inner = courant * (7.0 / 12.0)
    outer = jnp.where(limiter == 0, courant * (-1.0 / 12.0), 0.0)
    near_left = jnp.where(
        limiter == 0, inner, jnp.where(limiter == 1, jnp.where(upwind, courant, 0.0), half)
    )
    near_right = jnp.where(
        limiter == 0, inner, jnp.where(limiter == 1, jnp.where(upwind, 0.0, courant), half)
    )
    return jnp.stack([outer, near_left, near_right], axis=0)


def spread_weights(weights, species):
    levels = weights.shape[-1]
    spread_m = level_table(levels, species).T
    return jnp.einsum("...l,lq->...q", weights, spread_m, precision=lax.Precision.HIGHEST)


def zonal_window(window, courant, limiter, species):
    inner_count = window.shape[1] - 4
    weights = spread_weights(
        face_weights(courant[:, 2 : inner_count + 3], limiter[:, 2 : inner_count + 3]), species
    )
    fluxes = (
        weights[0] * (window[:, 0 : inner_count + 1] + window[:, 3 : inner_count + 4])
        + weights[1] * window[:, 1 : inner_count + 2]
        + weights[2] * window[:, 2 : inner_count + 3]
    )
    return window[:, 2 : inner_count + 2] - (fluxes[:, 1:] - fluxes[:, :-1])


def meridional_window(window, courant, limiter, first_row, species):
    inner_count = window.shape[0] - 4
    face_rows = first_row + jnp.arange(inner_count + 1, dtype=jnp.int32)
    opened = jnp.where(face_rows[:, None, None] > 0, courant[2 : inner_count + 3], 0.0)
    weights = spread_weights(face_weights(opened, limiter[2 : inner_count + 3]), species)
    fluxes = (
        weights[0] * (window[0 : inner_count + 1] + window[3 : inner_count + 4])
        + weights[1] * window[1 : inner_count + 2]
        + weights[2] * window[2 : inner_count + 3]
    )
    return window[2 : inner_count + 2] - (fluxes[1:] - fluxes[:-1])


def positive(field):
    return 0.5 * (field + jnp.sqrt(field * field + 1.0))


def level_table(levels, species):
    channel_level = jnp.arange(levels * species, dtype=jnp.int32) // species
    return (channel_level[:, None] == jnp.arange(levels, dtype=jnp.int32)[None, :]).astype(
        jnp.float32
    )


def partition(total_mass, seed_aerosol, volatility):
    levels = seed_aerosol.shape[-1]
    species = volatility.shape[0]
    grouping = level_table(levels, species)
    saturation = jnp.tile(volatility, levels)
    aerosol = seed_aerosol
    for newton_step in range(NEWTON):
        denominator = spread(aerosol, species) + saturation
        fraction = total_mass / denominator
        first_sum = jnp.dot(fraction, grouping, precision=lax.Precision.HIGHEST)
        second_sum = jnp.dot(fraction / denominator, grouping, precision=lax.Precision.HIGHEST)
        residue = 1.0 - seed_aerosol / aerosol - first_sum
        derivative = seed_aerosol / (aerosol * aerosol) + second_sum
        aerosol = aerosol - residue / derivative
    aerosol_q = spread(aerosol, species)
    return total_mass * aerosol_q / (aerosol_q + saturation)


def east_west(field):
    return with_halo(field, (("lon", 1),), 2, True)


def north_south(field):
    return with_halo(field, (("lat", 0),), 2, False)


def fold_rows(gradient):
    inner_rows = gradient.shape[0] - 4
    rim_cells = jnp.concatenate([gradient[:2], gradient[inner_rows + 2 :]], axis=0)
    arrived = north_south(rim_cells)
    middle = gradient[2 : inner_rows + 2]
    return jnp.concatenate(
        [
            middle[:2] + arrived[:2],
            middle[2 : inner_rows - 2],
            middle[inner_rows - 2 :] + arrived[6:],
        ],
        axis=0,
    )


def fold_columns(gradient):
    inner_cols = gradient.shape[1] - 4
    rim_cells = jnp.concatenate([gradient[:, :2], gradient[:, inner_cols + 2 :]], axis=1)
    arrived = east_west(rim_cells)
    middle = gradient[:, 2 : inner_cols + 2]
    return jnp.concatenate(
        [
            middle[:, :2] + arrived[:, :2],
            middle[:, 2 : inner_cols - 2],
            middle[:, inner_cols - 2 :] + arrived[:, 6:],
        ],
        axis=1,
    )


def wave_table(column_count, length):
    position = jnp.arange(column_count, dtype=jnp.int32)
    numbers = jnp.arange(KMAX, dtype=jnp.int32)
    phases = position[:, None] * numbers[None, :] % length
    angles = phases.astype(jnp.float32) * (2.0 * math.pi / length)
    return jnp.concatenate([jnp.cos(angles), jnp.sin(angles)], axis=1)


def wave_weights(keep_values, length):
    numbers = jnp.arange(2 * KMAX, dtype=jnp.int32) % KMAX
    scaling = jnp.where(numbers == 0, 1.0, 2.0) / length
    kept_mask = numbers[None, :] < keep_values[:, None]
    return jnp.where(kept_mask, scaling[None, :], 0.0)


def lowpass_circles(circles, keep_values):
    length = circles.shape[2]
    table_full = wave_table(length, length)
    coefficient = jnp.einsum("rqn,nk->rqk", circles, table_full, precision=lax.Precision.HIGHEST)
    coefficient = coefficient * wave_weights(keep_values, length)[:, None, :]
    lowpass = jnp.einsum("rqk,nk->rqn", coefficient, table_full, precision=lax.Precision.HIGHEST)
    return jnp.where((keep_values <= KMAX)[:, None, None], lowpass, circles)


def split_three(values):
    high = values.astype(jnp.bfloat16)
    rest = values - high.astype(jnp.float32)
    middle = rest.astype(jnp.bfloat16)
    low = (rest - middle.astype(jnp.float32)).astype(jnp.bfloat16)
    return high, middle, low


def select_dot(values, selector, dims):
    total = None
    for piece in split_three(values):
        term = lax.dot_general(piece, selector, dims, preferred_element_type=jnp.float32)
        total = term if total is None else total + term
    return total


def select_dot_left(selector, values, dims):
    total = None
    for piece in split_three(values):
        term = lax.dot_general(selector, piece, dims, preferred_element_type=jnp.float32)
        total = term if total is None else total + term
    return total


def polar_kernel(x_ref, w_ref, t_ref, y_ref, out_go, land_go, out_back, land_back,
                 sem_a, sem_b, sem_c, sem_d):
    count = t_ref.shape[0]
    polar_count, col_count, channels = x_ref.shape
    chunk = channels // count
    padded = out_go.shape[1]
    me = lax.axis_index("lon")
    band = lax.axis_index("lat")
    bands = lax.axis_size("lat")
    active = jnp.logical_or(band == 0, band == bands - 1)
    hi = lax.Precision.HIGHEST
    mesh_id = pl.DeviceIdType.MESH

    def remote(src, dst, send_sem, recv_sem, peer):
        return pltpu.make_async_remote_copy(
            src_ref=src, dst_ref=dst, send_sem=send_sem, recv_sem=recv_sem,
            device_id=(band, peer), device_id_type=mesh_id,
        )

    def round_trip(outbox, inbox, send_sems, recv_sems):
        for offset in range(1, count):
            peer = lax.rem(me + offset, count)
            remote(outbox.at[peer], inbox.at[me], send_sems.at[offset], recv_sems.at[me], peer).start()
        inbox[pl.ds(me, 1)] = outbox[pl.ds(me, 1)]
        for offset in range(1, count):
            peer = lax.rem(me + offset, count)
            remote(outbox.at[peer], inbox.at[me], send_sems.at[offset], recv_sems.at[me], peer).wait_send()
        for offset in range(1, count):
            peer = lax.rem(me + count - offset, count)
            remote(outbox.at[peer], inbox.at[peer], send_sems.at[offset], recv_sems.at[peer], peer).wait_recv()

    @pl.when(active)
    def _():
        barrier = pltpu.get_barrier_semaphore()
        for offset in range(1, count):
            peer = lax.rem(me + offset, count)
            pl.semaphore_signal(barrier, 1, device_id=(band, peer), device_id_type=mesh_id)
        pl.semaphore_wait(barrier, count - 1)
        rows = jnp.concatenate([x_ref[r] for r in range(polar_count)], axis=0)
        slot = lax.broadcasted_iota(jnp.int32, (count * padded, channels), 0)
        channel = lax.broadcasted_iota(jnp.int32, (count * padded, channels), 1)
        target = (channel // chunk) * padded + channel % chunk
        packer = jnp.where(slot == target, 1.0, 0.0).astype(jnp.bfloat16)
        packed = select_dot_left(packer, rows, (((1,), (1,)), ((), ())))
        out_go[...] = packed.reshape(count, padded, polar_count * col_count)
        round_trip(out_go, land_go, sem_a, sem_b)

        def analyse(s, acc):
            return acc + jnp.dot(land_go[s], t_ref[s], precision=hi,
                                 preferred_element_type=jnp.float32)

        coefficient = lax.fori_loop(
            0, count, analyse, jnp.zeros((padded, t_ref.shape[2]), jnp.float32)
        )
        coefficient = coefficient * w_ref[...]

        def synthesise(s, carry):
            out_back[s] = lax.dot_general(coefficient, t_ref[s], (((1,), (1,)), ((), ())),
                                          precision=hi, preferred_element_type=jnp.float32)
            return carry

        lax.fori_loop(0, count, synthesise, 0)
        round_trip(out_back, land_back, sem_c, sem_d)
        back = land_back[...].reshape(count * padded, polar_count * col_count)
        result = select_dot(back, packer, (((0,), (0,)), ((), ())))
        for r in range(polar_count):
            y_ref[r] = result[r * col_count : (r + 1) * col_count]

    @pl.when(jnp.logical_not(active))
    def _():
        y_ref[...] = x_ref[...]


def polar_lowpass(end_rows, weights, blocks, call_id):
    polar_count, col_count, channels = end_rows.shape
    count = blocks.shape[0]
    padded = -(-(channels // count) // 8) * 8
    slab = (count, padded, polar_count * col_count)
    vmem = pl.BlockSpec(memory_space=pltpu.VMEM)
    return pl.pallas_call(
        polar_kernel,
        out_shape=jax.ShapeDtypeStruct(end_rows.shape, end_rows.dtype),
        in_specs=[vmem, vmem, vmem],
        out_specs=vmem,
        scratch_shapes=[
            pltpu.VMEM(slab, jnp.float32),
            pltpu.VMEM(slab, jnp.float32),
            pltpu.VMEM(slab, jnp.float32),
            pltpu.VMEM(slab, jnp.float32),
            pltpu.SemaphoreType.DMA((count,)),
            pltpu.SemaphoreType.DMA((count,)),
            pltpu.SemaphoreType.DMA((count,)),
            pltpu.SemaphoreType.DMA((count,)),
        ],
        compiler_params=pltpu.CompilerParams(collective_id=call_id, has_side_effects=True),
    )(end_rows, weights, blocks)


def column_chemistry(x, seed, cot, sat, valid):
    root = jnp.sqrt(x * x + 1.0)
    mass = jnp.where(valid, 0.5 * (x + root), 0.0)
    cot = jnp.where(valid, cot, 0.0)
    aerosol = seed
    history = []
    for newton_step in range(NEWTON):
        denominator = aerosol + sat
        fraction = mass / denominator
        first_sum = jnp.sum(fraction, axis=-2, keepdims=True)
        second_sum = jnp.sum(fraction / denominator, axis=-2, keepdims=True)
        residue = 1.0 - seed / aerosol - first_sum
        derivative = seed / (aerosol * aerosol) + second_sum
        history.append((aerosol, residue, derivative))
        aerosol = aerosol - residue / derivative
    final_den = aerosol + sat
    particle = mass * aerosol / final_den
    mass_bar = cot * aerosol / final_den
    aerosol_bar = jnp.sum(cot * mass * sat / (final_den * final_den), axis=-2, keepdims=True)
    for newton_step in reversed(range(NEWTON)):
        a_n, residue, derivative = history[newton_step]
        inverse = 1.0 / (a_n + sat)
        third_sum = jnp.sum(mass * inverse * inverse * inverse, axis=-2, keepdims=True)
        slope = -2.0 * (seed / (a_n * a_n * a_n) + third_sum)
        over_g = aerosol_bar / derivative
        over_g2 = over_g * residue / derivative
        mass_bar = mass_bar + over_g * inverse + over_g2 * inverse * inverse
        aerosol_bar = over_g2 * slope
    gradient = mass_bar * 0.5 * (1.0 + x / root)
    return jnp.where(valid, particle, 0.0), jnp.where(valid, gradient, 0.0)


def owner_kernel(x_ref, c_ref, s_ref, w_ref, m_ref, v_ref, t_ref, p_ref, g_ref,
                 out_go, land_go, out_back, land_back, field_s, sem_a, sem_b, sem_c, sem_d):
    count = t_ref.shape[0]
    polar_count, col_count, channels = x_ref.shape
    levels = s_ref.shape[2]
    chunk = channels // count
    padded = out_go.shape[1] // 2
    me = lax.axis_index("lon")
    band = lax.axis_index("lat")
    bands = lax.axis_size("lat")
    active = jnp.logical_or(band == 0, band == bands - 1)
    hi = lax.Precision.HIGHEST
    mesh_id = pl.DeviceIdType.MESH
    nt = (((1,), (1,)), ((), ()))

    def remote(src, dst, send_sem, recv_sem, peer):
        return pltpu.make_async_remote_copy(
            src_ref=src, dst_ref=dst, send_sem=send_sem, recv_sem=recv_sem,
            device_id=(band, peer), device_id_type=mesh_id,
        )

    def round_trip(outbox, inbox, send_sems, recv_sems):
        for offset in range(1, count):
            peer = lax.rem(me + offset, count)
            remote(outbox.at[peer], inbox.at[me], send_sems.at[offset], recv_sems.at[me], peer).start()
        inbox[pl.ds(me, 1)] = outbox[pl.ds(me, 1)]
        for offset in range(1, count):
            peer = lax.rem(me + offset, count)
            remote(outbox.at[peer], inbox.at[me], send_sems.at[offset], recv_sems.at[me], peer).wait_send()
        for offset in range(1, count):
            peer = lax.rem(me + count - offset, count)
            remote(outbox.at[peer], inbox.at[peer], send_sems.at[offset], recv_sems.at[peer], peer).wait_recv()

    @pl.when(active)
    def _():
        barrier = pltpu.get_barrier_semaphore()
        for offset in range(1, count):
            peer = lax.rem(me + offset, count)
            pl.semaphore_signal(barrier, 1, device_id=(band, peer), device_id_type=mesh_id)
        pl.semaphore_wait(barrier, count - 1)
        wide = channels + levels
        slot = lax.broadcasted_iota(jnp.int32, (count * padded, wide), 0)
        channel = lax.broadcasted_iota(jnp.int32, (count * padded, wide), 1)
        target = jnp.where(
            channel < channels,
            (channel // chunk) * padded + channel % chunk,
            (channel - channels) * padded + chunk,
        )
        packer_wide = jnp.where(slot == target, 1.0, 0.0).astype(jnp.bfloat16)
        packer = packer_wide[:, :channels]
        rows = jnp.concatenate(
            [jnp.concatenate([x_ref[r], s_ref[r]], axis=1) for r in range(polar_count)], axis=0
        )
        cots = jnp.concatenate([c_ref[r] for r in range(polar_count)], axis=0)
        lanes = polar_count * col_count
        out_go[:, 0:padded, :] = select_dot_left(packer_wide, rows, nt).reshape(count, padded, lanes)
        out_go[:, padded:, :] = select_dot_left(packer, cots, nt).reshape(count, padded, lanes)
        round_trip(out_go, land_go, sem_a, sem_b)

        def analyse(s, acc):
            return acc + jnp.dot(land_go[s, 0:padded, :], t_ref[s], precision=hi,
                                 preferred_element_type=jnp.float32)

        zero = jnp.zeros((padded, t_ref.shape[2]), jnp.float32)
        coefficient = lax.fori_loop(0, count, analyse, zero) * w_ref[...]
        keep_lane = m_ref[...] > 0.5
        species_row = lax.broadcasted_iota(jnp.int32, (padded, lanes), 0)
        valid = species_row < chunk
        sat = v_ref[...]

        def smooth_out(s, carry):
            smooth = lax.dot_general(coefficient, t_ref[s], nt, precision=hi,
                                     preferred_element_type=jnp.float32)
            field_s[s] = jnp.where(keep_lane, smooth, land_go[s, 0:padded, :])
            return carry

        lax.fori_loop(0, count, smooth_out, 0)
        particle, gradient = column_chemistry(
            field_s[...],
            land_go[:, chunk : chunk + 1, :],
            land_go[:, padded:, :],
            sat[None],
            valid[None],
        )
        out_back[:, 0:padded, :] = particle
        field_s[...] = gradient

        def gather_adjoint(s, acc):
            return acc + jnp.dot(field_s[s], t_ref[s], precision=hi,
                                 preferred_element_type=jnp.float32)

        adjoint_coef = lax.fori_loop(0, count, gather_adjoint, zero) * w_ref[...]

        def synthesise(s, carry):
            smooth = lax.dot_general(adjoint_coef, t_ref[s], nt, precision=hi,
                                     preferred_element_type=jnp.float32)
            out_back[s, padded:, :] = jnp.where(keep_lane, smooth, field_s[s])
            return carry

        lax.fori_loop(0, count, synthesise, 0)
        round_trip(out_back, land_back, sem_c, sem_d)
        particle_back = land_back[:, 0:padded, :].reshape(count * padded, lanes)
        gradient_back = land_back[:, padded:, :].reshape(count * padded, lanes)
        particle_rows = select_dot(particle_back, packer, (((0,), (0,)), ((), ())))
        gradient_rows = select_dot(gradient_back, packer, (((0,), (0,)), ((), ())))
        for r in range(polar_count):
            p_ref[r] = particle_rows[r * col_count : (r + 1) * col_count]
            g_ref[r] = gradient_rows[r * col_count : (r + 1) * col_count]

    @pl.when(jnp.logical_not(active))
    def _():
        p_ref[...] = jnp.zeros_like(p_ref)
        g_ref[...] = jnp.zeros_like(g_ref)


def polar_step(field, seed_aerosol, volatility, cotangent, filter_keep, particle, gradient):
    row_count, col_count, channels = field.shape
    count = lax.axis_size("lon")
    length = col_count * count
    species = volatility.shape[0]
    polar_count = POLAR
    band = lax.axis_index("lat")
    at_north_end = band == 0
    at_south_end = band == lax.axis_size("lat") - 1

    def ends(values):
        return jnp.where(at_north_end, values[:polar_count], values[row_count - polar_count :])

    end_keep = ends(filter_keep)
    table = wave_table(length, length).reshape(count, col_count, 2 * KMAX)
    blocks = jnp.einsum(
        "sjk,rR->srjRk", table, jnp.eye(polar_count, dtype=jnp.float32)
    ).reshape(count, polar_count * col_count, polar_count * 2 * KMAX)
    weights = wave_weights(end_keep, length).reshape(1, polar_count * 2 * KMAX)
    lane_mask = jnp.repeat((end_keep <= KMAX).astype(jnp.float32), col_count)[None, :]
    padded = -(-(channels // count + 1) // 8) * 8
    sat = jnp.concatenate(
        [volatility, jnp.ones((padded - species,), jnp.float32)]
    )[:, None]
    slab = (count, 2 * padded, polar_count * col_count)
    vmem = pl.BlockSpec(memory_space=pltpu.VMEM)
    end_shape = jax.ShapeDtypeStruct((polar_count, col_count, channels), jnp.float32)
    polar_particle, polar_gradient = pl.pallas_call(
        owner_kernel,
        out_shape=[end_shape, end_shape],
        in_specs=[vmem] * 7,
        out_specs=[vmem, vmem],
        scratch_shapes=[
            pltpu.VMEM(slab, jnp.float32),
            pltpu.VMEM(slab, jnp.float32),
            pltpu.VMEM(slab, jnp.float32),
            pltpu.VMEM(slab, jnp.float32),
            pltpu.VMEM((count, padded, polar_count * col_count), jnp.float32),
            pltpu.SemaphoreType.DMA((count,)),
            pltpu.SemaphoreType.DMA((count,)),
            pltpu.SemaphoreType.DMA((count,)),
            pltpu.SemaphoreType.DMA((count,)),
        ],
        compiler_params=pltpu.CompilerParams(collective_id=0, has_side_effects=True),
    )(ends(field), ends(cotangent), ends(seed_aerosol), weights, lane_mask, sat, blocks)

    def merge(values, polar):
        top = jnp.where(at_north_end, polar, values[:polar_count])
        bottom = jnp.where(at_south_end, polar, values[row_count - polar_count :])
        return jnp.concatenate(
            [top, values[polar_count : row_count - polar_count], bottom], axis=0
        )

    return merge(particle, polar_particle), merge(gradient, polar_gradient)


def filter_field(field, filter_keep, call_id):
    row_count, col_count, channels = field.shape
    count = lax.axis_size("lon")
    length = col_count * count
    polar_count = POLAR
    band = lax.axis_index("lat")
    at_north_end = band == 0
    at_south_end = band == lax.axis_size("lat") - 1
    top_rows = field[:polar_count]
    bottom_rows = field[row_count - polar_count :]
    end_rows = jnp.where(at_north_end, top_rows, bottom_rows)
    end_keep = jnp.where(
        at_north_end, filter_keep[:polar_count], filter_keep[row_count - polar_count :]
    )
    table = wave_table(length, length).reshape(count, col_count, 2 * KMAX)
    blocks = jnp.einsum(
        "sjk,rR->srjRk", table, jnp.eye(polar_count, dtype=jnp.float32)
    ).reshape(count, polar_count * col_count, polar_count * 2 * KMAX)
    weights = wave_weights(end_keep, length).reshape(1, polar_count * 2 * KMAX)
    lowpass = polar_lowpass(end_rows, weights, blocks, call_id)
    smoothed = jnp.where((end_keep <= KMAX)[:, None, None], lowpass, end_rows)
    new_top = jnp.where(at_north_end, smoothed, top_rows)
    new_bottom = jnp.where(at_south_end, smoothed, bottom_rows)
    return jnp.concatenate(
        [new_top, field[polar_count : row_count - polar_count], new_bottom], axis=0
    )


def chem_kernel(x_ref, seed_ref, cot_ref, sat_ref, spread_ref, group_ref, p_ref, g_ref):
    hi = lax.Precision.HIGHEST
    x = x_ref[0]
    seed = seed_ref[0]
    cot = cot_ref[0]
    sat = sat_ref[...]
    spread_m = spread_ref[...].astype(jnp.bfloat16)
    group_m = group_ref[...].astype(jnp.bfloat16)

    plain = (((1,), (0,)), ((), ()))

    def up(v):
        return select_dot(v, spread_m, plain)

    def down(v):
        return select_dot(v, group_m, plain)

    root = jnp.sqrt(x * x + 1.0)
    mass = 0.5 * (x + root)
    aerosol = seed
    history = []
    for newton_step in range(NEWTON):
        denominator = up(aerosol) + sat
        fraction = mass / denominator
        first_sum = down(fraction)
        second_sum = down(fraction / denominator)
        residue = 1.0 - seed / aerosol - first_sum
        derivative = seed / (aerosol * aerosol) + second_sum
        history.append((aerosol, residue, derivative))
        aerosol = aerosol - residue / derivative
    aerosol_q = up(aerosol)
    final_den = aerosol_q + sat
    p_ref[0] = mass * aerosol_q / final_den
    mass_bar = cot * aerosol_q / final_den
    aerosol_bar = down(cot * mass * sat / (final_den * final_den))
    for newton_step in reversed(range(NEWTON)):
        a_n, residue, derivative = history[newton_step]
        inverse = 1.0 / (up(a_n) + sat)
        third_sum = down(mass * inverse * inverse * inverse)
        slope = -2.0 * (seed / (a_n * a_n * a_n) + third_sum)
        over_g = aerosol_bar / derivative
        over_g2 = over_g * residue / derivative
        mass_bar = mass_bar + up(over_g) * inverse + up(over_g2) * inverse * inverse
        aerosol_bar = over_g2 * slope
    g_ref[0] = mass_bar * 0.5 * (1.0 + x / root)


def chemistry_step(filtered, seed_aerosol, volatility, cotangent):
    rows, cols, channels = filtered.shape
    levels = seed_aerosol.shape[-1]
    species = volatility.shape[0]
    group_m = level_table(levels, species)
    spread_m = group_m.T
    sat = jnp.tile(volatility, levels)[None, :]
    big = pl.BlockSpec((1, cols, channels), lambda i: (i, 0, 0))
    small = pl.BlockSpec((1, cols, levels), lambda i: (i, 0, 0))
    return pl.pallas_call(
        chem_kernel,
        grid=(rows,),
        in_specs=[
            big,
            small,
            big,
            pl.BlockSpec((1, channels), lambda i: (0, 0)),
            pl.BlockSpec((levels, channels), lambda i: (0, 0)),
            pl.BlockSpec((channels, levels), lambda i: (0, 0)),
        ],
        out_specs=[big, big],
        out_shape=[
            jax.ShapeDtypeStruct(filtered.shape, jnp.float32),
            jax.ShapeDtypeStruct(filtered.shape, jnp.float32),
        ],
    )(filtered, seed_aerosol, cotangent, sat, spread_m, group_m)


def local(
    tracer,
    east_courant,
    north_courant,
    east_limiter,
    north_limiter,
    filter_keep,
    seed_aerosol,
    volatility,
    cotangent,
):
    row_count = tracer.shape[0]
    channels = tracer.shape[2]
    levels = east_courant.shape[2]
    species = volatility.shape[0]
    first_row = lax.axis_index("lat") * row_count
    packed = jnp.concatenate([tracer, east_courant, east_limiter.astype(jnp.float32)], axis=2)
    widened = east_west(packed)
    east_speed = widened[:, :, channels : channels + levels]
    east_choice = widened[:, :, channels + levels :].astype(jnp.int32)

    def zonal_only(window):
        return zonal_window(window, east_speed, east_choice, species)

    after_east, east_back = jax.vjp(zonal_only, widened[:, :, :channels])
    stacked = jnp.concatenate(
        [after_east, north_courant, north_limiter.astype(jnp.float32)], axis=2
    )
    tall_window = north_south(stacked)
    north_speed = tall_window[:, :, channels : channels + levels]
    north_choice = tall_window[:, :, channels + levels :].astype(jnp.int32)

    def meridional_only(window):
        return meridional_window(window, north_speed, north_choice, first_row, species)

    after_north, north_back = jax.vjp(meridional_only, tall_window[:, :, :channels])
    particle, chem_grad = chemistry_step(after_north, seed_aerosol, volatility, cotangent)
    particle, adjoint_filtered = polar_step(
        after_north, seed_aerosol, volatility, cotangent, filter_keep, particle, chem_grad
    )
    return (particle, fold_columns(east_back(fold_rows(north_back(adjoint_filtered)[0]))[0]))


def solution(mesh):
    in_specs = (
        P("lat", "lon", None),
        P("lat", "lon", None),
        P("lat", "lon", None),
        P("lat", "lon", None),
        P("lat", "lon", None),
        P("lat"),
        P("lat", "lon", None),
        P(),
        P("lat", "lon", None),
    )
    out_specs = (P("lat", "lon", None), P("lat", "lon", None))
    return jax.shard_map(local, mesh=mesh, in_specs=in_specs, out_specs=out_specs, check_vma=False)
```

```python
import math

import jax
import jax.numpy as jnp
from jax import lax
from jax.sharding import PartitionSpec as P
from jax.experimental import pallas as pl
from jax.experimental.pallas import tpu as pltpu

NEWTON = 4
KMAX = 32
POLAR = 2


def with_halo(cells, sides, width, closed):
    for axis, dim in sides:
        count = lax.axis_size(axis)
        ends = count if closed else count - 1
        head = lax.slice_in_dim(cells, 0, width, axis=dim)
        tail = lax.slice_in_dim(cells, cells.shape[dim] - width, cells.shape[dim], axis=dim)
        cells = jnp.concatenate(
            [
                lax.ppermute(tail, axis, [(i, (i + 1) % count) for i in range(ends)]),
                cells,
                lax.ppermute(head, axis, [((i + 1) % count, i) for i in range(ends)]),
            ],
            axis=dim,
        )
    return cells


def spread(values, copies):
    return jnp.repeat(values, copies, axis=-1)


def face_weights(courant, limiter):
    upwind = courant >= 0.0
    half = 0.5 * courant
    inner = courant * (7.0 / 12.0)
    outer = jnp.where(limiter == 0, courant * (-1.0 / 12.0), 0.0)
    near_left = jnp.where(
        limiter == 0, inner, jnp.where(limiter == 1, jnp.where(upwind, courant, 0.0), half)
    )
    near_right = jnp.where(
        limiter == 0, inner, jnp.where(limiter == 1, jnp.where(upwind, 0.0, courant), half)
    )
    return jnp.stack([outer, near_left, near_right], axis=0)


def spread_weights(weights, species):
    levels = weights.shape[-1]
    spread_m = level_table(levels, species).T
    return jnp.einsum("...l,lq->...q", weights, spread_m, precision=lax.Precision.HIGHEST)


def zonal_window(window, courant, limiter, species):
    inner_count = window.shape[1] - 4
    weights = spread_weights(
        face_weights(courant[:, 2 : inner_count + 3], limiter[:, 2 : inner_count + 3]), species
    )
    fluxes = (
        weights[0] * (window[:, 0 : inner_count + 1] + window[:, 3 : inner_count + 4])
        + weights[1] * window[:, 1 : inner_count + 2]
        + weights[2] * window[:, 2 : inner_count + 3]
    )
    return window[:, 2 : inner_count + 2] - (fluxes[:, 1:] - fluxes[:, :-1])


def meridional_window(window, courant, limiter, first_row, species):
    inner_count = window.shape[0] - 4
    face_rows = first_row + jnp.arange(inner_count + 1, dtype=jnp.int32)
    opened = jnp.where(face_rows[:, None, None] > 0, courant[2 : inner_count + 3], 0.0)
    weights = spread_weights(face_weights(opened, limiter[2 : inner_count + 3]), species)
    fluxes = (
        weights[0] * (window[0 : inner_count + 1] + window[3 : inner_count + 4])
        + weights[1] * window[1 : inner_count + 2]
        + weights[2] * window[2 : inner_count + 3]
    )
    return window[2 : inner_count + 2] - (fluxes[1:] - fluxes[:-1])


def positive(field):
    return 0.5 * (field + jnp.sqrt(field * field + 1.0))


def level_table(levels, species):
    channel_level = jnp.arange(levels * species, dtype=jnp.int32) // species
    return (channel_level[:, None] == jnp.arange(levels, dtype=jnp.int32)[None, :]).astype(
        jnp.float32
    )


def partition(total_mass, seed_aerosol, volatility):
    levels = seed_aerosol.shape[-1]
    species = volatility.shape[0]
    grouping = level_table(levels, species)
    saturation = jnp.tile(volatility, levels)
    aerosol = seed_aerosol
    for newton_step in range(NEWTON):
        denominator = spread(aerosol, species) + saturation
        fraction = total_mass / denominator
        first_sum = jnp.dot(fraction, grouping, precision=lax.Precision.HIGHEST)
        second_sum = jnp.dot(fraction / denominator, grouping, precision=lax.Precision.HIGHEST)
        residue = 1.0 - seed_aerosol / aerosol - first_sum
        derivative = seed_aerosol / (aerosol * aerosol) + second_sum
        aerosol = aerosol - residue / derivative
    aerosol_q = spread(aerosol, species)
    return total_mass * aerosol_q / (aerosol_q + saturation)


def east_west(field):
    return with_halo(field, (("lon", 1),), 2, True)


def north_south(field):
    return with_halo(field, (("lat", 0),), 2, False)


def fold_rows(gradient):
    inner_rows = gradient.shape[0] - 4
    rim_cells = jnp.concatenate([gradient[:2], gradient[inner_rows + 2 :]], axis=0)
    arrived = north_south(rim_cells)
    middle = gradient[2 : inner_rows + 2]
    return jnp.concatenate(
        [
            middle[:2] + arrived[:2],
            middle[2 : inner_rows - 2],
            middle[inner_rows - 2 :] + arrived[6:],
        ],
        axis=0,
    )


def fold_columns(gradient):
    inner_cols = gradient.shape[1] - 4
    rim_cells = jnp.concatenate([gradient[:, :2], gradient[:, inner_cols + 2 :]], axis=1)
    arrived = east_west(rim_cells)
    middle = gradient[:, 2 : inner_cols + 2]
    return jnp.concatenate(
        [
            middle[:, :2] + arrived[:, :2],
            middle[:, 2 : inner_cols - 2],
            middle[:, inner_cols - 2 :] + arrived[:, 6:],
        ],
        axis=1,
    )


def wave_table(column_count, length):
    position = jnp.arange(column_count, dtype=jnp.int32)
    numbers = jnp.arange(KMAX, dtype=jnp.int32)
    phases = position[:, None] * numbers[None, :] % length
    angles = phases.astype(jnp.float32) * (2.0 * math.pi / length)
    return jnp.concatenate([jnp.cos(angles), jnp.sin(angles)], axis=1)


def wave_weights(keep_values, length):
    numbers = jnp.arange(2 * KMAX, dtype=jnp.int32) % KMAX
    scaling = jnp.where(numbers == 0, 1.0, 2.0) / length
    kept_mask = numbers[None, :] < keep_values[:, None]
    return jnp.where(kept_mask, scaling[None, :], 0.0)


def lowpass_circles(circles, keep_values):
    length = circles.shape[2]
    table_full = wave_table(length, length)
    coefficient = jnp.einsum("rqn,nk->rqk", circles, table_full, precision=lax.Precision.HIGHEST)
    coefficient = coefficient * wave_weights(keep_values, length)[:, None, :]
    lowpass = jnp.einsum("rqk,nk->rqn", coefficient, table_full, precision=lax.Precision.HIGHEST)
    return jnp.where((keep_values <= KMAX)[:, None, None], lowpass, circles)


def split_three(values):
    high = values.astype(jnp.bfloat16)
    rest = values - high.astype(jnp.float32)
    middle = rest.astype(jnp.bfloat16)
    low = (rest - middle.astype(jnp.float32)).astype(jnp.bfloat16)
    return high, middle, low


def select_dot(values, selector, dims):
    total = None
    for piece in split_three(values):
        term = lax.dot_general(piece, selector, dims, preferred_element_type=jnp.float32)
        total = term if total is None else total + term
    return total


def select_dot_left(selector, values, dims):
    total = None
    for piece in split_three(values):
        term = lax.dot_general(selector, piece, dims, preferred_element_type=jnp.float32)
        total = term if total is None else total + term
    return total


def polar_kernel(x_ref, w_ref, t_ref, y_ref, out_go, land_go, out_back, land_back,
                 sem_a, sem_b, sem_c, sem_d):
    count = t_ref.shape[0]
    polar_count, col_count, channels = x_ref.shape
    chunk = channels // count
    padded = out_go.shape[1]
    me = lax.axis_index("lon")
    band = lax.axis_index("lat")
    bands = lax.axis_size("lat")
    active = jnp.logical_or(band == 0, band == bands - 1)
    hi = lax.Precision.HIGHEST
    mesh_id = pl.DeviceIdType.MESH

    def remote(src, dst, send_sem, recv_sem, peer):
        return pltpu.make_async_remote_copy(
            src_ref=src, dst_ref=dst, send_sem=send_sem, recv_sem=recv_sem,
            device_id=(band, peer), device_id_type=mesh_id,
        )

    def round_trip(outbox, inbox, send_sems, recv_sems):
        for offset in range(1, count):
            peer = lax.rem(me + offset, count)
            remote(outbox.at[peer], inbox.at[me], send_sems.at[offset], recv_sems.at[me], peer).start()
        inbox[pl.ds(me, 1)] = outbox[pl.ds(me, 1)]
        for offset in range(1, count):
            peer = lax.rem(me + offset, count)
            remote(outbox.at[peer], inbox.at[me], send_sems.at[offset], recv_sems.at[me], peer).wait_send()
        for offset in range(1, count):
            peer = lax.rem(me + count - offset, count)
            remote(outbox.at[peer], inbox.at[peer], send_sems.at[offset], recv_sems.at[peer], peer).wait_recv()

    @pl.when(active)
    def _():
        barrier = pltpu.get_barrier_semaphore()
        for offset in range(1, count):
            peer = lax.rem(me + offset, count)
            pl.semaphore_signal(barrier, 1, device_id=(band, peer), device_id_type=mesh_id)
        pl.semaphore_wait(barrier, count - 1)
        rows = jnp.concatenate([x_ref[r] for r in range(polar_count)], axis=0)
        slot = lax.broadcasted_iota(jnp.int32, (count * padded, channels), 0)
        channel = lax.broadcasted_iota(jnp.int32, (count * padded, channels), 1)
        target = (channel // chunk) * padded + channel % chunk
        packer = jnp.where(slot == target, 1.0, 0.0).astype(jnp.bfloat16)
        packed = select_dot_left(packer, rows, (((1,), (1,)), ((), ())))
        out_go[...] = packed.reshape(count, padded, polar_count * col_count)
        round_trip(out_go, land_go, sem_a, sem_b)

        def analyse(s, acc):
            return acc + jnp.dot(land_go[s], t_ref[s], precision=hi,
                                 preferred_element_type=jnp.float32)

        coefficient = lax.fori_loop(
            0, count, analyse, jnp.zeros((padded, t_ref.shape[2]), jnp.float32)
        )
        coefficient = coefficient * w_ref[...]

        def synthesise(s, carry):
            out_back[s] = lax.dot_general(coefficient, t_ref[s], (((1,), (1,)), ((), ())),
                                          precision=hi, preferred_element_type=jnp.float32)
            return carry

        lax.fori_loop(0, count, synthesise, 0)
        round_trip(out_back, land_back, sem_c, sem_d)
        back = land_back[...].reshape(count * padded, polar_count * col_count)
        result = select_dot(back, packer, (((0,), (0,)), ((), ())))
        for r in range(polar_count):
            y_ref[r] = result[r * col_count : (r + 1) * col_count]

    @pl.when(jnp.logical_not(active))
    def _():
        y_ref[...] = x_ref[...]


def polar_lowpass(end_rows, weights, blocks, call_id):
    polar_count, col_count, channels = end_rows.shape
    count = blocks.shape[0]
    padded = -(-(channels // count) // 8) * 8
    slab = (count, padded, polar_count * col_count)
    vmem = pl.BlockSpec(memory_space=pltpu.VMEM)
    return pl.pallas_call(
        polar_kernel,
        out_shape=jax.ShapeDtypeStruct(end_rows.shape, end_rows.dtype),
        in_specs=[vmem, vmem, vmem],
        out_specs=vmem,
        scratch_shapes=[
            pltpu.VMEM(slab, jnp.float32),
            pltpu.VMEM(slab, jnp.float32),
            pltpu.VMEM(slab, jnp.float32),
            pltpu.VMEM(slab, jnp.float32),
            pltpu.SemaphoreType.DMA((count,)),
            pltpu.SemaphoreType.DMA((count,)),
            pltpu.SemaphoreType.DMA((count,)),
            pltpu.SemaphoreType.DMA((count,)),
        ],
        compiler_params=pltpu.CompilerParams(collective_id=call_id, has_side_effects=True),
    )(end_rows, weights, blocks)


def column_chemistry(x, seed, cot, sat, valid):
    root = jnp.sqrt(x * x + 1.0)
    mass = jnp.where(valid, 0.5 * (x + root), 0.0)
    cot = jnp.where(valid, cot, 0.0)
    aerosol = seed
    history = []
    for newton_step in range(NEWTON):
        denominator = aerosol + sat
        fraction = mass / denominator
        first_sum = jnp.sum(fraction, axis=-2, keepdims=True)
        second_sum = jnp.sum(fraction / denominator, axis=-2, keepdims=True)
        residue = 1.0 - seed / aerosol - first_sum
        derivative = seed / (aerosol * aerosol) + second_sum
        history.append((aerosol, residue, derivative))
        aerosol = aerosol - residue / derivative
    final_den = aerosol + sat
    particle = mass * aerosol / final_den
    mass_bar = cot * aerosol / final_den
    aerosol_bar = jnp.sum(cot * mass * sat / (final_den * final_den), axis=-2, keepdims=True)
    for newton_step in reversed(range(NEWTON)):
        a_n, residue, derivative = history[newton_step]
        inverse = 1.0 / (a_n + sat)
        third_sum = jnp.sum(mass * inverse * inverse * inverse, axis=-2, keepdims=True)
        slope = -2.0 * (seed / (a_n * a_n * a_n) + third_sum)
        over_g = aerosol_bar / derivative
        over_g2 = over_g * residue / derivative
        mass_bar = mass_bar + over_g * inverse + over_g2 * inverse * inverse
        aerosol_bar = over_g2 * slope
    gradient = mass_bar * 0.5 * (1.0 + x / root)
    return jnp.where(valid, particle, 0.0), jnp.where(valid, gradient, 0.0)


def owner_kernel(x_ref, c_ref, s_ref, w_ref, m_ref, v_ref, t_ref, p_ref, g_ref,
                 out_go, land_go, out_back, land_back, field_s, sem_a, sem_b, sem_c, sem_d):
    count = t_ref.shape[0]
    polar_count, col_count, channels = x_ref.shape
    levels = s_ref.shape[2]
    chunk = channels // count
    padded = out_go.shape[1] // 2
    me = lax.axis_index("lon")
    band = lax.axis_index("lat")
    bands = lax.axis_size("lat")
    active = jnp.logical_or(band == 0, band == bands - 1)
    hi = lax.Precision.HIGHEST
    mesh_id = pl.DeviceIdType.MESH
    nt = (((1,), (1,)), ((), ()))

    def remote(src, dst, send_sem, recv_sem, peer):
        return pltpu.make_async_remote_copy(
            src_ref=src, dst_ref=dst, send_sem=send_sem, recv_sem=recv_sem,
            device_id=(band, peer), device_id_type=mesh_id,
        )

    def round_trip(outbox, inbox, send_sems, recv_sems):
        for offset in range(1, count):
            peer = lax.rem(me + offset, count)
            remote(outbox.at[peer], inbox.at[me], send_sems.at[offset], recv_sems.at[me], peer).start()
        inbox[pl.ds(me, 1)] = outbox[pl.ds(me, 1)]
        for offset in range(1, count):
            peer = lax.rem(me + offset, count)
            remote(outbox.at[peer], inbox.at[me], send_sems.at[offset], recv_sems.at[me], peer).wait_send()
        for offset in range(1, count):
            peer = lax.rem(me + count - offset, count)
            remote(outbox.at[peer], inbox.at[peer], send_sems.at[offset], recv_sems.at[peer], peer).wait_recv()

    @pl.when(active)
    def _():
        barrier = pltpu.get_barrier_semaphore()
        for offset in range(1, count):
            peer = lax.rem(me + offset, count)
            pl.semaphore_signal(barrier, 1, device_id=(band, peer), device_id_type=mesh_id)
        pl.semaphore_wait(barrier, count - 1)
        wide = channels + levels
        slot = lax.broadcasted_iota(jnp.int32, (count * padded, wide), 0)
        channel = lax.broadcasted_iota(jnp.int32, (count * padded, wide), 1)
        target = jnp.where(
            channel < channels,
            (channel // chunk) * padded + channel % chunk,
            (channel - channels) * padded + chunk,
        )
        packer_wide = jnp.where(slot == target, 1.0, 0.0).astype(jnp.bfloat16)
        packer = packer_wide[:, :channels]
        rows = jnp.concatenate(
            [jnp.concatenate([x_ref[r], s_ref[r]], axis=1) for r in range(polar_count)], axis=0
        )
        cots = jnp.concatenate([c_ref[r] for r in range(polar_count)], axis=0)
        lanes = polar_count * col_count
        out_go[:, 0:padded, :] = select_dot_left(packer_wide, rows, nt).reshape(count, padded, lanes)
        out_go[:, padded:, :] = select_dot_left(packer, cots, nt).reshape(count, padded, lanes)
        round_trip(out_go, land_go, sem_a, sem_b)

        def analyse(s, acc):
            return acc + jnp.dot(land_go[s, 0:padded, :], t_ref[s], precision=hi,
                                 preferred_element_type=jnp.float32)

        zero = jnp.zeros((padded, t_ref.shape[2]), jnp.float32)
        coefficient = lax.fori_loop(0, count, analyse, zero) * w_ref[...]
        keep_lane = m_ref[...] > 0.5
        species_row = lax.broadcasted_iota(jnp.int32, (padded, lanes), 0)
        valid = species_row < chunk
        sat = v_ref[...]

        def smooth_out(s, carry):
            smooth = lax.dot_general(coefficient, t_ref[s], nt, precision=hi,
                                     preferred_element_type=jnp.float32)
            field_s[s] = jnp.where(keep_lane, smooth, land_go[s, 0:padded, :])
            return carry

        lax.fori_loop(0, count, smooth_out, 0)
        particle, gradient = column_chemistry(
            field_s[...],
            land_go[:, chunk : chunk + 1, :],
            land_go[:, padded:, :],
            sat[None],
            valid[None],
        )
        out_back[:, 0:padded, :] = particle
        field_s[...] = gradient

        def gather_adjoint(s, acc):
            return acc + jnp.dot(field_s[s], t_ref[s], precision=hi,
                                 preferred_element_type=jnp.float32)

        adjoint_coef = lax.fori_loop(0, count, gather_adjoint, zero) * w_ref[...]

        def synthesise(s, carry):
            smooth = lax.dot_general(adjoint_coef, t_ref[s], nt, precision=hi,
                                     preferred_element_type=jnp.float32)
            out_back[s, padded:, :] = jnp.where(keep_lane, smooth, field_s[s])
            return carry

        lax.fori_loop(0, count, synthesise, 0)
        round_trip(out_back, land_back, sem_c, sem_d)
        particle_back = land_back[:, 0:padded, :].reshape(count * padded, lanes)
        gradient_back = land_back[:, padded:, :].reshape(count * padded, lanes)
        particle_rows = select_dot(particle_back, packer, (((0,), (0,)), ((), ())))
        gradient_rows = select_dot(gradient_back, packer, (((0,), (0,)), ((), ())))
        for r in range(polar_count):
            p_ref[r] = particle_rows[r * col_count : (r + 1) * col_count]
            g_ref[r] = gradient_rows[r * col_count : (r + 1) * col_count]

    @pl.when(jnp.logical_not(active))
    def _():
        p_ref[...] = jnp.zeros_like(p_ref)
        g_ref[...] = jnp.zeros_like(g_ref)


def polar_step(field, seed_aerosol, volatility, cotangent, filter_keep, particle, gradient):
    row_count, col_count, channels = field.shape
    count = lax.axis_size("lon")
    length = col_count * count
    species = volatility.shape[0]
    polar_count = POLAR
    band = lax.axis_index("lat")
    at_north_end = band == 0
    at_south_end = band == lax.axis_size("lat") - 1

    def ends(values):
        return jnp.where(at_north_end, values[:polar_count], values[row_count - polar_count :])

    end_keep = ends(filter_keep)
    table = wave_table(length, length).reshape(count, col_count, 2 * KMAX)
    blocks = jnp.einsum(
        "sjk,rR->srjRk", table, jnp.eye(polar_count, dtype=jnp.float32)
    ).reshape(count, polar_count * col_count, polar_count * 2 * KMAX)
    weights = wave_weights(end_keep, length).reshape(1, polar_count * 2 * KMAX)
    lane_mask = jnp.repeat((end_keep <= KMAX).astype(jnp.float32), col_count)[None, :]
    padded = -(-(channels // count + 1) // 8) * 8
    sat = jnp.concatenate(
        [volatility, jnp.ones((padded - species,), jnp.float32)]
    )[:, None]
    slab = (count, 2 * padded, polar_count * col_count)
    vmem = pl.BlockSpec(memory_space=pltpu.VMEM)
    end_shape = jax.ShapeDtypeStruct((polar_count, col_count, channels), jnp.float32)
    polar_particle, polar_gradient = pl.pallas_call(
        owner_kernel,
        out_shape=[end_shape, end_shape],
        in_specs=[vmem] * 7,
        out_specs=[vmem, vmem],
        scratch_shapes=[
            pltpu.VMEM(slab, jnp.float32),
            pltpu.VMEM(slab, jnp.float32),
            pltpu.VMEM(slab, jnp.float32),
            pltpu.VMEM(slab, jnp.float32),
            pltpu.VMEM((count, padded, polar_count * col_count), jnp.float32),
            pltpu.SemaphoreType.DMA((count,)),
            pltpu.SemaphoreType.DMA((count,)),
            pltpu.SemaphoreType.DMA((count,)),
            pltpu.SemaphoreType.DMA((count,)),
        ],
        compiler_params=pltpu.CompilerParams(collective_id=0, has_side_effects=True),
    )(ends(field), ends(cotangent), ends(seed_aerosol), weights, lane_mask, sat, blocks)

    def merge(values, polar):
        top = jnp.where(at_north_end, polar, values[:polar_count])
        bottom = jnp.where(at_south_end, polar, values[row_count - polar_count :])
        return jnp.concatenate(
            [top, values[polar_count : row_count - polar_count], bottom], axis=0
        )

    return merge(particle, polar_particle), merge(gradient, polar_gradient)


def filter_field(field, filter_keep, call_id):
    row_count, col_count, channels = field.shape
    count = lax.axis_size("lon")
    length = col_count * count
    polar_count = POLAR
    band = lax.axis_index("lat")
    at_north_end = band == 0
    at_south_end = band == lax.axis_size("lat") - 1
    top_rows = field[:polar_count]
    bottom_rows = field[row_count - polar_count :]
    end_rows = jnp.where(at_north_end, top_rows, bottom_rows)
    end_keep = jnp.where(
        at_north_end, filter_keep[:polar_count], filter_keep[row_count - polar_count :]
    )
    table = wave_table(length, length).reshape(count, col_count, 2 * KMAX)
    blocks = jnp.einsum(
        "sjk,rR->srjRk", table, jnp.eye(polar_count, dtype=jnp.float32)
    ).reshape(count, polar_count * col_count, polar_count * 2 * KMAX)
    weights = wave_weights(end_keep, length).reshape(1, polar_count * 2 * KMAX)
    lowpass = polar_lowpass(end_rows, weights, blocks, call_id)
    smoothed = jnp.where((end_keep <= KMAX)[:, None, None], lowpass, end_rows)
    new_top = jnp.where(at_north_end, smoothed, top_rows)
    new_bottom = jnp.where(at_south_end, smoothed, bottom_rows)
    return jnp.concatenate(
        [new_top, field[polar_count : row_count - polar_count], new_bottom], axis=0
    )


def chem_kernel(x_ref, seed_ref, cot_ref, sat_ref, spread_ref, group_ref, p_ref, g_ref):
    row = pl.program_id(0)
    rows = pl.num_programs(0)
    band = lax.axis_index("lat")
    bands = lax.axis_size("lat")
    polar = jnp.logical_or(
        jnp.logical_and(band == 0, row < POLAR),
        jnp.logical_and(band == bands - 1, row >= rows - POLAR),
    )

    @pl.when(jnp.logical_not(polar))
    def _():
        chem_body(x_ref, seed_ref, cot_ref, sat_ref, spread_ref, group_ref, p_ref, g_ref)


def chem_body(x_ref, seed_ref, cot_ref, sat_ref, spread_ref, group_ref, p_ref, g_ref):
    hi = lax.Precision.HIGHEST
    x = x_ref[0]
    seed = seed_ref[0]
    cot = cot_ref[0]
    sat = sat_ref[...]
    spread_m = spread_ref[...].astype(jnp.bfloat16)
    group_m = group_ref[...].astype(jnp.bfloat16)

    plain = (((1,), (0,)), ((), ()))

    def up(v):
        return select_dot(v, spread_m, plain)

    def down(v):
        return select_dot(v, group_m, plain)

    root = jnp.sqrt(x * x + 1.0)
    mass = 0.5 * (x + root)
    aerosol = seed
    history = []
    for newton_step in range(NEWTON):
        denominator = up(aerosol) + sat
        fraction = mass / denominator
        first_sum = down(fraction)
        second_sum = down(fraction / denominator)
        residue = 1.0 - seed / aerosol - first_sum
        derivative = seed / (aerosol * aerosol) + second_sum
        history.append((aerosol, residue, derivative))
        aerosol = aerosol - residue / derivative
    aerosol_q = up(aerosol)
    final_den = aerosol_q + sat
    p_ref[0] = mass * aerosol_q / final_den
    mass_bar = cot * aerosol_q / final_den
    aerosol_bar = down(cot * mass * sat / (final_den * final_den))
    for newton_step in reversed(range(NEWTON)):
        a_n, residue, derivative = history[newton_step]
        inverse = 1.0 / (up(a_n) + sat)
        third_sum = down(mass * inverse * inverse * inverse)
        slope = -2.0 * (seed / (a_n * a_n * a_n) + third_sum)
        over_g = aerosol_bar / derivative
        over_g2 = over_g * residue / derivative
        mass_bar = mass_bar + up(over_g) * inverse + up(over_g2) * inverse * inverse
        aerosol_bar = over_g2 * slope
    g_ref[0] = mass_bar * 0.5 * (1.0 + x / root)


def chemistry_step(filtered, seed_aerosol, volatility, cotangent):
    rows, cols, channels = filtered.shape
    levels = seed_aerosol.shape[-1]
    species = volatility.shape[0]
    group_m = level_table(levels, species)
    spread_m = group_m.T
    sat = jnp.tile(volatility, levels)[None, :]
    big = pl.BlockSpec((1, cols, channels), lambda i: (i, 0, 0))
    small = pl.BlockSpec((1, cols, levels), lambda i: (i, 0, 0))
    return pl.pallas_call(
        chem_kernel,
        grid=(rows,),
        in_specs=[
            big,
            small,
            big,
            pl.BlockSpec((1, channels), lambda i: (0, 0)),
            pl.BlockSpec((levels, channels), lambda i: (0, 0)),
            pl.BlockSpec((channels, levels), lambda i: (0, 0)),
        ],
        out_specs=[big, big],
        out_shape=[
            jax.ShapeDtypeStruct(filtered.shape, jnp.float32),
            jax.ShapeDtypeStruct(filtered.shape, jnp.float32),
        ],
    )(filtered, seed_aerosol, cotangent, sat, spread_m, group_m)


def local(
    tracer,
    east_courant,
    north_courant,
    east_limiter,
    north_limiter,
    filter_keep,
    seed_aerosol,
    volatility,
    cotangent,
):
    row_count = tracer.shape[0]
    channels = tracer.shape[2]
    levels = east_courant.shape[2]
    species = volatility.shape[0]
    first_row = lax.axis_index("lat") * row_count
    packed = jnp.concatenate([tracer, east_courant, east_limiter.astype(jnp.float32)], axis=2)
    widened = east_west(packed)
    east_speed = widened[:, :, channels : channels + levels]
    east_choice = widened[:, :, channels + levels :].astype(jnp.int32)

    def zonal_only(window):
        return zonal_window(window, east_speed, east_choice, species)

    after_east, east_back = jax.vjp(zonal_only, widened[:, :, :channels])
    stacked = jnp.concatenate(
        [after_east, north_courant, north_limiter.astype(jnp.float32)], axis=2
    )
    tall_window = north_south(stacked)
    north_speed = tall_window[:, :, channels : channels + levels]
    north_choice = tall_window[:, :, channels + levels :].astype(jnp.int32)

    def meridional_only(window):
        return meridional_window(window, north_speed, north_choice, first_row, species)

    after_north, north_back = jax.vjp(meridional_only, tall_window[:, :, :channels])
    particle, chem_grad = chemistry_step(after_north, seed_aerosol, volatility, cotangent)
    particle, adjoint_filtered = polar_step(
        after_north, seed_aerosol, volatility, cotangent, filter_keep, particle, chem_grad
    )
    return (particle, fold_columns(east_back(fold_rows(north_back(adjoint_filtered)[0]))[0]))


def solution(mesh):
    in_specs = (
        P("lat", "lon", None),
        P("lat", "lon", None),
        P("lat", "lon", None),
        P("lat", "lon", None),
        P("lat", "lon", None),
        P("lat"),
        P("lat", "lon", None),
        P(),
        P("lat", "lon", None),
    )
    out_specs = (P("lat", "lon", None), P("lat", "lon", None))
    return jax.shard_map(local, mesh=mesh, in_specs=in_specs, out_specs=out_specs, check_vma=False)
```

```python
import math

import jax
import jax.numpy as jnp
from jax import lax
from jax.sharding import PartitionSpec as P
from jax.experimental import pallas as pl
from jax.experimental.pallas import tpu as pltpu

NEWTON = 4
KMAX = 32
POLAR = 2


def with_halo(cells, sides, width, closed):
    for axis, dim in sides:
        count = lax.axis_size(axis)
        ends = count if closed else count - 1
        head = lax.slice_in_dim(cells, 0, width, axis=dim)
        tail = lax.slice_in_dim(cells, cells.shape[dim] - width, cells.shape[dim], axis=dim)
        cells = jnp.concatenate(
            [
                lax.ppermute(tail, axis, [(i, (i + 1) % count) for i in range(ends)]),
                cells,
                lax.ppermute(head, axis, [((i + 1) % count, i) for i in range(ends)]),
            ],
            axis=dim,
        )
    return cells


def spread(values, copies):
    return jnp.repeat(values, copies, axis=-1)


def face_weights(courant, limiter):
    upwind = courant >= 0.0
    half = 0.5 * courant
    inner = courant * (7.0 / 12.0)
    outer = jnp.where(limiter == 0, courant * (-1.0 / 12.0), 0.0)
    near_left = jnp.where(
        limiter == 0, inner, jnp.where(limiter == 1, jnp.where(upwind, courant, 0.0), half)
    )
    near_right = jnp.where(
        limiter == 0, inner, jnp.where(limiter == 1, jnp.where(upwind, 0.0, courant), half)
    )
    return jnp.stack([outer, near_left, near_right], axis=0)


def spread_weights(weights, species):
    levels = weights.shape[-1]
    spread_m = level_table(levels, species).T
    return jnp.einsum("...l,lq->...q", weights, spread_m, precision=lax.Precision.HIGHEST)


def zonal_window(window, courant, limiter, species):
    inner_count = window.shape[1] - 4
    weights = spread_weights(
        face_weights(courant[:, 2 : inner_count + 3], limiter[:, 2 : inner_count + 3]), species
    )
    fluxes = (
        weights[0] * (window[:, 0 : inner_count + 1] + window[:, 3 : inner_count + 4])
        + weights[1] * window[:, 1 : inner_count + 2]
        + weights[2] * window[:, 2 : inner_count + 3]
    )
    return window[:, 2 : inner_count + 2] - (fluxes[:, 1:] - fluxes[:, :-1])


def meridional_window(window, courant, limiter, first_row, species):
    inner_count = window.shape[0] - 4
    face_rows = first_row + jnp.arange(inner_count + 1, dtype=jnp.int32)
    opened = jnp.where(face_rows[:, None, None] > 0, courant[2 : inner_count + 3], 0.0)
    weights = spread_weights(face_weights(opened, limiter[2 : inner_count + 3]), species)
    fluxes = (
        weights[0] * (window[0 : inner_count + 1] + window[3 : inner_count + 4])
        + weights[1] * window[1 : inner_count + 2]
        + weights[2] * window[2 : inner_count + 3]
    )
    return window[2 : inner_count + 2] - (fluxes[1:] - fluxes[:-1])


def positive(field):
    return 0.5 * (field + jnp.sqrt(field * field + 1.0))


def level_table(levels, species):
    channel_level = jnp.arange(levels * species, dtype=jnp.int32) // species
    return (channel_level[:, None] == jnp.arange(levels, dtype=jnp.int32)[None, :]).astype(
        jnp.float32
    )


def partition(total_mass, seed_aerosol, volatility):
    levels = seed_aerosol.shape[-1]
    species = volatility.shape[0]
    grouping = level_table(levels, species)
    saturation = jnp.tile(volatility, levels)
    aerosol = seed_aerosol
    for newton_step in range(NEWTON):
        denominator = spread(aerosol, species) + saturation
        fraction = total_mass / denominator
        first_sum = jnp.dot(fraction, grouping, precision=lax.Precision.HIGHEST)
        second_sum = jnp.dot(fraction / denominator, grouping, precision=lax.Precision.HIGHEST)
        residue = 1.0 - seed_aerosol / aerosol - first_sum
        derivative = seed_aerosol / (aerosol * aerosol) + second_sum
        aerosol = aerosol - residue / derivative
    aerosol_q = spread(aerosol, species)
    return total_mass * aerosol_q / (aerosol_q + saturation)


def east_west(field):
    return with_halo(field, (("lon", 1),), 2, True)


def north_south(field):
    return with_halo(field, (("lat", 0),), 2, False)


def fold_rows(gradient):
    inner_rows = gradient.shape[0] - 4
    rim_cells = jnp.concatenate([gradient[:2], gradient[inner_rows + 2 :]], axis=0)
    arrived = north_south(rim_cells)
    middle = gradient[2 : inner_rows + 2]
    return jnp.concatenate(
        [
            middle[:2] + arrived[:2],
            middle[2 : inner_rows - 2],
            middle[inner_rows - 2 :] + arrived[6:],
        ],
        axis=0,
    )


def fold_columns(gradient):
    inner_cols = gradient.shape[1] - 4
    rim_cells = jnp.concatenate([gradient[:, :2], gradient[:, inner_cols + 2 :]], axis=1)
    arrived = east_west(rim_cells)
    middle = gradient[:, 2 : inner_cols + 2]
    return jnp.concatenate(
        [
            middle[:, :2] + arrived[:, :2],
            middle[:, 2 : inner_cols - 2],
            middle[:, inner_cols - 2 :] + arrived[:, 6:],
        ],
        axis=1,
    )


def wave_table(column_count, length):
    position = jnp.arange(column_count, dtype=jnp.int32)
    numbers = jnp.arange(KMAX, dtype=jnp.int32)
    phases = position[:, None] * numbers[None, :] % length
    angles = phases.astype(jnp.float32) * (2.0 * math.pi / length)
    return jnp.concatenate([jnp.cos(angles), jnp.sin(angles)], axis=1)


def wave_weights(keep_values, length):
    numbers = jnp.arange(2 * KMAX, dtype=jnp.int32) % KMAX
    scaling = jnp.where(numbers == 0, 1.0, 2.0) / length
    kept_mask = numbers[None, :] < keep_values[:, None]
    return jnp.where(kept_mask, scaling[None, :], 0.0)


def lowpass_circles(circles, keep_values):
    length = circles.shape[2]
    table_full = wave_table(length, length)
    coefficient = jnp.einsum("rqn,nk->rqk", circles, table_full, precision=lax.Precision.HIGHEST)
    coefficient = coefficient * wave_weights(keep_values, length)[:, None, :]
    lowpass = jnp.einsum("rqk,nk->rqn", coefficient, table_full, precision=lax.Precision.HIGHEST)
    return jnp.where((keep_values <= KMAX)[:, None, None], lowpass, circles)


def split_three(values):
    high = values.astype(jnp.bfloat16)
    rest = values - high.astype(jnp.float32)
    middle = rest.astype(jnp.bfloat16)
    low = (rest - middle.astype(jnp.float32)).astype(jnp.bfloat16)
    return high, middle, low


def select_dot(values, selector, dims):
    total = None
    for piece in split_three(values):
        term = lax.dot_general(piece, selector, dims, preferred_element_type=jnp.float32)
        total = term if total is None else total + term
    return total


def select_dot_left(selector, values, dims):
    total = None
    for piece in split_three(values):
        term = lax.dot_general(selector, piece, dims, preferred_element_type=jnp.float32)
        total = term if total is None else total + term
    return total


def polar_kernel(x_ref, w_ref, t_ref, y_ref, out_go, land_go, out_back, land_back,
                 sem_a, sem_b, sem_c, sem_d):
    count = t_ref.shape[0]
    polar_count, col_count, channels = x_ref.shape
    chunk = channels // count
    padded = out_go.shape[1]
    me = lax.axis_index("lon")
    band = lax.axis_index("lat")
    bands = lax.axis_size("lat")
    active = jnp.logical_or(band == 0, band == bands - 1)
    hi = lax.Precision.HIGHEST
    mesh_id = pl.DeviceIdType.MESH

    def remote(src, dst, send_sem, recv_sem, peer):
        return pltpu.make_async_remote_copy(
            src_ref=src, dst_ref=dst, send_sem=send_sem, recv_sem=recv_sem,
            device_id=(band, peer), device_id_type=mesh_id,
        )

    def round_trip(outbox, inbox, send_sems, recv_sems):
        for offset in range(1, count):
            peer = lax.rem(me + offset, count)
            remote(outbox.at[peer], inbox.at[me], send_sems.at[offset], recv_sems.at[me], peer).start()
        inbox[pl.ds(me, 1)] = outbox[pl.ds(me, 1)]
        for offset in range(1, count):
            peer = lax.rem(me + offset, count)
            remote(outbox.at[peer], inbox.at[me], send_sems.at[offset], recv_sems.at[me], peer).wait_send()
        for offset in range(1, count):
            peer = lax.rem(me + count - offset, count)
            remote(outbox.at[peer], inbox.at[peer], send_sems.at[offset], recv_sems.at[peer], peer).wait_recv()

    @pl.when(active)
    def _():
        barrier = pltpu.get_barrier_semaphore()
        for offset in range(1, count):
            peer = lax.rem(me + offset, count)
            pl.semaphore_signal(barrier, 1, device_id=(band, peer), device_id_type=mesh_id)
        pl.semaphore_wait(barrier, count - 1)
        rows = jnp.concatenate([x_ref[r] for r in range(polar_count)], axis=0)
        slot = lax.broadcasted_iota(jnp.int32, (count * padded, channels), 0)
        channel = lax.broadcasted_iota(jnp.int32, (count * padded, channels), 1)
        target = (channel // chunk) * padded + channel % chunk
        packer = jnp.where(slot == target, 1.0, 0.0).astype(jnp.bfloat16)
        packed = select_dot_left(packer, rows, (((1,), (1,)), ((), ())))
        out_go[...] = packed.reshape(count, padded, polar_count * col_count)
        round_trip(out_go, land_go, sem_a, sem_b)

        def analyse(s, acc):
            return acc + jnp.dot(land_go[s], t_ref[s], precision=hi,
                                 preferred_element_type=jnp.float32)

        coefficient = lax.fori_loop(
            0, count, analyse, jnp.zeros((padded, t_ref.shape[2]), jnp.float32)
        )
        coefficient = coefficient * w_ref[...]

        def synthesise(s, carry):
            out_back[s] = lax.dot_general(coefficient, t_ref[s], (((1,), (1,)), ((), ())),
                                          precision=hi, preferred_element_type=jnp.float32)
            return carry

        lax.fori_loop(0, count, synthesise, 0)
        round_trip(out_back, land_back, sem_c, sem_d)
        back = land_back[...].reshape(count * padded, polar_count * col_count)
        result = select_dot(back, packer, (((0,), (0,)), ((), ())))
        for r in range(polar_count):
            y_ref[r] = result[r * col_count : (r + 1) * col_count]

    @pl.when(jnp.logical_not(active))
    def _():
        y_ref[...] = x_ref[...]


def polar_lowpass(end_rows, weights, blocks, call_id):
    polar_count, col_count, channels = end_rows.shape
    count = blocks.shape[0]
    padded = -(-(channels // count) // 8) * 8
    slab = (count, padded, polar_count * col_count)
    vmem = pl.BlockSpec(memory_space=pltpu.VMEM)
    return pl.pallas_call(
        polar_kernel,
        out_shape=jax.ShapeDtypeStruct(end_rows.shape, end_rows.dtype),
        in_specs=[vmem, vmem, vmem],
        out_specs=vmem,
        scratch_shapes=[
            pltpu.VMEM(slab, jnp.float32),
            pltpu.VMEM(slab, jnp.float32),
            pltpu.VMEM(slab, jnp.float32),
            pltpu.VMEM(slab, jnp.float32),
            pltpu.SemaphoreType.DMA((count,)),
            pltpu.SemaphoreType.DMA((count,)),
            pltpu.SemaphoreType.DMA((count,)),
            pltpu.SemaphoreType.DMA((count,)),
        ],
        compiler_params=pltpu.CompilerParams(collective_id=call_id, has_side_effects=True),
    )(end_rows, weights, blocks)


def column_chemistry(x, seed, cot, sat, valid):
    root = jnp.sqrt(x * x + 1.0)
    mass = jnp.where(valid, 0.5 * (x + root), 0.0)
    cot = jnp.where(valid, cot, 0.0)
    aerosol = seed
    history = []
    for newton_step in range(NEWTON):
        denominator = aerosol + sat
        fraction = mass / denominator
        first_sum = jnp.sum(fraction, axis=-2, keepdims=True)
        second_sum = jnp.sum(fraction / denominator, axis=-2, keepdims=True)
        residue = 1.0 - seed / aerosol - first_sum
        derivative = seed / (aerosol * aerosol) + second_sum
        history.append((aerosol, residue, derivative))
        aerosol = aerosol - residue / derivative
    final_den = aerosol + sat
    particle = mass * aerosol / final_den
    mass_bar = cot * aerosol / final_den
    aerosol_bar = jnp.sum(cot * mass * sat / (final_den * final_den), axis=-2, keepdims=True)
    for newton_step in reversed(range(NEWTON)):
        a_n, residue, derivative = history[newton_step]
        inverse = 1.0 / (a_n + sat)
        third_sum = jnp.sum(mass * inverse * inverse * inverse, axis=-2, keepdims=True)
        slope = -2.0 * (seed / (a_n * a_n * a_n) + third_sum)
        over_g = aerosol_bar / derivative
        over_g2 = over_g * residue / derivative
        mass_bar = mass_bar + over_g * inverse + over_g2 * inverse * inverse
        aerosol_bar = over_g2 * slope
    gradient = mass_bar * 0.5 * (1.0 + x / root)
    return jnp.where(valid, particle, 0.0), jnp.where(valid, gradient, 0.0)


def owner_kernel(x_ref, c_ref, s_ref, w_ref, m_ref, v_ref, t_ref, p_ref, g_ref,
                 out_go, land_go, out_back, land_back, field_s, sem_a, sem_b, sem_c, sem_d):
    count = t_ref.shape[0]
    polar_count, col_count, channels = x_ref.shape
    levels = s_ref.shape[2]
    chunk = channels // count
    padded = out_go.shape[1] // 2
    me = lax.axis_index("lon")
    band = lax.axis_index("lat")
    bands = lax.axis_size("lat")
    active = jnp.logical_or(band == 0, band == bands - 1)
    hi = lax.Precision.HIGHEST
    mesh_id = pl.DeviceIdType.MESH
    nt = (((1,), (1,)), ((), ()))

    def remote(src, dst, send_sem, recv_sem, peer):
        return pltpu.make_async_remote_copy(
            src_ref=src, dst_ref=dst, send_sem=send_sem, recv_sem=recv_sem,
            device_id=(band, peer), device_id_type=mesh_id,
        )

    def round_trip(outbox, inbox, send_sems, recv_sems):
        for offset in range(1, count):
            peer = lax.rem(me + offset, count)
            remote(outbox.at[peer], inbox.at[me], send_sems.at[offset], recv_sems.at[me], peer).start()
        inbox[pl.ds(me, 1)] = outbox[pl.ds(me, 1)]
        for offset in range(1, count):
            peer = lax.rem(me + offset, count)
            remote(outbox.at[peer], inbox.at[me], send_sems.at[offset], recv_sems.at[me], peer).wait_send()
        for offset in range(1, count):
            peer = lax.rem(me + count - offset, count)
            remote(outbox.at[peer], inbox.at[peer], send_sems.at[offset], recv_sems.at[peer], peer).wait_recv()

    @pl.when(active)
    def _():
        barrier = pltpu.get_barrier_semaphore()
        for offset in range(1, count):
            peer = lax.rem(me + offset, count)
            pl.semaphore_signal(barrier, 1, device_id=(band, peer), device_id_type=mesh_id)
        pl.semaphore_wait(barrier, count - 1)
        wide = channels + levels
        slot = lax.broadcasted_iota(jnp.int32, (count * padded, wide), 0)
        channel = lax.broadcasted_iota(jnp.int32, (count * padded, wide), 1)
        target = jnp.where(
            channel < channels,
            (channel // chunk) * padded + channel % chunk,
            (channel - channels) * padded + chunk,
        )
        packer_wide = jnp.where(slot == target, 1.0, 0.0).astype(jnp.bfloat16)
        packer = packer_wide[:, :channels]
        rows = jnp.concatenate(
            [jnp.concatenate([x_ref[r], s_ref[r]], axis=1) for r in range(polar_count)], axis=0
        )
        cots = jnp.concatenate([c_ref[r] for r in range(polar_count)], axis=0)
        lanes = polar_count * col_count
        out_go[:, 0:padded, :] = select_dot_left(packer_wide, rows, nt).reshape(count, padded, lanes)
        out_go[:, padded:, :] = select_dot_left(packer, cots, nt).reshape(count, padded, lanes)
        round_trip(out_go, land_go, sem_a, sem_b)

        def analyse(s, acc):
            return acc + jnp.dot(land_go[s, 0:padded, :], t_ref[s], precision=hi,
                                 preferred_element_type=jnp.float32)

        zero = jnp.zeros((padded, t_ref.shape[2]), jnp.float32)
        coefficient = lax.fori_loop(0, count, analyse, zero, unroll=8) * w_ref[...]
        keep_lane = m_ref[...] > 0.5
        species_row = lax.broadcasted_iota(jnp.int32, (padded, lanes), 0)
        valid = species_row < chunk
        sat = v_ref[...]

        def smooth_out(s, carry):
            smooth = lax.dot_general(coefficient, t_ref[s], nt, precision=hi,
                                     preferred_element_type=jnp.float32)
            field_s[s] = jnp.where(keep_lane, smooth, land_go[s, 0:padded, :])
            return carry

        lax.fori_loop(0, count, smooth_out, 0, unroll=8)
        particle, gradient = column_chemistry(
            field_s[...],
            land_go[:, chunk : chunk + 1, :],
            land_go[:, padded:, :],
            sat[None],
            valid[None],
        )
        out_back[:, 0:padded, :] = particle
        field_s[...] = gradient

        def gather_adjoint(s, acc):
            return acc + jnp.dot(field_s[s], t_ref[s], precision=hi,
                                 preferred_element_type=jnp.float32)

        adjoint_coef = lax.fori_loop(0, count, gather_adjoint, zero, unroll=8) * w_ref[...]

        def synthesise(s, carry):
            smooth = lax.dot_general(adjoint_coef, t_ref[s], nt, precision=hi,
                                     preferred_element_type=jnp.float32)
            out_back[s, padded:, :] = jnp.where(keep_lane, smooth, field_s[s])
            return carry

        lax.fori_loop(0, count, synthesise, 0, unroll=8)
        round_trip(out_back, land_back, sem_c, sem_d)
        particle_back = land_back[:, 0:padded, :].reshape(count * padded, lanes)
        gradient_back = land_back[:, padded:, :].reshape(count * padded, lanes)
        particle_rows = select_dot(particle_back, packer, (((0,), (0,)), ((), ())))
        gradient_rows = select_dot(gradient_back, packer, (((0,), (0,)), ((), ())))
        for r in range(polar_count):
            p_ref[r] = particle_rows[r * col_count : (r + 1) * col_count]
            g_ref[r] = gradient_rows[r * col_count : (r + 1) * col_count]

    @pl.when(jnp.logical_not(active))
    def _():
        p_ref[...] = jnp.zeros_like(p_ref)
        g_ref[...] = jnp.zeros_like(g_ref)


def polar_step(field, seed_aerosol, volatility, cotangent, filter_keep, particle, gradient):
    row_count, col_count, channels = field.shape
    count = lax.axis_size("lon")
    length = col_count * count
    species = volatility.shape[0]
    polar_count = POLAR
    band = lax.axis_index("lat")
    at_north_end = band == 0
    at_south_end = band == lax.axis_size("lat") - 1

    def ends(values):
        return jnp.where(at_north_end, values[:polar_count], values[row_count - polar_count :])

    end_keep = ends(filter_keep)
    table = wave_table(length, length).reshape(count, col_count, 2 * KMAX)
    blocks = jnp.einsum(
        "sjk,rR->srjRk", table, jnp.eye(polar_count, dtype=jnp.float32)
    ).reshape(count, polar_count * col_count, polar_count * 2 * KMAX)
    weights = wave_weights(end_keep, length).reshape(1, polar_count * 2 * KMAX)
    lane_mask = jnp.repeat((end_keep <= KMAX).astype(jnp.float32), col_count)[None, :]
    padded = -(-(channels // count + 1) // 8) * 8
    sat = jnp.concatenate(
        [volatility, jnp.ones((padded - species,), jnp.float32)]
    )[:, None]
    slab = (count, 2 * padded, polar_count * col_count)
    vmem = pl.BlockSpec(memory_space=pltpu.VMEM)
    end_shape = jax.ShapeDtypeStruct((polar_count, col_count, channels), jnp.float32)
    polar_particle, polar_gradient = pl.pallas_call(
        owner_kernel,
        out_shape=[end_shape, end_shape],
        in_specs=[vmem] * 7,
        out_specs=[vmem, vmem],
        scratch_shapes=[
            pltpu.VMEM(slab, jnp.float32),
            pltpu.VMEM(slab, jnp.float32),
            pltpu.VMEM(slab, jnp.float32),
            pltpu.VMEM(slab, jnp.float32),
            pltpu.VMEM((count, padded, polar_count * col_count), jnp.float32),
            pltpu.SemaphoreType.DMA((count,)),
            pltpu.SemaphoreType.DMA((count,)),
            pltpu.SemaphoreType.DMA((count,)),
            pltpu.SemaphoreType.DMA((count,)),
        ],
        compiler_params=pltpu.CompilerParams(collective_id=0, has_side_effects=True),
    )(ends(field), ends(cotangent), ends(seed_aerosol), weights, lane_mask, sat, blocks)

    def merge(values, polar):
        top = jnp.where(at_north_end, polar, values[:polar_count])
        bottom = jnp.where(at_south_end, polar, values[row_count - polar_count :])
        return jnp.concatenate(
            [top, values[polar_count : row_count - polar_count], bottom], axis=0
        )

    return merge(particle, polar_particle), merge(gradient, polar_gradient)


def filter_field(field, filter_keep, call_id):
    row_count, col_count, channels = field.shape
    count = lax.axis_size("lon")
    length = col_count * count
    polar_count = POLAR
    band = lax.axis_index("lat")
    at_north_end = band == 0
    at_south_end = band == lax.axis_size("lat") - 1
    top_rows = field[:polar_count]
    bottom_rows = field[row_count - polar_count :]
    end_rows = jnp.where(at_north_end, top_rows, bottom_rows)
    end_keep = jnp.where(
        at_north_end, filter_keep[:polar_count], filter_keep[row_count - polar_count :]
    )
    table = wave_table(length, length).reshape(count, col_count, 2 * KMAX)
    blocks = jnp.einsum(
        "sjk,rR->srjRk", table, jnp.eye(polar_count, dtype=jnp.float32)
    ).reshape(count, polar_count * col_count, polar_count * 2 * KMAX)
    weights = wave_weights(end_keep, length).reshape(1, polar_count * 2 * KMAX)
    lowpass = polar_lowpass(end_rows, weights, blocks, call_id)
    smoothed = jnp.where((end_keep <= KMAX)[:, None, None], lowpass, end_rows)
    new_top = jnp.where(at_north_end, smoothed, top_rows)
    new_bottom = jnp.where(at_south_end, smoothed, bottom_rows)
    return jnp.concatenate(
        [new_top, field[polar_count : row_count - polar_count], new_bottom], axis=0
    )


def chem_kernel(x_ref, seed_ref, cot_ref, sat_ref, spread_ref, group_ref, p_ref, g_ref):
    row = pl.program_id(0)
    rows = pl.num_programs(0)
    band = lax.axis_index("lat")
    bands = lax.axis_size("lat")
    polar = jnp.logical_or(
        jnp.logical_and(band == 0, row < POLAR),
        jnp.logical_and(band == bands - 1, row >= rows - POLAR),
    )

    @pl.when(jnp.logical_not(polar))
    def _():
        chem_body(x_ref, seed_ref, cot_ref, sat_ref, spread_ref, group_ref, p_ref, g_ref)


def chem_body(x_ref, seed_ref, cot_ref, sat_ref, spread_ref, group_ref, p_ref, g_ref):
    hi = lax.Precision.HIGHEST
    x = x_ref[0]
    seed = seed_ref[0]
    cot = cot_ref[0]
    sat = sat_ref[...]
    spread_m = spread_ref[...].astype(jnp.bfloat16)
    group_m = group_ref[...].astype(jnp.bfloat16)

    plain = (((1,), (0,)), ((), ()))

    def up(v):
        return select_dot(v, spread_m, plain)

    def down(v):
        return select_dot(v, group_m, plain)

    root = jnp.sqrt(x * x + 1.0)
    mass = 0.5 * (x + root)
    aerosol = seed
    history = []
    for newton_step in range(NEWTON):
        denominator = up(aerosol) + sat
        fraction = mass / denominator
        first_sum = down(fraction)
        second_sum = down(fraction / denominator)
        residue = 1.0 - seed / aerosol - first_sum
        derivative = seed / (aerosol * aerosol) + second_sum
        history.append((aerosol, residue, derivative))
        aerosol = aerosol - residue / derivative
    aerosol_q = up(aerosol)
    final_den = aerosol_q + sat
    p_ref[0] = mass * aerosol_q / final_den
    mass_bar = cot * aerosol_q / final_den
    aerosol_bar = down(cot * mass * sat / (final_den * final_den))
    for newton_step in reversed(range(NEWTON)):
        a_n, residue, derivative = history[newton_step]
        inverse = 1.0 / (up(a_n) + sat)
        third_sum = down(mass * inverse * inverse * inverse)
        slope = -2.0 * (seed / (a_n * a_n * a_n) + third_sum)
        over_g = aerosol_bar / derivative
        over_g2 = over_g * residue / derivative
        mass_bar = mass_bar + up(over_g) * inverse + up(over_g2) * inverse * inverse
        aerosol_bar = over_g2 * slope
    g_ref[0] = mass_bar * 0.5 * (1.0 + x / root)


def chemistry_step(filtered, seed_aerosol, volatility, cotangent):
    rows, cols, channels = filtered.shape
    levels = seed_aerosol.shape[-1]
    species = volatility.shape[0]
    group_m = level_table(levels, species)
    spread_m = group_m.T
    sat = jnp.tile(volatility, levels)[None, :]
    big = pl.BlockSpec((1, cols, channels), lambda i: (i, 0, 0))
    small = pl.BlockSpec((1, cols, levels), lambda i: (i, 0, 0))
    return pl.pallas_call(
        chem_kernel,
        grid=(rows,),
        in_specs=[
            big,
            small,
            big,
            pl.BlockSpec((1, channels), lambda i: (0, 0)),
            pl.BlockSpec((levels, channels), lambda i: (0, 0)),
            pl.BlockSpec((channels, levels), lambda i: (0, 0)),
        ],
        out_specs=[big, big],
        out_shape=[
            jax.ShapeDtypeStruct(filtered.shape, jnp.float32),
            jax.ShapeDtypeStruct(filtered.shape, jnp.float32),
        ],
    )(filtered, seed_aerosol, cotangent, sat, spread_m, group_m)


def local(
    tracer,
    east_courant,
    north_courant,
    east_limiter,
    north_limiter,
    filter_keep,
    seed_aerosol,
    volatility,
    cotangent,
):
    row_count = tracer.shape[0]
    channels = tracer.shape[2]
    levels = east_courant.shape[2]
    species = volatility.shape[0]
    first_row = lax.axis_index("lat") * row_count
    packed = jnp.concatenate([tracer, east_courant, east_limiter.astype(jnp.float32)], axis=2)
    widened = east_west(packed)
    east_speed = widened[:, :, channels : channels + levels]
    east_choice = widened[:, :, channels + levels :].astype(jnp.int32)

    def zonal_only(window):
        return zonal_window(window, east_speed, east_choice, species)

    after_east, east_back = jax.vjp(zonal_only, widened[:, :, :channels])
    stacked = jnp.concatenate(
        [after_east, north_courant, north_limiter.astype(jnp.float32)], axis=2
    )
    tall_window = north_south(stacked)
    north_speed = tall_window[:, :, channels : channels + levels]
    north_choice = tall_window[:, :, channels + levels :].astype(jnp.int32)

    def meridional_only(window):
        return meridional_window(window, north_speed, north_choice, first_row, species)

    after_north, north_back = jax.vjp(meridional_only, tall_window[:, :, :channels])
    particle, chem_grad = chemistry_step(after_north, seed_aerosol, volatility, cotangent)
    particle, adjoint_filtered = polar_step(
        after_north, seed_aerosol, volatility, cotangent, filter_keep, particle, chem_grad
    )
    return (particle, fold_columns(east_back(fold_rows(north_back(adjoint_filtered)[0]))[0]))


def solution(mesh):
    in_specs = (
        P("lat", "lon", None),
        P("lat", "lon", None),
        P("lat", "lon", None),
        P("lat", "lon", None),
        P("lat", "lon", None),
        P("lat"),
        P("lat", "lon", None),
        P(),
        P("lat", "lon", None),
    )
    out_specs = (P("lat", "lon", None), P("lat", "lon", None))
    return jax.shard_map(local, mesh=mesh, in_specs=in_specs, out_specs=out_specs, check_vma=False)
```

```python
import math

import jax
import jax.numpy as jnp
from jax import lax
from jax.sharding import PartitionSpec as P
from jax.experimental import pallas as pl
from jax.experimental.pallas import tpu as pltpu

NEWTON = 4
KMAX = 32
POLAR = 2


def with_halo(cells, sides, width, closed):
    for axis, dim in sides:
        count = lax.axis_size(axis)
        ends = count if closed else count - 1
        head = lax.slice_in_dim(cells, 0, width, axis=dim)
        tail = lax.slice_in_dim(cells, cells.shape[dim] - width, cells.shape[dim], axis=dim)
        cells = jnp.concatenate(
            [
                lax.ppermute(tail, axis, [(i, (i + 1) % count) for i in range(ends)]),
                cells,
                lax.ppermute(head, axis, [((i + 1) % count, i) for i in range(ends)]),
            ],
            axis=dim,
        )
    return cells


def spread(values, copies):
    return jnp.repeat(values, copies, axis=-1)


def face_weights(courant, limiter):
    upwind = courant >= 0.0
    half = 0.5 * courant
    inner = courant * (7.0 / 12.0)
    outer = jnp.where(limiter == 0, courant * (-1.0 / 12.0), 0.0)
    near_left = jnp.where(
        limiter == 0, inner, jnp.where(limiter == 1, jnp.where(upwind, courant, 0.0), half)
    )
    near_right = jnp.where(
        limiter == 0, inner, jnp.where(limiter == 1, jnp.where(upwind, 0.0, courant), half)
    )
    return jnp.stack([outer, near_left, near_right], axis=0)


def spread_weights(weights, species):
    levels = weights.shape[-1]
    spread_m = level_table(levels, species).T
    return jnp.einsum("...l,lq->...q", weights, spread_m, precision=lax.Precision.HIGHEST)


def zonal_window(window, courant, limiter, species):
    inner_count = window.shape[1] - 4
    weights = spread_weights(
        face_weights(courant[:, 2 : inner_count + 3], limiter[:, 2 : inner_count + 3]), species
    )
    fluxes = (
        weights[0] * (window[:, 0 : inner_count + 1] + window[:, 3 : inner_count + 4])
        + weights[1] * window[:, 1 : inner_count + 2]
        + weights[2] * window[:, 2 : inner_count + 3]
    )
    return window[:, 2 : inner_count + 2] - (fluxes[:, 1:] - fluxes[:, :-1])


def meridional_window(window, courant, limiter, first_row, species):
    inner_count = window.shape[0] - 4
    face_rows = first_row + jnp.arange(inner_count + 1, dtype=jnp.int32)
    opened = jnp.where(face_rows[:, None, None] > 0, courant[2 : inner_count + 3], 0.0)
    weights = spread_weights(face_weights(opened, limiter[2 : inner_count + 3]), species)
    fluxes = (
        weights[0] * (window[0 : inner_count + 1] + window[3 : inner_count + 4])
        + weights[1] * window[1 : inner_count + 2]
        + weights[2] * window[2 : inner_count + 3]
    )
    return window[2 : inner_count + 2] - (fluxes[1:] - fluxes[:-1])


def positive(field):
    return 0.5 * (field + jnp.sqrt(field * field + 1.0))


def level_table(levels, species):
    channel_level = jnp.arange(levels * species, dtype=jnp.int32) // species
    return (channel_level[:, None] == jnp.arange(levels, dtype=jnp.int32)[None, :]).astype(
        jnp.float32
    )


def partition(total_mass, seed_aerosol, volatility):
    levels = seed_aerosol.shape[-1]
    species = volatility.shape[0]
    grouping = level_table(levels, species)
    saturation = jnp.tile(volatility, levels)
    aerosol = seed_aerosol
    for newton_step in range(NEWTON):
        denominator = spread(aerosol, species) + saturation
        fraction = total_mass / denominator
        first_sum = jnp.dot(fraction, grouping, precision=lax.Precision.HIGHEST)
        second_sum = jnp.dot(fraction / denominator, grouping, precision=lax.Precision.HIGHEST)
        residue = 1.0 - seed_aerosol / aerosol - first_sum
        derivative = seed_aerosol / (aerosol * aerosol) + second_sum
        aerosol = aerosol - residue / derivative
    aerosol_q = spread(aerosol, species)
    return total_mass * aerosol_q / (aerosol_q + saturation)


def east_west(field):
    return with_halo(field, (("lon", 1),), 2, True)


def north_south(field):
    return with_halo(field, (("lat", 0),), 2, False)


def fold_rows(gradient):
    inner_rows = gradient.shape[0] - 4
    rim_cells = jnp.concatenate([gradient[:2], gradient[inner_rows + 2 :]], axis=0)
    arrived = north_south(rim_cells)
    middle = gradient[2 : inner_rows + 2]
    return jnp.concatenate(
        [
            middle[:2] + arrived[:2],
            middle[2 : inner_rows - 2],
            middle[inner_rows - 2 :] + arrived[6:],
        ],
        axis=0,
    )


def fold_columns(gradient):
    inner_cols = gradient.shape[1] - 4
    rim_cells = jnp.concatenate([gradient[:, :2], gradient[:, inner_cols + 2 :]], axis=1)
    arrived = east_west(rim_cells)
    middle = gradient[:, 2 : inner_cols + 2]
    return jnp.concatenate(
        [
            middle[:, :2] + arrived[:, :2],
            middle[:, 2 : inner_cols - 2],
            middle[:, inner_cols - 2 :] + arrived[:, 6:],
        ],
        axis=1,
    )


def wave_table(column_count, length):
    position = jnp.arange(column_count, dtype=jnp.int32)
    numbers = jnp.arange(KMAX, dtype=jnp.int32)
    phases = position[:, None] * numbers[None, :] % length
    angles = phases.astype(jnp.float32) * (2.0 * math.pi / length)
    return jnp.concatenate([jnp.cos(angles), jnp.sin(angles)], axis=1)


def wave_weights(keep_values, length):
    numbers = jnp.arange(2 * KMAX, dtype=jnp.int32) % KMAX
    scaling = jnp.where(numbers == 0, 1.0, 2.0) / length
    kept_mask = numbers[None, :] < keep_values[:, None]
    return jnp.where(kept_mask, scaling[None, :], 0.0)


def lowpass_circles(circles, keep_values):
    length = circles.shape[2]
    table_full = wave_table(length, length)
    coefficient = jnp.einsum("rqn,nk->rqk", circles, table_full, precision=lax.Precision.HIGHEST)
    coefficient = coefficient * wave_weights(keep_values, length)[:, None, :]
    lowpass = jnp.einsum("rqk,nk->rqn", coefficient, table_full, precision=lax.Precision.HIGHEST)
    return jnp.where((keep_values <= KMAX)[:, None, None], lowpass, circles)


def split_three(values):
    high = values.astype(jnp.bfloat16)
    rest = values - high.astype(jnp.float32)
    middle = rest.astype(jnp.bfloat16)
    low = (rest - middle.astype(jnp.float32)).astype(jnp.bfloat16)
    return high, middle, low


def select_dot(values, selector, dims):
    total = None
    for piece in split_three(values):
        term = lax.dot_general(piece, selector, dims, preferred_element_type=jnp.float32)
        total = term if total is None else total + term
    return total


def select_dot_left(selector, values, dims):
    total = None
    for piece in split_three(values):
        term = lax.dot_general(selector, piece, dims, preferred_element_type=jnp.float32)
        total = term if total is None else total + term
    return total


def polar_kernel(x_ref, w_ref, t_ref, y_ref, out_go, land_go, out_back, land_back,
                 sem_a, sem_b, sem_c, sem_d):
    count = t_ref.shape[0]
    polar_count, col_count, channels = x_ref.shape
    chunk = channels // count
    padded = out_go.shape[1]
    me = lax.axis_index("lon")
    band = lax.axis_index("lat")
    bands = lax.axis_size("lat")
    active = jnp.logical_or(band == 0, band == bands - 1)
    hi = lax.Precision.HIGHEST
    mesh_id = pl.DeviceIdType.MESH

    def remote(src, dst, send_sem, recv_sem, peer):
        return pltpu.make_async_remote_copy(
            src_ref=src, dst_ref=dst, send_sem=send_sem, recv_sem=recv_sem,
            device_id=(band, peer), device_id_type=mesh_id,
        )

    def round_trip(outbox, inbox, send_sems, recv_sems):
        for offset in range(1, count):
            peer = lax.rem(me + offset, count)
            remote(outbox.at[peer], inbox.at[me], send_sems.at[offset], recv_sems.at[me], peer).start()
        inbox[pl.ds(me, 1)] = outbox[pl.ds(me, 1)]
        for offset in range(1, count):
            peer = lax.rem(me + offset, count)
            remote(outbox.at[peer], inbox.at[me], send_sems.at[offset], recv_sems.at[me], peer).wait_send()
        for offset in range(1, count):
            peer = lax.rem(me + count - offset, count)
            remote(outbox.at[peer], inbox.at[peer], send_sems.at[offset], recv_sems.at[peer], peer).wait_recv()

    @pl.when(active)
    def _():
        barrier = pltpu.get_barrier_semaphore()
        for offset in range(1, count):
            peer = lax.rem(me + offset, count)
            pl.semaphore_signal(barrier, 1, device_id=(band, peer), device_id_type=mesh_id)
        pl.semaphore_wait(barrier, count - 1)
        rows = jnp.concatenate([x_ref[r] for r in range(polar_count)], axis=0)
        slot = lax.broadcasted_iota(jnp.int32, (count * padded, channels), 0)
        channel = lax.broadcasted_iota(jnp.int32, (count * padded, channels), 1)
        target = (channel // chunk) * padded + channel % chunk
        packer = jnp.where(slot == target, 1.0, 0.0).astype(jnp.bfloat16)
        packed = select_dot_left(packer, rows, (((1,), (1,)), ((), ())))
        out_go[...] = packed.reshape(count, padded, polar_count * col_count)
        round_trip(out_go, land_go, sem_a, sem_b)

        def analyse(s, acc):
            return acc + jnp.dot(land_go[s], t_ref[s], precision=hi,
                                 preferred_element_type=jnp.float32)

        coefficient = lax.fori_loop(
            0, count, analyse, jnp.zeros((padded, t_ref.shape[2]), jnp.float32)
        )
        coefficient = coefficient * w_ref[...]

        def synthesise(s, carry):
            out_back[s] = lax.dot_general(coefficient, t_ref[s], (((1,), (1,)), ((), ())),
                                          precision=hi, preferred_element_type=jnp.float32)
            return carry

        lax.fori_loop(0, count, synthesise, 0)
        round_trip(out_back, land_back, sem_c, sem_d)
        back = land_back[...].reshape(count * padded, polar_count * col_count)
        result = select_dot(back, packer, (((0,), (0,)), ((), ())))
        for r in range(polar_count):
            y_ref[r] = result[r * col_count : (r + 1) * col_count]

    @pl.when(jnp.logical_not(active))
    def _():
        y_ref[...] = x_ref[...]


def polar_lowpass(end_rows, weights, blocks, call_id):
    polar_count, col_count, channels = end_rows.shape
    count = blocks.shape[0]
    padded = -(-(channels // count) // 8) * 8
    slab = (count, padded, polar_count * col_count)
    vmem = pl.BlockSpec(memory_space=pltpu.VMEM)
    return pl.pallas_call(
        polar_kernel,
        out_shape=jax.ShapeDtypeStruct(end_rows.shape, end_rows.dtype),
        in_specs=[vmem, vmem, vmem],
        out_specs=vmem,
        scratch_shapes=[
            pltpu.VMEM(slab, jnp.float32),
            pltpu.VMEM(slab, jnp.float32),
            pltpu.VMEM(slab, jnp.float32),
            pltpu.VMEM(slab, jnp.float32),
            pltpu.SemaphoreType.DMA((count,)),
            pltpu.SemaphoreType.DMA((count,)),
            pltpu.SemaphoreType.DMA((count,)),
            pltpu.SemaphoreType.DMA((count,)),
        ],
        compiler_params=pltpu.CompilerParams(collective_id=call_id, has_side_effects=True),
    )(end_rows, weights, blocks)


def column_chemistry(x, seed, cot, sat, valid):
    root = jnp.sqrt(x * x + 1.0)
    mass = jnp.where(valid, 0.5 * (x + root), 0.0)
    cot = jnp.where(valid, cot, 0.0)
    aerosol = seed
    history = []
    for newton_step in range(NEWTON):
        denominator = aerosol + sat
        fraction = mass / denominator
        first_sum = jnp.sum(fraction, axis=-2, keepdims=True)
        second_sum = jnp.sum(fraction / denominator, axis=-2, keepdims=True)
        residue = 1.0 - seed / aerosol - first_sum
        derivative = seed / (aerosol * aerosol) + second_sum
        history.append((aerosol, residue, derivative))
        aerosol = aerosol - residue / derivative
    final_den = aerosol + sat
    particle = mass * aerosol / final_den
    mass_bar = cot * aerosol / final_den
    aerosol_bar = jnp.sum(cot * mass * sat / (final_den * final_den), axis=-2, keepdims=True)
    for newton_step in reversed(range(NEWTON)):
        a_n, residue, derivative = history[newton_step]
        inverse = 1.0 / (a_n + sat)
        third_sum = jnp.sum(mass * inverse * inverse * inverse, axis=-2, keepdims=True)
        slope = -2.0 * (seed / (a_n * a_n * a_n) + third_sum)
        over_g = aerosol_bar / derivative
        over_g2 = over_g * residue / derivative
        mass_bar = mass_bar + over_g * inverse + over_g2 * inverse * inverse
        aerosol_bar = over_g2 * slope
    gradient = mass_bar * 0.5 * (1.0 + x / root)
    return jnp.where(valid, particle, 0.0), jnp.where(valid, gradient, 0.0)


def owner_kernel(x_ref, c_ref, s_ref, w_ref, m_ref, v_ref, t_ref, p_ref, g_ref,
                 out_go, land_go, out_back, land_back, field_s, sem_a, sem_b, sem_c, sem_d):
    count = t_ref.shape[0]
    polar_count, col_count, channels = x_ref.shape
    levels = s_ref.shape[2]
    chunk = channels // count
    padded = out_go.shape[1] // 2
    me = lax.axis_index("lon")
    band = lax.axis_index("lat")
    bands = lax.axis_size("lat")
    active = jnp.logical_or(band == 0, band == bands - 1)
    hi = lax.Precision.HIGHEST
    mesh_id = pl.DeviceIdType.MESH
    nt = (((1,), (1,)), ((), ()))

    def remote(src, dst, send_sem, recv_sem, peer):
        return pltpu.make_async_remote_copy(
            src_ref=src, dst_ref=dst, send_sem=send_sem, recv_sem=recv_sem,
            device_id=(band, peer), device_id_type=mesh_id,
        )

    def round_trip(outbox, inbox, send_sems, recv_sems):
        for offset in range(1, count):
            peer = lax.rem(me + offset, count)
            remote(outbox.at[peer], inbox.at[me], send_sems.at[offset], recv_sems.at[me], peer).start()
        inbox[pl.ds(me, 1)] = outbox[pl.ds(me, 1)]
        for offset in range(1, count):
            peer = lax.rem(me + offset, count)
            remote(outbox.at[peer], inbox.at[me], send_sems.at[offset], recv_sems.at[me], peer).wait_send()
        for offset in range(1, count):
            peer = lax.rem(me + count - offset, count)
            remote(outbox.at[peer], inbox.at[peer], send_sems.at[offset], recv_sems.at[peer], peer).wait_recv()

    @pl.when(active)
    def _():
        barrier = pltpu.get_barrier_semaphore()
        for offset in range(1, count):
            peer = lax.rem(me + offset, count)
            pl.semaphore_signal(barrier, 1, device_id=(band, peer), device_id_type=mesh_id)
        pl.semaphore_wait(barrier, count - 1)
        wide = channels + levels
        slot = lax.broadcasted_iota(jnp.int32, (count * padded, wide), 0)
        channel = lax.broadcasted_iota(jnp.int32, (count * padded, wide), 1)
        target = jnp.where(
            channel < channels,
            (channel // chunk) * padded + channel % chunk,
            (channel - channels) * padded + chunk,
        )
        packer_wide = jnp.where(slot == target, 1.0, 0.0).astype(jnp.bfloat16)
        packer = packer_wide[:, :channels]
        rows = jnp.concatenate(
            [jnp.concatenate([x_ref[r], s_ref[r]], axis=1) for r in range(polar_count)], axis=0
        )
        cots = jnp.concatenate([c_ref[r] for r in range(polar_count)], axis=0)
        lanes = polar_count * col_count
        out_go[:, 0:padded, :] = select_dot_left(packer_wide, rows, nt).reshape(count, padded, lanes)
        out_go[:, padded:, :] = select_dot_left(packer, cots, nt).reshape(count, padded, lanes)
        round_trip(out_go, land_go, sem_a, sem_b)

        def analyse(s, acc):
            return acc + jnp.dot(land_go[s, 0:padded, :], t_ref[s], precision=hi,
                                 preferred_element_type=jnp.float32)

        zero = jnp.zeros((padded, t_ref.shape[2]), jnp.float32)
        coefficient = lax.fori_loop(0, count, analyse, zero, unroll=True) * w_ref[...]
        keep_lane = m_ref[...] > 0.5
        species_row = lax.broadcasted_iota(jnp.int32, (padded, lanes), 0)
        valid = species_row < chunk
        sat = v_ref[...]

        def smooth_out(s, carry):
            smooth = lax.dot_general(coefficient, t_ref[s], nt, precision=hi,
                                     preferred_element_type=jnp.float32)
            field_s[s] = jnp.where(keep_lane, smooth, land_go[s, 0:padded, :])
            return carry

        lax.fori_loop(0, count, smooth_out, 0, unroll=True)
        particle, gradient = column_chemistry(
            field_s[...],
            land_go[:, chunk : chunk + 1, :],
            land_go[:, padded:, :],
            sat[None],
            valid[None],
        )
        out_back[:, 0:padded, :] = particle
        field_s[...] = gradient

        def gather_adjoint(s, acc):
            return acc + jnp.dot(field_s[s], t_ref[s], precision=hi,
                                 preferred_element_type=jnp.float32)

        adjoint_coef = lax.fori_loop(0, count, gather_adjoint, zero, unroll=True) * w_ref[...]

        def synthesise(s, carry):
            smooth = lax.dot_general(adjoint_coef, t_ref[s], nt, precision=hi,
                                     preferred_element_type=jnp.float32)
            out_back[s, padded:, :] = jnp.where(keep_lane, smooth, field_s[s])
            return carry

        lax.fori_loop(0, count, synthesise, 0, unroll=True)
        round_trip(out_back, land_back, sem_c, sem_d)
        particle_back = land_back[:, 0:padded, :].reshape(count * padded, lanes)
        gradient_back = land_back[:, padded:, :].reshape(count * padded, lanes)
        particle_rows = select_dot(particle_back, packer, (((0,), (0,)), ((), ())))
        gradient_rows = select_dot(gradient_back, packer, (((0,), (0,)), ((), ())))
        for r in range(polar_count):
            p_ref[r] = particle_rows[r * col_count : (r + 1) * col_count]
            g_ref[r] = gradient_rows[r * col_count : (r + 1) * col_count]

    @pl.when(jnp.logical_not(active))
    def _():
        p_ref[...] = jnp.zeros_like(p_ref)
        g_ref[...] = jnp.zeros_like(g_ref)


def polar_step(field, seed_aerosol, volatility, cotangent, filter_keep, particle, gradient):
    row_count, col_count, channels = field.shape
    count = lax.axis_size("lon")
    length = col_count * count
    species = volatility.shape[0]
    polar_count = POLAR
    band = lax.axis_index("lat")
    at_north_end = band == 0
    at_south_end = band == lax.axis_size("lat") - 1

    def ends(values):
        return jnp.where(at_north_end, values[:polar_count], values[row_count - polar_count :])

    end_keep = ends(filter_keep)
    table = wave_table(length, length).reshape(count, col_count, 2 * KMAX)
    blocks = jnp.einsum(
        "sjk,rR->srjRk", table, jnp.eye(polar_count, dtype=jnp.float32)
    ).reshape(count, polar_count * col_count, polar_count * 2 * KMAX)
    weights = wave_weights(end_keep, length).reshape(1, polar_count * 2 * KMAX)
    lane_mask = jnp.repeat((end_keep <= KMAX).astype(jnp.float32), col_count)[None, :]
    padded = -(-(channels // count + 1) // 8) * 8
    sat = jnp.concatenate(
        [volatility, jnp.ones((padded - species,), jnp.float32)]
    )[:, None]
    slab = (count, 2 * padded, polar_count * col_count)
    vmem = pl.BlockSpec(memory_space=pltpu.VMEM)
    end_shape = jax.ShapeDtypeStruct((polar_count, col_count, channels), jnp.float32)
    polar_particle, polar_gradient = pl.pallas_call(
        owner_kernel,
        out_shape=[end_shape, end_shape],
        in_specs=[vmem] * 7,
        out_specs=[vmem, vmem],
        scratch_shapes=[
            pltpu.VMEM(slab, jnp.float32),
            pltpu.VMEM(slab, jnp.float32),
            pltpu.VMEM(slab, jnp.float32),
            pltpu.VMEM(slab, jnp.float32),
            pltpu.VMEM((count, padded, polar_count * col_count), jnp.float32),
            pltpu.SemaphoreType.DMA((count,)),
            pltpu.SemaphoreType.DMA((count,)),
            pltpu.SemaphoreType.DMA((count,)),
            pltpu.SemaphoreType.DMA((count,)),
        ],
        compiler_params=pltpu.CompilerParams(collective_id=0, has_side_effects=True),
    )(ends(field), ends(cotangent), ends(seed_aerosol), weights, lane_mask, sat, blocks)

    def merge(values, polar):
        top = jnp.where(at_north_end, polar, values[:polar_count])
        bottom = jnp.where(at_south_end, polar, values[row_count - polar_count :])
        return jnp.concatenate(
            [top, values[polar_count : row_count - polar_count], bottom], axis=0
        )

    return merge(particle, polar_particle), merge(gradient, polar_gradient)


def filter_field(field, filter_keep, call_id):
    row_count, col_count, channels = field.shape
    count = lax.axis_size("lon")
    length = col_count * count
    polar_count = POLAR
    band = lax.axis_index("lat")
    at_north_end = band == 0
    at_south_end = band == lax.axis_size("lat") - 1
    top_rows = field[:polar_count]
    bottom_rows = field[row_count - polar_count :]
    end_rows = jnp.where(at_north_end, top_rows, bottom_rows)
    end_keep = jnp.where(
        at_north_end, filter_keep[:polar_count], filter_keep[row_count - polar_count :]
    )
    table = wave_table(length, length).reshape(count, col_count, 2 * KMAX)
    blocks = jnp.einsum(
        "sjk,rR->srjRk", table, jnp.eye(polar_count, dtype=jnp.float32)
    ).reshape(count, polar_count * col_count, polar_count * 2 * KMAX)
    weights = wave_weights(end_keep, length).reshape(1, polar_count * 2 * KMAX)
    lowpass = polar_lowpass(end_rows, weights, blocks, call_id)
    smoothed = jnp.where((end_keep <= KMAX)[:, None, None], lowpass, end_rows)
    new_top = jnp.where(at_north_end, smoothed, top_rows)
    new_bottom = jnp.where(at_south_end, smoothed, bottom_rows)
    return jnp.concatenate(
        [new_top, field[polar_count : row_count - polar_count], new_bottom], axis=0
    )


def chem_kernel(x_ref, seed_ref, cot_ref, sat_ref, spread_ref, group_ref, p_ref, g_ref):
    row = pl.program_id(0)
    rows = pl.num_programs(0)
    band = lax.axis_index("lat")
    bands = lax.axis_size("lat")
    polar = jnp.logical_or(
        jnp.logical_and(band == 0, row < POLAR),
        jnp.logical_and(band == bands - 1, row >= rows - POLAR),
    )

    @pl.when(jnp.logical_not(polar))
    def _():
        chem_body(x_ref, seed_ref, cot_ref, sat_ref, spread_ref, group_ref, p_ref, g_ref)


def chem_body(x_ref, seed_ref, cot_ref, sat_ref, spread_ref, group_ref, p_ref, g_ref):
    hi = lax.Precision.HIGHEST
    x = x_ref[0]
    seed = seed_ref[0]
    cot = cot_ref[0]
    sat = sat_ref[...]
    spread_m = spread_ref[...].astype(jnp.bfloat16)
    group_m = group_ref[...].astype(jnp.bfloat16)

    plain = (((1,), (0,)), ((), ()))

    def up(v):
        return select_dot(v, spread_m, plain)

    def down(v):
        return select_dot(v, group_m, plain)

    root = jnp.sqrt(x * x + 1.0)
    mass = 0.5 * (x + root)
    aerosol = seed
    history = []
    for newton_step in range(NEWTON):
        denominator = up(aerosol) + sat
        fraction = mass / denominator
        first_sum = down(fraction)
        second_sum = down(fraction / denominator)
        residue = 1.0 - seed / aerosol - first_sum
        derivative = seed / (aerosol * aerosol) + second_sum
        history.append((aerosol, residue, derivative))
        aerosol = aerosol - residue / derivative
    aerosol_q = up(aerosol)
    final_den = aerosol_q + sat
    p_ref[0] = mass * aerosol_q / final_den
    mass_bar = cot * aerosol_q / final_den
    aerosol_bar = down(cot * mass * sat / (final_den * final_den))
    for newton_step in reversed(range(NEWTON)):
        a_n, residue, derivative = history[newton_step]
        inverse = 1.0 / (up(a_n) + sat)
        third_sum = down(mass * inverse * inverse * inverse)
        slope = -2.0 * (seed / (a_n * a_n * a_n) + third_sum)
        over_g = aerosol_bar / derivative
        over_g2 = over_g * residue / derivative
        mass_bar = mass_bar + up(over_g) * inverse + up(over_g2) * inverse * inverse
        aerosol_bar = over_g2 * slope
    g_ref[0] = mass_bar * 0.5 * (1.0 + x / root)


def chemistry_step(filtered, seed_aerosol, volatility, cotangent):
    rows, cols, channels = filtered.shape
    levels = seed_aerosol.shape[-1]
    species = volatility.shape[0]
    group_m = level_table(levels, species)
    spread_m = group_m.T
    sat = jnp.tile(volatility, levels)[None, :]
    big = pl.BlockSpec((1, cols, channels), lambda i: (i, 0, 0))
    small = pl.BlockSpec((1, cols, levels), lambda i: (i, 0, 0))
    return pl.pallas_call(
        chem_kernel,
        grid=(rows,),
        in_specs=[
            big,
            small,
            big,
            pl.BlockSpec((1, channels), lambda i: (0, 0)),
            pl.BlockSpec((levels, channels), lambda i: (0, 0)),
            pl.BlockSpec((channels, levels), lambda i: (0, 0)),
        ],
        out_specs=[big, big],
        out_shape=[
            jax.ShapeDtypeStruct(filtered.shape, jnp.float32),
            jax.ShapeDtypeStruct(filtered.shape, jnp.float32),
        ],
    )(filtered, seed_aerosol, cotangent, sat, spread_m, group_m)


def local(
    tracer,
    east_courant,
    north_courant,
    east_limiter,
    north_limiter,
    filter_keep,
    seed_aerosol,
    volatility,
    cotangent,
):
    row_count = tracer.shape[0]
    channels = tracer.shape[2]
    levels = east_courant.shape[2]
    species = volatility.shape[0]
    first_row = lax.axis_index("lat") * row_count
    packed = jnp.concatenate([tracer, east_courant, east_limiter.astype(jnp.float32)], axis=2)
    widened = east_west(packed)
    east_speed = widened[:, :, channels : channels + levels]
    east_choice = widened[:, :, channels + levels :].astype(jnp.int32)

    def zonal_only(window):
        return zonal_window(window, east_speed, east_choice, species)

    after_east, east_back = jax.vjp(zonal_only, widened[:, :, :channels])
    stacked = jnp.concatenate(
        [after_east, north_courant, north_limiter.astype(jnp.float32)], axis=2
    )
    tall_window = north_south(stacked)
    north_speed = tall_window[:, :, channels : channels + levels]
    north_choice = tall_window[:, :, channels + levels :].astype(jnp.int32)

    def meridional_only(window):
        return meridional_window(window, north_speed, north_choice, first_row, species)

    after_north, north_back = jax.vjp(meridional_only, tall_window[:, :, :channels])
    particle, chem_grad = chemistry_step(after_north, seed_aerosol, volatility, cotangent)
    particle, adjoint_filtered = polar_step(
        after_north, seed_aerosol, volatility, cotangent, filter_keep, particle, chem_grad
    )
    return (particle, fold_columns(east_back(fold_rows(north_back(adjoint_filtered)[0]))[0]))


def solution(mesh):
    in_specs = (
        P("lat", "lon", None),
        P("lat", "lon", None),
        P("lat", "lon", None),
        P("lat", "lon", None),
        P("lat", "lon", None),
        P("lat"),
        P("lat", "lon", None),
        P(),
        P("lat", "lon", None),
    )
    out_specs = (P("lat", "lon", None), P("lat", "lon", None))
    return jax.shard_map(local, mesh=mesh, in_specs=in_specs, out_specs=out_specs, check_vma=False)
```

```python
import math

import jax
import jax.numpy as jnp
from jax import lax
from jax.sharding import PartitionSpec as P
from jax.experimental import pallas as pl
from jax.experimental.pallas import tpu as pltpu

NEWTON = 4
KMAX = 32
POLAR = 2


def with_halo(cells, sides, width, closed):
    for axis, dim in sides:
        count = lax.axis_size(axis)
        ends = count if closed else count - 1
        head = lax.slice_in_dim(cells, 0, width, axis=dim)
        tail = lax.slice_in_dim(cells, cells.shape[dim] - width, cells.shape[dim], axis=dim)
        cells = jnp.concatenate(
            [
                lax.ppermute(tail, axis, [(i, (i + 1) % count) for i in range(ends)]),
                cells,
                lax.ppermute(head, axis, [((i + 1) % count, i) for i in range(ends)]),
            ],
            axis=dim,
        )
    return cells


def spread(values, copies):
    return jnp.repeat(values, copies, axis=-1)


def face_weights(courant, limiter):
    upwind = courant >= 0.0
    half = 0.5 * courant
    inner = courant * (7.0 / 12.0)
    outer = jnp.where(limiter == 0, courant * (-1.0 / 12.0), 0.0)
    near_left = jnp.where(
        limiter == 0, inner, jnp.where(limiter == 1, jnp.where(upwind, courant, 0.0), half)
    )
    near_right = jnp.where(
        limiter == 0, inner, jnp.where(limiter == 1, jnp.where(upwind, 0.0, courant), half)
    )
    return jnp.stack([outer, near_left, near_right], axis=0)


def spread_weights(weights, species):
    levels = weights.shape[-1]
    spread_m = level_table(levels, species).T
    return jnp.einsum("...l,lq->...q", weights, spread_m, precision=lax.Precision.HIGHEST)


def zonal_window(window, courant, limiter, species):
    inner_count = window.shape[1] - 4
    weights = spread_weights(
        face_weights(courant[:, 2 : inner_count + 3], limiter[:, 2 : inner_count + 3]), species
    )
    fluxes = (
        weights[0] * (window[:, 0 : inner_count + 1] + window[:, 3 : inner_count + 4])
        + weights[1] * window[:, 1 : inner_count + 2]
        + weights[2] * window[:, 2 : inner_count + 3]
    )
    return window[:, 2 : inner_count + 2] - (fluxes[:, 1:] - fluxes[:, :-1])


def meridional_window(window, courant, limiter, first_row, species):
    inner_count = window.shape[0] - 4
    face_rows = first_row + jnp.arange(inner_count + 1, dtype=jnp.int32)
    opened = jnp.where(face_rows[:, None, None] > 0, courant[2 : inner_count + 3], 0.0)
    weights = spread_weights(face_weights(opened, limiter[2 : inner_count + 3]), species)
    fluxes = (
        weights[0] * (window[0 : inner_count + 1] + window[3 : inner_count + 4])
        + weights[1] * window[1 : inner_count + 2]
        + weights[2] * window[2 : inner_count + 3]
    )
    return window[2 : inner_count + 2] - (fluxes[1:] - fluxes[:-1])


def positive(field):
    return 0.5 * (field + jnp.sqrt(field * field + 1.0))


def level_table(levels, species):
    channel_level = jnp.arange(levels * species, dtype=jnp.int32) // species
    return (channel_level[:, None] == jnp.arange(levels, dtype=jnp.int32)[None, :]).astype(
        jnp.float32
    )


def partition(total_mass, seed_aerosol, volatility):
    levels = seed_aerosol.shape[-1]
    species = volatility.shape[0]
    grouping = level_table(levels, species)
    saturation = jnp.tile(volatility, levels)
    aerosol = seed_aerosol
    for newton_step in range(NEWTON):
        denominator = spread(aerosol, species) + saturation
        fraction = total_mass / denominator
        first_sum = jnp.dot(fraction, grouping, precision=lax.Precision.HIGHEST)
        second_sum = jnp.dot(fraction / denominator, grouping, precision=lax.Precision.HIGHEST)
        residue = 1.0 - seed_aerosol / aerosol - first_sum
        derivative = seed_aerosol / (aerosol * aerosol) + second_sum
        aerosol = aerosol - residue / derivative
    aerosol_q = spread(aerosol, species)
    return total_mass * aerosol_q / (aerosol_q + saturation)


def east_west(field):
    return with_halo(field, (("lon", 1),), 2, True)


def north_south(field):
    return with_halo(field, (("lat", 0),), 2, False)


def fold_rows(gradient):
    inner_rows = gradient.shape[0] - 4
    rim_cells = jnp.concatenate([gradient[:2], gradient[inner_rows + 2 :]], axis=0)
    arrived = north_south(rim_cells)
    middle = gradient[2 : inner_rows + 2]
    return jnp.concatenate(
        [
            middle[:2] + arrived[:2],
            middle[2 : inner_rows - 2],
            middle[inner_rows - 2 :] + arrived[6:],
        ],
        axis=0,
    )


def fold_columns(gradient):
    inner_cols = gradient.shape[1] - 4
    rim_cells = jnp.concatenate([gradient[:, :2], gradient[:, inner_cols + 2 :]], axis=1)
    arrived = east_west(rim_cells)
    middle = gradient[:, 2 : inner_cols + 2]
    return jnp.concatenate(
        [
            middle[:, :2] + arrived[:, :2],
            middle[:, 2 : inner_cols - 2],
            middle[:, inner_cols - 2 :] + arrived[:, 6:],
        ],
        axis=1,
    )


def wave_table(column_count, length):
    position = jnp.arange(column_count, dtype=jnp.int32)
    numbers = jnp.arange(KMAX, dtype=jnp.int32)
    phases = position[:, None] * numbers[None, :] % length
    angles = phases.astype(jnp.float32) * (2.0 * math.pi / length)
    return jnp.concatenate([jnp.cos(angles), jnp.sin(angles)], axis=1)


def wave_weights(keep_values, length):
    numbers = jnp.arange(2 * KMAX, dtype=jnp.int32) % KMAX
    scaling = jnp.where(numbers == 0, 1.0, 2.0) / length
    kept_mask = numbers[None, :] < keep_values[:, None]
    return jnp.where(kept_mask, scaling[None, :], 0.0)


def lowpass_circles(circles, keep_values):
    length = circles.shape[2]
    table_full = wave_table(length, length)
    coefficient = jnp.einsum("rqn,nk->rqk", circles, table_full, precision=lax.Precision.HIGHEST)
    coefficient = coefficient * wave_weights(keep_values, length)[:, None, :]
    lowpass = jnp.einsum("rqk,nk->rqn", coefficient, table_full, precision=lax.Precision.HIGHEST)
    return jnp.where((keep_values <= KMAX)[:, None, None], lowpass, circles)


def split_three(values):
    high = values.astype(jnp.bfloat16)
    rest = values - high.astype(jnp.float32)
    middle = rest.astype(jnp.bfloat16)
    low = (rest - middle.astype(jnp.float32)).astype(jnp.bfloat16)
    return high, middle, low


def select_dot(values, selector, dims):
    total = None
    for piece in split_three(values):
        term = lax.dot_general(piece, selector, dims, preferred_element_type=jnp.float32)
        total = term if total is None else total + term
    return total


def select_dot_left(selector, values, dims):
    total = None
    for piece in split_three(values):
        term = lax.dot_general(selector, piece, dims, preferred_element_type=jnp.float32)
        total = term if total is None else total + term
    return total


def polar_kernel(x_ref, w_ref, t_ref, y_ref, out_go, land_go, out_back, land_back,
                 sem_a, sem_b, sem_c, sem_d):
    count = t_ref.shape[0]
    polar_count, col_count, channels = x_ref.shape
    chunk = channels // count
    padded = out_go.shape[1]
    me = lax.axis_index("lon")
    band = lax.axis_index("lat")
    bands = lax.axis_size("lat")
    active = jnp.logical_or(band == 0, band == bands - 1)
    hi = lax.Precision.HIGHEST
    mesh_id = pl.DeviceIdType.MESH

    def remote(src, dst, send_sem, recv_sem, peer):
        return pltpu.make_async_remote_copy(
            src_ref=src, dst_ref=dst, send_sem=send_sem, recv_sem=recv_sem,
            device_id=(band, peer), device_id_type=mesh_id,
        )

    def round_trip(outbox, inbox, send_sems, recv_sems):
        for offset in range(1, count):
            peer = lax.rem(me + offset, count)
            remote(outbox.at[peer], inbox.at[me], send_sems.at[offset], recv_sems.at[me], peer).start()
        inbox[pl.ds(me, 1)] = outbox[pl.ds(me, 1)]
        for offset in range(1, count):
            peer = lax.rem(me + offset, count)
            remote(outbox.at[peer], inbox.at[me], send_sems.at[offset], recv_sems.at[me], peer).wait_send()
        for offset in range(1, count):
            peer = lax.rem(me + count - offset, count)
            remote(outbox.at[peer], inbox.at[peer], send_sems.at[offset], recv_sems.at[peer], peer).wait_recv()

    @pl.when(active)
    def _():
        barrier = pltpu.get_barrier_semaphore()
        for offset in range(1, count):
            peer = lax.rem(me + offset, count)
            pl.semaphore_signal(barrier, 1, device_id=(band, peer), device_id_type=mesh_id)
        pl.semaphore_wait(barrier, count - 1)
        rows = jnp.concatenate([x_ref[r] for r in range(polar_count)], axis=0)
        slot = lax.broadcasted_iota(jnp.int32, (count * padded, channels), 0)
        channel = lax.broadcasted_iota(jnp.int32, (count * padded, channels), 1)
        target = (channel // chunk) * padded + channel % chunk
        packer = jnp.where(slot == target, 1.0, 0.0).astype(jnp.bfloat16)
        packed = select_dot_left(packer, rows, (((1,), (1,)), ((), ())))
        out_go[...] = packed.reshape(count, padded, polar_count * col_count)
        round_trip(out_go, land_go, sem_a, sem_b)

        def analyse(s, acc):
            return acc + jnp.dot(land_go[s], t_ref[s], precision=hi,
                                 preferred_element_type=jnp.float32)

        coefficient = lax.fori_loop(
            0, count, analyse, jnp.zeros((padded, t_ref.shape[2]), jnp.float32)
        )
        coefficient = coefficient * w_ref[...]

        def synthesise(s, carry):
            out_back[s] = lax.dot_general(coefficient, t_ref[s], (((1,), (1,)), ((), ())),
                                          precision=hi, preferred_element_type=jnp.float32)
            return carry

        lax.fori_loop(0, count, synthesise, 0)
        round_trip(out_back, land_back, sem_c, sem_d)
        back = land_back[...].reshape(count * padded, polar_count * col_count)
        result = select_dot(back, packer, (((0,), (0,)), ((), ())))
        for r in range(polar_count):
            y_ref[r] = result[r * col_count : (r + 1) * col_count]

    @pl.when(jnp.logical_not(active))
    def _():
        y_ref[...] = x_ref[...]


def polar_lowpass(end_rows, weights, blocks, call_id):
    polar_count, col_count, channels = end_rows.shape
    count = blocks.shape[0]
    padded = -(-(channels // count) // 8) * 8
    slab = (count, padded, polar_count * col_count)
    vmem = pl.BlockSpec(memory_space=pltpu.VMEM)
    return pl.pallas_call(
        polar_kernel,
        out_shape=jax.ShapeDtypeStruct(end_rows.shape, end_rows.dtype),
        in_specs=[vmem, vmem, vmem],
        out_specs=vmem,
        scratch_shapes=[
            pltpu.VMEM(slab, jnp.float32),
            pltpu.VMEM(slab, jnp.float32),
            pltpu.VMEM(slab, jnp.float32),
            pltpu.VMEM(slab, jnp.float32),
            pltpu.SemaphoreType.DMA((count,)),
            pltpu.SemaphoreType.DMA((count,)),
            pltpu.SemaphoreType.DMA((count,)),
            pltpu.SemaphoreType.DMA((count,)),
        ],
        compiler_params=pltpu.CompilerParams(collective_id=call_id, has_side_effects=True),
    )(end_rows, weights, blocks)


def column_chemistry(x, seed, cot, sat, valid):
    root = jnp.sqrt(x * x + 1.0)
    mass = jnp.where(valid, 0.5 * (x + root), 0.0)
    cot = jnp.where(valid, cot, 0.0)
    aerosol = seed
    history = []
    for newton_step in range(NEWTON):
        denominator = aerosol + sat
        fraction = mass / denominator
        first_sum = jnp.sum(fraction, axis=-2, keepdims=True)
        second_sum = jnp.sum(fraction / denominator, axis=-2, keepdims=True)
        residue = 1.0 - seed / aerosol - first_sum
        derivative = seed / (aerosol * aerosol) + second_sum
        history.append((aerosol, residue, derivative))
        aerosol = aerosol - residue / derivative
    final_den = aerosol + sat
    particle = mass * aerosol / final_den
    mass_bar = cot * aerosol / final_den
    aerosol_bar = jnp.sum(cot * mass * sat / (final_den * final_den), axis=-2, keepdims=True)
    for newton_step in reversed(range(NEWTON)):
        a_n, residue, derivative = history[newton_step]
        inverse = 1.0 / (a_n + sat)
        third_sum = jnp.sum(mass * inverse * inverse * inverse, axis=-2, keepdims=True)
        slope = -2.0 * (seed / (a_n * a_n * a_n) + third_sum)
        over_g = aerosol_bar / derivative
        over_g2 = over_g * residue / derivative
        mass_bar = mass_bar + over_g * inverse + over_g2 * inverse * inverse
        aerosol_bar = over_g2 * slope
    gradient = mass_bar * 0.5 * (1.0 + x / root)
    return jnp.where(valid, particle, 0.0), jnp.where(valid, gradient, 0.0)


def owner_kernel(x_ref, c_ref, s_ref, w_ref, m_ref, v_ref, t_ref, p_ref, g_ref,
                 out_go, land_go, out_back, land_back, field_s, sem_a, sem_b, sem_c, sem_d):
    count = t_ref.shape[0]
    polar_count, col_count, channels = x_ref.shape
    levels = s_ref.shape[2]
    chunk = channels // count
    padded = out_go.shape[1] // 2
    me = lax.axis_index("lon")
    band = lax.axis_index("lat")
    bands = lax.axis_size("lat")
    active = jnp.logical_or(band == 0, band == bands - 1)
    hi = lax.Precision.HIGHEST
    mesh_id = pl.DeviceIdType.MESH
    nt = (((1,), (1,)), ((), ()))

    def remote(src, dst, send_sem, recv_sem, peer):
        return pltpu.make_async_remote_copy(
            src_ref=src, dst_ref=dst, send_sem=send_sem, recv_sem=recv_sem,
            device_id=(band, peer), device_id_type=mesh_id,
        )

    def round_trip(outbox, inbox, send_sems, recv_sems):
        for offset in range(1, count):
            peer = lax.rem(me + offset, count)
            remote(outbox.at[peer], inbox.at[me], send_sems.at[offset], recv_sems.at[me], peer).start()
        inbox[pl.ds(me, 1)] = outbox[pl.ds(me, 1)]
        for offset in range(1, count):
            peer = lax.rem(me + offset, count)
            remote(outbox.at[peer], inbox.at[me], send_sems.at[offset], recv_sems.at[me], peer).wait_send()
        for offset in range(1, count):
            peer = lax.rem(me + count - offset, count)
            remote(outbox.at[peer], inbox.at[peer], send_sems.at[offset], recv_sems.at[peer], peer).wait_recv()

    @pl.when(active)
    def _():
        barrier = pltpu.get_barrier_semaphore()
        for offset in range(1, count):
            peer = lax.rem(me + offset, count)
            pl.semaphore_signal(barrier, 1, device_id=(band, peer), device_id_type=mesh_id)
        pl.semaphore_wait(barrier, count - 1)
        wide = channels + levels
        slot = lax.broadcasted_iota(jnp.int32, (count * padded, wide), 0)
        channel = lax.broadcasted_iota(jnp.int32, (count * padded, wide), 1)
        target = jnp.where(
            channel < channels,
            (channel // chunk) * padded + channel % chunk,
            (channel - channels) * padded + chunk,
        )
        packer_wide = jnp.where(slot == target, 1.0, 0.0).astype(jnp.bfloat16)
        packer = packer_wide[:, :channels]
        rows = jnp.concatenate(
            [jnp.concatenate([x_ref[r], s_ref[r]], axis=1) for r in range(polar_count)], axis=0
        )
        cots = jnp.concatenate([c_ref[r] for r in range(polar_count)], axis=0)
        lanes = polar_count * col_count
        out_go[:, 0:padded, :] = select_dot_left(packer_wide, rows, nt).reshape(count, padded, lanes)
        out_go[:, padded:, :] = select_dot_left(packer, cots, nt).reshape(count, padded, lanes)
        round_trip(out_go, land_go, sem_a, sem_b)

        def analyse(s, acc):
            return acc + jnp.dot(land_go[s, 0:padded, :], t_ref[s], precision=hi,
                                 preferred_element_type=jnp.float32)

        zero = jnp.zeros((padded, t_ref.shape[2]), jnp.float32)
        coefficient = lax.fori_loop(0, count, analyse, zero, unroll=8) * w_ref[...]
        keep_lane = m_ref[...] > 0.5
        species_row = lax.broadcasted_iota(jnp.int32, (padded, lanes), 0)
        valid = species_row < chunk
        sat = v_ref[...]

        def smooth_out(s, carry):
            smooth = lax.dot_general(coefficient, t_ref[s], nt, precision=hi,
                                     preferred_element_type=jnp.float32)
            field_s[s] = jnp.where(keep_lane, smooth, land_go[s, 0:padded, :])
            return carry

        lax.fori_loop(0, count, smooth_out, 0, unroll=8)
        particle, gradient = column_chemistry(
            field_s[...],
            land_go[:, chunk : chunk + 1, :],
            land_go[:, padded:, :],
            sat[None],
            valid[None],
        )
        out_back[:, 0:padded, :] = particle
        field_s[...] = gradient

        def gather_adjoint(s, acc):
            return acc + jnp.dot(field_s[s], t_ref[s], precision=hi,
                                 preferred_element_type=jnp.float32)

        adjoint_coef = lax.fori_loop(0, count, gather_adjoint, zero, unroll=8) * w_ref[...]

        def synthesise(s, carry):
            smooth = lax.dot_general(adjoint_coef, t_ref[s], nt, precision=hi,
                                     preferred_element_type=jnp.float32)
            out_back[s, padded:, :] = jnp.where(keep_lane, smooth, field_s[s])
            return carry

        lax.fori_loop(0, count, synthesise, 0, unroll=8)
        round_trip(out_back, land_back, sem_c, sem_d)
        particle_back = land_back[:, 0:padded, :].reshape(count * padded, lanes)
        gradient_back = land_back[:, padded:, :].reshape(count * padded, lanes)
        particle_rows = select_dot(particle_back, packer, (((0,), (0,)), ((), ())))
        gradient_rows = select_dot(gradient_back, packer, (((0,), (0,)), ((), ())))
        for r in range(polar_count):
            p_ref[r] = particle_rows[r * col_count : (r + 1) * col_count]
            g_ref[r] = gradient_rows[r * col_count : (r + 1) * col_count]

    @pl.when(jnp.logical_not(active))
    def _():
        p_ref[...] = jnp.zeros_like(p_ref)
        g_ref[...] = jnp.zeros_like(g_ref)


def polar_step(field, seed_aerosol, volatility, cotangent, filter_keep, particle, gradient):
    row_count, col_count, channels = field.shape
    count = lax.axis_size("lon")
    length = col_count * count
    species = volatility.shape[0]
    polar_count = POLAR
    band = lax.axis_index("lat")
    at_north_end = band == 0
    at_south_end = band == lax.axis_size("lat") - 1

    def ends(values):
        return jnp.where(at_north_end, values[:polar_count], values[row_count - polar_count :])

    end_keep = ends(filter_keep)
    table = wave_table(length, length).reshape(count, col_count, 2 * KMAX)
    blocks = jnp.einsum(
        "sjk,rR->srjRk", table, jnp.eye(polar_count, dtype=jnp.float32)
    ).reshape(count, polar_count * col_count, polar_count * 2 * KMAX)
    weights = wave_weights(end_keep, length).reshape(1, polar_count * 2 * KMAX)
    lane_mask = jnp.repeat((end_keep <= KMAX).astype(jnp.float32), col_count)[None, :]
    padded = -(-(channels // count + 1) // 8) * 8
    sat = jnp.concatenate(
        [volatility, jnp.ones((padded - species,), jnp.float32)]
    )[:, None]
    slab = (count, 2 * padded, polar_count * col_count)
    vmem = pl.BlockSpec(memory_space=pltpu.VMEM)
    end_shape = jax.ShapeDtypeStruct((polar_count, col_count, channels), jnp.float32)
    polar_particle, polar_gradient = pl.pallas_call(
        owner_kernel,
        out_shape=[end_shape, end_shape],
        in_specs=[vmem] * 7,
        out_specs=[vmem, vmem],
        scratch_shapes=[
            pltpu.VMEM(slab, jnp.float32),
            pltpu.VMEM(slab, jnp.float32),
            pltpu.VMEM(slab, jnp.float32),
            pltpu.VMEM(slab, jnp.float32),
            pltpu.VMEM((count, padded, polar_count * col_count), jnp.float32),
            pltpu.SemaphoreType.DMA((count,)),
            pltpu.SemaphoreType.DMA((count,)),
            pltpu.SemaphoreType.DMA((count,)),
            pltpu.SemaphoreType.DMA((count,)),
        ],
        compiler_params=pltpu.CompilerParams(collective_id=0, has_side_effects=True),
    )(ends(field), ends(cotangent), ends(seed_aerosol), weights, lane_mask, sat, blocks)

    def merge(values, polar):
        top = jnp.where(at_north_end, polar, values[:polar_count])
        bottom = jnp.where(at_south_end, polar, values[row_count - polar_count :])
        return jnp.concatenate(
            [top, values[polar_count : row_count - polar_count], bottom], axis=0
        )

    return merge(particle, polar_particle), merge(gradient, polar_gradient)


def filter_field(field, filter_keep, call_id):
    row_count, col_count, channels = field.shape
    count = lax.axis_size("lon")
    length = col_count * count
    polar_count = POLAR
    band = lax.axis_index("lat")
    at_north_end = band == 0
    at_south_end = band == lax.axis_size("lat") - 1
    top_rows = field[:polar_count]
    bottom_rows = field[row_count - polar_count :]
    end_rows = jnp.where(at_north_end, top_rows, bottom_rows)
    end_keep = jnp.where(
        at_north_end, filter_keep[:polar_count], filter_keep[row_count - polar_count :]
    )
    table = wave_table(length, length).reshape(count, col_count, 2 * KMAX)
    blocks = jnp.einsum(
        "sjk,rR->srjRk", table, jnp.eye(polar_count, dtype=jnp.float32)
    ).reshape(count, polar_count * col_count, polar_count * 2 * KMAX)
    weights = wave_weights(end_keep, length).reshape(1, polar_count * 2 * KMAX)
    lowpass = polar_lowpass(end_rows, weights, blocks, call_id)
    smoothed = jnp.where((end_keep <= KMAX)[:, None, None], lowpass, end_rows)
    new_top = jnp.where(at_north_end, smoothed, top_rows)
    new_bottom = jnp.where(at_south_end, smoothed, bottom_rows)
    return jnp.concatenate(
        [new_top, field[polar_count : row_count - polar_count], new_bottom], axis=0
    )


def chem_kernel(x_ref, seed_ref, cot_ref, sat_ref, spread_ref, group_ref, p_ref, g_ref):
    row = pl.program_id(0)
    rows = pl.num_programs(0)
    band = lax.axis_index("lat")
    bands = lax.axis_size("lat")
    polar = jnp.logical_or(
        jnp.logical_and(band == 0, row == 0),
        jnp.logical_and(band == bands - 1, row == rows - 1),
    )

    @pl.when(jnp.logical_not(polar))
    def _():
        for part in range(POLAR):
            chem_body(part, x_ref, seed_ref, cot_ref, sat_ref, spread_ref, group_ref, p_ref, g_ref)


def chem_body(part, x_ref, seed_ref, cot_ref, sat_ref, spread_ref, group_ref, p_ref, g_ref):
    hi = lax.Precision.HIGHEST
    x = x_ref[part]
    seed = seed_ref[part]
    cot = cot_ref[part]
    sat = sat_ref[...]
    spread_m = spread_ref[...].astype(jnp.bfloat16)
    group_m = group_ref[...].astype(jnp.bfloat16)

    plain = (((1,), (0,)), ((), ()))

    def up(v):
        return select_dot(v, spread_m, plain)

    def down(v):
        return select_dot(v, group_m, plain)

    root = jnp.sqrt(x * x + 1.0)
    mass = 0.5 * (x + root)
    aerosol = seed
    history = []
    for newton_step in range(NEWTON):
        denominator = up(aerosol) + sat
        fraction = mass / denominator
        first_sum = down(fraction)
        second_sum = down(fraction / denominator)
        residue = 1.0 - seed / aerosol - first_sum
        derivative = seed / (aerosol * aerosol) + second_sum
        history.append((aerosol, residue, derivative))
        aerosol = aerosol - residue / derivative
    aerosol_q = up(aerosol)
    final_den = aerosol_q + sat
    p_ref[part] = mass * aerosol_q / final_den
    mass_bar = cot * aerosol_q / final_den
    aerosol_bar = down(cot * mass * sat / (final_den * final_den))
    for newton_step in reversed(range(NEWTON)):
        a_n, residue, derivative = history[newton_step]
        inverse = 1.0 / (up(a_n) + sat)
        third_sum = down(mass * inverse * inverse * inverse)
        slope = -2.0 * (seed / (a_n * a_n * a_n) + third_sum)
        over_g = aerosol_bar / derivative
        over_g2 = over_g * residue / derivative
        mass_bar = mass_bar + up(over_g) * inverse + up(over_g2) * inverse * inverse
        aerosol_bar = over_g2 * slope
    g_ref[part] = mass_bar * 0.5 * (1.0 + x / root)


def chemistry_step(filtered, seed_aerosol, volatility, cotangent):
    rows, cols, channels = filtered.shape
    levels = seed_aerosol.shape[-1]
    species = volatility.shape[0]
    group_m = level_table(levels, species)
    spread_m = group_m.T
    sat = jnp.tile(volatility, levels)[None, :]
    big = pl.BlockSpec((POLAR, cols, channels), lambda i: (i, 0, 0))
    small = pl.BlockSpec((POLAR, cols, levels), lambda i: (i, 0, 0))
    return pl.pallas_call(
        chem_kernel,
        grid=(rows // POLAR,),
        in_specs=[
            big,
            small,
            big,
            pl.BlockSpec((1, channels), lambda i: (0, 0)),
            pl.BlockSpec((levels, channels), lambda i: (0, 0)),
            pl.BlockSpec((channels, levels), lambda i: (0, 0)),
        ],
        out_specs=[big, big],
        out_shape=[
            jax.ShapeDtypeStruct(filtered.shape, jnp.float32),
            jax.ShapeDtypeStruct(filtered.shape, jnp.float32),
        ],
    )(filtered, seed_aerosol, cotangent, sat, spread_m, group_m)


def local(
    tracer,
    east_courant,
    north_courant,
    east_limiter,
    north_limiter,
    filter_keep,
    seed_aerosol,
    volatility,
    cotangent,
):
    row_count = tracer.shape[0]
    channels = tracer.shape[2]
    levels = east_courant.shape[2]
    species = volatility.shape[0]
    first_row = lax.axis_index("lat") * row_count
    packed = jnp.concatenate([tracer, east_courant, east_limiter.astype(jnp.float32)], axis=2)
    widened = east_west(packed)
    east_speed = widened[:, :, channels : channels + levels]
    east_choice = widened[:, :, channels + levels :].astype(jnp.int32)

    def zonal_only(window):
        return zonal_window(window, east_speed, east_choice, species)

    after_east, east_back = jax.vjp(zonal_only, widened[:, :, :channels])
    stacked = jnp.concatenate(
        [after_east, north_courant, north_limiter.astype(jnp.float32)], axis=2
    )
    tall_window = north_south(stacked)
    north_speed = tall_window[:, :, channels : channels + levels]
    north_choice = tall_window[:, :, channels + levels :].astype(jnp.int32)

    def meridional_only(window):
        return meridional_window(window, north_speed, north_choice, first_row, species)

    after_north, north_back = jax.vjp(meridional_only, tall_window[:, :, :channels])
    particle, chem_grad = chemistry_step(after_north, seed_aerosol, volatility, cotangent)
    particle, adjoint_filtered = polar_step(
        after_north, seed_aerosol, volatility, cotangent, filter_keep, particle, chem_grad
    )
    return (particle, fold_columns(east_back(fold_rows(north_back(adjoint_filtered)[0]))[0]))


def solution(mesh):
    in_specs = (
        P("lat", "lon", None),
        P("lat", "lon", None),
        P("lat", "lon", None),
        P("lat", "lon", None),
        P("lat", "lon", None),
        P("lat"),
        P("lat", "lon", None),
        P(),
        P("lat", "lon", None),
    )
    out_specs = (P("lat", "lon", None), P("lat", "lon", None))
    return jax.shard_map(local, mesh=mesh, in_specs=in_specs, out_specs=out_specs, check_vma=False)
```

```python
import math

import jax
import jax.numpy as jnp
from jax import lax
from jax.sharding import PartitionSpec as P
from jax.experimental import pallas as pl
from jax.experimental.pallas import tpu as pltpu

NEWTON = 4
KMAX = 32
POLAR = 2


def with_halo(cells, sides, width, closed):
    for axis, dim in sides:
        count = lax.axis_size(axis)
        ends = count if closed else count - 1
        head = lax.slice_in_dim(cells, 0, width, axis=dim)
        tail = lax.slice_in_dim(cells, cells.shape[dim] - width, cells.shape[dim], axis=dim)
        cells = jnp.concatenate(
            [
                lax.ppermute(tail, axis, [(i, (i + 1) % count) for i in range(ends)]),
                cells,
                lax.ppermute(head, axis, [((i + 1) % count, i) for i in range(ends)]),
            ],
            axis=dim,
        )
    return cells


def spread(values, copies):
    return jnp.repeat(values, copies, axis=-1)


def face_weights(courant, limiter):
    upwind = courant >= 0.0
    half = 0.5 * courant
    inner = courant * (7.0 / 12.0)
    outer = jnp.where(limiter == 0, courant * (-1.0 / 12.0), 0.0)
    near_left = jnp.where(
        limiter == 0, inner, jnp.where(limiter == 1, jnp.where(upwind, courant, 0.0), half)
    )
    near_right = jnp.where(
        limiter == 0, inner, jnp.where(limiter == 1, jnp.where(upwind, 0.0, courant), half)
    )
    return jnp.stack([outer, near_left, near_right], axis=0)


def spread_weights(weights, species):
    levels = weights.shape[-1]
    spread_m = level_table(levels, species).T
    return jnp.einsum("...l,lq->...q", weights, spread_m, precision=lax.Precision.HIGHEST)


def zonal_window(window, courant, limiter, species):
    inner_count = window.shape[1] - 4
    weights = spread_weights(
        face_weights(courant[:, 2 : inner_count + 3], limiter[:, 2 : inner_count + 3]), species
    )
    fluxes = (
        weights[0] * (window[:, 0 : inner_count + 1] + window[:, 3 : inner_count + 4])
        + weights[1] * window[:, 1 : inner_count + 2]
        + weights[2] * window[:, 2 : inner_count + 3]
    )
    return window[:, 2 : inner_count + 2] - (fluxes[:, 1:] - fluxes[:, :-1])


def meridional_window(window, courant, limiter, first_row, species):
    inner_count = window.shape[0] - 4
    face_rows = first_row + jnp.arange(inner_count + 1, dtype=jnp.int32)
    opened = jnp.where(face_rows[:, None, None] > 0, courant[2 : inner_count + 3], 0.0)
    weights = spread_weights(face_weights(opened, limiter[2 : inner_count + 3]), species)
    fluxes = (
        weights[0] * (window[0 : inner_count + 1] + window[3 : inner_count + 4])
        + weights[1] * window[1 : inner_count + 2]
        + weights[2] * window[2 : inner_count + 3]
    )
    return window[2 : inner_count + 2] - (fluxes[1:] - fluxes[:-1])


def positive(field):
    return 0.5 * (field + jnp.sqrt(field * field + 1.0))


def level_table(levels, species):
    channel_level = jnp.arange(levels * species, dtype=jnp.int32) // species
    return (channel_level[:, None] == jnp.arange(levels, dtype=jnp.int32)[None, :]).astype(
        jnp.float32
    )


def partition(total_mass, seed_aerosol, volatility):
    levels = seed_aerosol.shape[-1]
    species = volatility.shape[0]
    grouping = level_table(levels, species)
    saturation = jnp.tile(volatility, levels)
    aerosol = seed_aerosol
    for newton_step in range(NEWTON):
        denominator = spread(aerosol, species) + saturation
        fraction = total_mass / denominator
        first_sum = jnp.dot(fraction, grouping, precision=lax.Precision.HIGHEST)
        second_sum = jnp.dot(fraction / denominator, grouping, precision=lax.Precision.HIGHEST)
        residue = 1.0 - seed_aerosol / aerosol - first_sum
        derivative = seed_aerosol / (aerosol * aerosol) + second_sum
        aerosol = aerosol - residue / derivative
    aerosol_q = spread(aerosol, species)
    return total_mass * aerosol_q / (aerosol_q + saturation)


def east_west(field):
    return with_halo(field, (("lon", 1),), 2, True)


def north_south(field):
    return with_halo(field, (("lat", 0),), 2, False)


def fold_rows(gradient):
    inner_rows = gradient.shape[0] - 4
    rim_cells = jnp.concatenate([gradient[:2], gradient[inner_rows + 2 :]], axis=0)
    arrived = north_south(rim_cells)
    middle = gradient[2 : inner_rows + 2]
    return jnp.concatenate(
        [
            middle[:2] + arrived[:2],
            middle[2 : inner_rows - 2],
            middle[inner_rows - 2 :] + arrived[6:],
        ],
        axis=0,
    )


def fold_columns(gradient):
    inner_cols = gradient.shape[1] - 4
    rim_cells = jnp.concatenate([gradient[:, :2], gradient[:, inner_cols + 2 :]], axis=1)
    arrived = east_west(rim_cells)
    middle = gradient[:, 2 : inner_cols + 2]
    return jnp.concatenate(
        [
            middle[:, :2] + arrived[:, :2],
            middle[:, 2 : inner_cols - 2],
            middle[:, inner_cols - 2 :] + arrived[:, 6:],
        ],
        axis=1,
    )


def wave_table(column_count, length):
    position = jnp.arange(column_count, dtype=jnp.int32)
    numbers = jnp.arange(KMAX, dtype=jnp.int32)
    phases = position[:, None] * numbers[None, :] % length
    angles = phases.astype(jnp.float32) * (2.0 * math.pi / length)
    return jnp.concatenate([jnp.cos(angles), jnp.sin(angles)], axis=1)


def wave_weights(keep_values, length):
    numbers = jnp.arange(2 * KMAX, dtype=jnp.int32) % KMAX
    scaling = jnp.where(numbers == 0, 1.0, 2.0) / length
    kept_mask = numbers[None, :] < keep_values[:, None]
    return jnp.where(kept_mask, scaling[None, :], 0.0)


def lowpass_circles(circles, keep_values):
    length = circles.shape[2]
    table_full = wave_table(length, length)
    coefficient = jnp.einsum("rqn,nk->rqk", circles, table_full, precision=lax.Precision.HIGHEST)
    coefficient = coefficient * wave_weights(keep_values, length)[:, None, :]
    lowpass = jnp.einsum("rqk,nk->rqn", coefficient, table_full, precision=lax.Precision.HIGHEST)
    return jnp.where((keep_values <= KMAX)[:, None, None], lowpass, circles)


def split_three(values):
    high = values.astype(jnp.bfloat16)
    rest = values - high.astype(jnp.float32)
    middle = rest.astype(jnp.bfloat16)
    low = (rest - middle.astype(jnp.float32)).astype(jnp.bfloat16)
    return high, middle, low


def select_dot(values, selector, dims):
    total = None
    for piece in split_three(values):
        term = lax.dot_general(piece, selector, dims, preferred_element_type=jnp.float32)
        total = term if total is None else total + term
    return total


def select_dot_left(selector, values, dims):
    total = None
    for piece in split_three(values):
        term = lax.dot_general(selector, piece, dims, preferred_element_type=jnp.float32)
        total = term if total is None else total + term
    return total


def polar_kernel(x_ref, w_ref, t_ref, y_ref, out_go, land_go, out_back, land_back,
                 sem_a, sem_b, sem_c, sem_d):
    count = t_ref.shape[0]
    polar_count, col_count, channels = x_ref.shape
    chunk = channels // count
    padded = out_go.shape[1]
    me = lax.axis_index("lon")
    band = lax.axis_index("lat")
    bands = lax.axis_size("lat")
    active = jnp.logical_or(band == 0, band == bands - 1)
    hi = lax.Precision.HIGHEST
    mesh_id = pl.DeviceIdType.MESH

    def remote(src, dst, send_sem, recv_sem, peer):
        return pltpu.make_async_remote_copy(
            src_ref=src, dst_ref=dst, send_sem=send_sem, recv_sem=recv_sem,
            device_id=(band, peer), device_id_type=mesh_id,
        )

    def round_trip(outbox, inbox, send_sems, recv_sems):
        for offset in range(1, count):
            peer = lax.rem(me + offset, count)
            remote(outbox.at[peer], inbox.at[me], send_sems.at[offset], recv_sems.at[me], peer).start()
        inbox[pl.ds(me, 1)] = outbox[pl.ds(me, 1)]
        for offset in range(1, count):
            peer = lax.rem(me + offset, count)
            remote(outbox.at[peer], inbox.at[me], send_sems.at[offset], recv_sems.at[me], peer).wait_send()
        for offset in range(1, count):
            peer = lax.rem(me + count - offset, count)
            remote(outbox.at[peer], inbox.at[peer], send_sems.at[offset], recv_sems.at[peer], peer).wait_recv()

    @pl.when(active)
    def _():
        barrier = pltpu.get_barrier_semaphore()
        for offset in range(1, count):
            peer = lax.rem(me + offset, count)
            pl.semaphore_signal(barrier, 1, device_id=(band, peer), device_id_type=mesh_id)
        pl.semaphore_wait(barrier, count - 1)
        rows = jnp.concatenate([x_ref[r] for r in range(polar_count)], axis=0)
        slot = lax.broadcasted_iota(jnp.int32, (count * padded, channels), 0)
        channel = lax.broadcasted_iota(jnp.int32, (count * padded, channels), 1)
        target = (channel // chunk) * padded + channel % chunk
        packer = jnp.where(slot == target, 1.0, 0.0).astype(jnp.bfloat16)
        packed = select_dot_left(packer, rows, (((1,), (1,)), ((), ())))
        out_go[...] = packed.reshape(count, padded, polar_count * col_count)
        round_trip(out_go, land_go, sem_a, sem_b)

        def analyse(s, acc):
            return acc + jnp.dot(land_go[s], t_ref[s], precision=hi,
                                 preferred_element_type=jnp.float32)

        coefficient = lax.fori_loop(
            0, count, analyse, jnp.zeros((padded, t_ref.shape[2]), jnp.float32)
        )
        coefficient = coefficient * w_ref[...]

        def synthesise(s, carry):
            out_back[s] = lax.dot_general(coefficient, t_ref[s], (((1,), (1,)), ((), ())),
                                          precision=hi, preferred_element_type=jnp.float32)
            return carry

        lax.fori_loop(0, count, synthesise, 0)
        round_trip(out_back, land_back, sem_c, sem_d)
        back = land_back[...].reshape(count * padded, polar_count * col_count)
        result = select_dot(back, packer, (((0,), (0,)), ((), ())))
        for r in range(polar_count):
            y_ref[r] = result[r * col_count : (r + 1) * col_count]

    @pl.when(jnp.logical_not(active))
    def _():
        y_ref[...] = x_ref[...]


def polar_lowpass(end_rows, weights, blocks, call_id):
    polar_count, col_count, channels = end_rows.shape
    count = blocks.shape[0]
    padded = -(-(channels // count) // 8) * 8
    slab = (count, padded, polar_count * col_count)
    vmem = pl.BlockSpec(memory_space=pltpu.VMEM)
    return pl.pallas_call(
        polar_kernel,
        out_shape=jax.ShapeDtypeStruct(end_rows.shape, end_rows.dtype),
        in_specs=[vmem, vmem, vmem],
        out_specs=vmem,
        scratch_shapes=[
            pltpu.VMEM(slab, jnp.float32),
            pltpu.VMEM(slab, jnp.float32),
            pltpu.VMEM(slab, jnp.float32),
            pltpu.VMEM(slab, jnp.float32),
            pltpu.SemaphoreType.DMA((count,)),
            pltpu.SemaphoreType.DMA((count,)),
            pltpu.SemaphoreType.DMA((count,)),
            pltpu.SemaphoreType.DMA((count,)),
        ],
        compiler_params=pltpu.CompilerParams(collective_id=call_id, has_side_effects=True),
    )(end_rows, weights, blocks)


def column_chemistry(x, seed, cot, sat, valid):
    root = jnp.sqrt(x * x + 1.0)
    mass = jnp.where(valid, 0.5 * (x + root), 0.0)
    cot = jnp.where(valid, cot, 0.0)
    aerosol = seed
    history = []
    for newton_step in range(NEWTON):
        denominator = aerosol + sat
        fraction = mass / denominator
        first_sum = jnp.sum(fraction, axis=-2, keepdims=True)
        second_sum = jnp.sum(fraction / denominator, axis=-2, keepdims=True)
        residue = 1.0 - seed / aerosol - first_sum
        derivative = seed / (aerosol * aerosol) + second_sum
        history.append((aerosol, residue, derivative))
        aerosol = aerosol - residue / derivative
    final_den = aerosol + sat
    particle = mass * aerosol / final_den
    mass_bar = cot * aerosol / final_den
    aerosol_bar = jnp.sum(cot * mass * sat / (final_den * final_den), axis=-2, keepdims=True)
    for newton_step in reversed(range(NEWTON)):
        a_n, residue, derivative = history[newton_step]
        inverse = 1.0 / (a_n + sat)
        third_sum = jnp.sum(mass * inverse * inverse * inverse, axis=-2, keepdims=True)
        slope = -2.0 * (seed / (a_n * a_n * a_n) + third_sum)
        over_g = aerosol_bar / derivative
        over_g2 = over_g * residue / derivative
        mass_bar = mass_bar + over_g * inverse + over_g2 * inverse * inverse
        aerosol_bar = over_g2 * slope
    gradient = mass_bar * 0.5 * (1.0 + x / root)
    return jnp.where(valid, particle, 0.0), jnp.where(valid, gradient, 0.0)


def owner_kernel(x_ref, c_ref, s_ref, w_ref, m_ref, v_ref, t_ref, p_ref, g_ref,
                 out_go, land_go, out_back, land_back, field_s, sem_a, sem_b, sem_c, sem_d):
    count = t_ref.shape[0]
    polar_count, col_count, channels = x_ref.shape
    levels = s_ref.shape[2]
    chunk = channels // count
    padded = out_go.shape[1] // 2
    me = lax.axis_index("lon")
    band = lax.axis_index("lat")
    bands = lax.axis_size("lat")
    active = jnp.logical_or(band == 0, band == bands - 1)
    hi = lax.Precision.HIGH
    mesh_id = pl.DeviceIdType.MESH
    nt = (((1,), (1,)), ((), ()))

    def remote(src, dst, send_sem, recv_sem, peer):
        return pltpu.make_async_remote_copy(
            src_ref=src, dst_ref=dst, send_sem=send_sem, recv_sem=recv_sem,
            device_id=(band, peer), device_id_type=mesh_id,
        )

    def round_trip(outbox, inbox, send_sems, recv_sems):
        for offset in range(1, count):
            peer = lax.rem(me + offset, count)
            remote(outbox.at[peer], inbox.at[me], send_sems.at[offset], recv_sems.at[me], peer).start()
        inbox[pl.ds(me, 1)] = outbox[pl.ds(me, 1)]
        for offset in range(1, count):
            peer = lax.rem(me + offset, count)
            remote(outbox.at[peer], inbox.at[me], send_sems.at[offset], recv_sems.at[me], peer).wait_send()
        for offset in range(1, count):
            peer = lax.rem(me + count - offset, count)
            remote(outbox.at[peer], inbox.at[peer], send_sems.at[offset], recv_sems.at[peer], peer).wait_recv()

    @pl.when(active)
    def _():
        barrier = pltpu.get_barrier_semaphore()
        for offset in range(1, count):
            peer = lax.rem(me + offset, count)
            pl.semaphore_signal(barrier, 1, device_id=(band, peer), device_id_type=mesh_id)
        pl.semaphore_wait(barrier, count - 1)
        wide = channels + levels
        slot = lax.broadcasted_iota(jnp.int32, (count * padded, wide), 0)
        channel = lax.broadcasted_iota(jnp.int32, (count * padded, wide), 1)
        target = jnp.where(
            channel < channels,
            (channel // chunk) * padded + channel % chunk,
            (channel - channels) * padded + chunk,
        )
        packer_wide = jnp.where(slot == target, 1.0, 0.0).astype(jnp.bfloat16)
        packer = packer_wide[:, :channels]
        rows = jnp.concatenate(
            [jnp.concatenate([x_ref[r], s_ref[r]], axis=1) for r in range(polar_count)], axis=0
        )
        cots = jnp.concatenate([c_ref[r] for r in range(polar_count)], axis=0)
        lanes = polar_count * col_count
        out_go[:, 0:padded, :] = select_dot_left(packer_wide, rows, nt).reshape(count, padded, lanes)
        out_go[:, padded:, :] = select_dot_left(packer, cots, nt).reshape(count, padded, lanes)
        round_trip(out_go, land_go, sem_a, sem_b)

        def analyse(s, acc):
            return acc + jnp.dot(land_go[s, 0:padded, :], t_ref[s], precision=hi,
                                 preferred_element_type=jnp.float32)

        zero = jnp.zeros((padded, t_ref.shape[2]), jnp.float32)
        coefficient = lax.fori_loop(0, count, analyse, zero, unroll=8) * w_ref[...]
        keep_lane = m_ref[...] > 0.5
        species_row = lax.broadcasted_iota(jnp.int32, (padded, lanes), 0)
        valid = species_row < chunk
        sat = v_ref[...]

        def smooth_out(s, carry):
            smooth = lax.dot_general(coefficient, t_ref[s], nt, precision=hi,
                                     preferred_element_type=jnp.float32)
            field_s[s] = jnp.where(keep_lane, smooth, land_go[s, 0:padded, :])
            return carry

        lax.fori_loop(0, count, smooth_out, 0, unroll=8)
        particle, gradient = column_chemistry(
            field_s[...],
            land_go[:, chunk : chunk + 1, :],
            land_go[:, padded:, :],
            sat[None],
            valid[None],
        )
        out_back[:, 0:padded, :] = particle
        field_s[...] = gradient

        def gather_adjoint(s, acc):
            return acc + jnp.dot(field_s[s], t_ref[s], precision=hi,
                                 preferred_element_type=jnp.float32)

        adjoint_coef = lax.fori_loop(0, count, gather_adjoint, zero, unroll=8) * w_ref[...]

        def synthesise(s, carry):
            smooth = lax.dot_general(adjoint_coef, t_ref[s], nt, precision=hi,
                                     preferred_element_type=jnp.float32)
            out_back[s, padded:, :] = jnp.where(keep_lane, smooth, field_s[s])
            return carry

        lax.fori_loop(0, count, synthesise, 0, unroll=8)
        round_trip(out_back, land_back, sem_c, sem_d)
        particle_back = land_back[:, 0:padded, :].reshape(count * padded, lanes)
        gradient_back = land_back[:, padded:, :].reshape(count * padded, lanes)
        particle_rows = select_dot(particle_back, packer, (((0,), (0,)), ((), ())))
        gradient_rows = select_dot(gradient_back, packer, (((0,), (0,)), ((), ())))
        for r in range(polar_count):
            p_ref[r] = particle_rows[r * col_count : (r + 1) * col_count]
            g_ref[r] = gradient_rows[r * col_count : (r + 1) * col_count]

    @pl.when(jnp.logical_not(active))
    def _():
        p_ref[...] = jnp.zeros_like(p_ref)
        g_ref[...] = jnp.zeros_like(g_ref)


def polar_step(field, seed_aerosol, volatility, cotangent, filter_keep, particle, gradient):
    row_count, col_count, channels = field.shape
    count = lax.axis_size("lon")
    length = col_count * count
    species = volatility.shape[0]
    polar_count = POLAR
    band = lax.axis_index("lat")
    at_north_end = band == 0
    at_south_end = band == lax.axis_size("lat") - 1

    def ends(values):
        return jnp.where(at_north_end, values[:polar_count], values[row_count - polar_count :])

    end_keep = ends(filter_keep)
    table = wave_table(length, length).reshape(count, col_count, 2 * KMAX)
    blocks = jnp.einsum(
        "sjk,rR->srjRk", table, jnp.eye(polar_count, dtype=jnp.float32)
    ).reshape(count, polar_count * col_count, polar_count * 2 * KMAX)
    weights = wave_weights(end_keep, length).reshape(1, polar_count * 2 * KMAX)
    lane_mask = jnp.repeat((end_keep <= KMAX).astype(jnp.float32), col_count)[None, :]
    padded = -(-(channels // count + 1) // 8) * 8
    sat = jnp.concatenate(
        [volatility, jnp.ones((padded - species,), jnp.float32)]
    )[:, None]
    slab = (count, 2 * padded, polar_count * col_count)
    vmem = pl.BlockSpec(memory_space=pltpu.VMEM)
    end_shape = jax.ShapeDtypeStruct((polar_count, col_count, channels), jnp.float32)
    polar_particle, polar_gradient = pl.pallas_call(
        owner_kernel,
        out_shape=[end_shape, end_shape],
        in_specs=[vmem] * 7,
        out_specs=[vmem, vmem],
        scratch_shapes=[
            pltpu.VMEM(slab, jnp.float32),
            pltpu.VMEM(slab, jnp.float32),
            pltpu.VMEM(slab, jnp.float32),
            pltpu.VMEM(slab, jnp.float32),
            pltpu.VMEM((count, padded, polar_count * col_count), jnp.float32),
            pltpu.SemaphoreType.DMA((count,)),
            pltpu.SemaphoreType.DMA((count,)),
            pltpu.SemaphoreType.DMA((count,)),
            pltpu.SemaphoreType.DMA((count,)),
        ],
        compiler_params=pltpu.CompilerParams(collective_id=0, has_side_effects=True),
    )(ends(field), ends(cotangent), ends(seed_aerosol), weights, lane_mask, sat, blocks)

    def merge(values, polar):
        top = jnp.where(at_north_end, polar, values[:polar_count])
        bottom = jnp.where(at_south_end, polar, values[row_count - polar_count :])
        return jnp.concatenate(
            [top, values[polar_count : row_count - polar_count], bottom], axis=0
        )

    return merge(particle, polar_particle), merge(gradient, polar_gradient)


def filter_field(field, filter_keep, call_id):
    row_count, col_count, channels = field.shape
    count = lax.axis_size("lon")
    length = col_count * count
    polar_count = POLAR
    band = lax.axis_index("lat")
    at_north_end = band == 0
    at_south_end = band == lax.axis_size("lat") - 1
    top_rows = field[:polar_count]
    bottom_rows = field[row_count - polar_count :]
    end_rows = jnp.where(at_north_end, top_rows, bottom_rows)
    end_keep = jnp.where(
        at_north_end, filter_keep[:polar_count], filter_keep[row_count - polar_count :]
    )
    table = wave_table(length, length).reshape(count, col_count, 2 * KMAX)
    blocks = jnp.einsum(
        "sjk,rR->srjRk", table, jnp.eye(polar_count, dtype=jnp.float32)
    ).reshape(count, polar_count * col_count, polar_count * 2 * KMAX)
    weights = wave_weights(end_keep, length).reshape(1, polar_count * 2 * KMAX)
    lowpass = polar_lowpass(end_rows, weights, blocks, call_id)
    smoothed = jnp.where((end_keep <= KMAX)[:, None, None], lowpass, end_rows)
    new_top = jnp.where(at_north_end, smoothed, top_rows)
    new_bottom = jnp.where(at_south_end, smoothed, bottom_rows)
    return jnp.concatenate(
        [new_top, field[polar_count : row_count - polar_count], new_bottom], axis=0
    )


def chem_kernel(x_ref, seed_ref, cot_ref, sat_ref, spread_ref, group_ref, p_ref, g_ref):
    row = pl.program_id(0)
    rows = pl.num_programs(0)
    band = lax.axis_index("lat")
    bands = lax.axis_size("lat")
    polar = jnp.logical_or(
        jnp.logical_and(band == 0, row == 0),
        jnp.logical_and(band == bands - 1, row == rows - 1),
    )

    @pl.when(jnp.logical_not(polar))
    def _():
        for part in range(POLAR):
            chem_body(part, x_ref, seed_ref, cot_ref, sat_ref, spread_ref, group_ref, p_ref, g_ref)


def chem_body(part, x_ref, seed_ref, cot_ref, sat_ref, spread_ref, group_ref, p_ref, g_ref):
    hi = lax.Precision.HIGHEST
    x = x_ref[part]
    seed = seed_ref[part]
    cot = cot_ref[part]
    sat = sat_ref[...]
    spread_m = spread_ref[...].astype(jnp.bfloat16)
    group_m = group_ref[...].astype(jnp.bfloat16)

    plain = (((1,), (0,)), ((), ()))

    def up(v):
        return select_dot(v, spread_m, plain)

    def down(v):
        return select_dot(v, group_m, plain)

    root = jnp.sqrt(x * x + 1.0)
    mass = 0.5 * (x + root)
    aerosol = seed
    history = []
    for newton_step in range(NEWTON):
        denominator = up(aerosol) + sat
        fraction = mass / denominator
        first_sum = down(fraction)
        second_sum = down(fraction / denominator)
        residue = 1.0 - seed / aerosol - first_sum
        derivative = seed / (aerosol * aerosol) + second_sum
        history.append((aerosol, residue, derivative))
        aerosol = aerosol - residue / derivative
    aerosol_q = up(aerosol)
    final_den = aerosol_q + sat
    p_ref[part] = mass * aerosol_q / final_den
    mass_bar = cot * aerosol_q / final_den
    aerosol_bar = down(cot * mass * sat / (final_den * final_den))
    for newton_step in reversed(range(NEWTON)):
        a_n, residue, derivative = history[newton_step]
        inverse = 1.0 / (up(a_n) + sat)
        third_sum = down(mass * inverse * inverse * inverse)
        slope = -2.0 * (seed / (a_n * a_n * a_n) + third_sum)
        over_g = aerosol_bar / derivative
        over_g2 = over_g * residue / derivative
        mass_bar = mass_bar + up(over_g) * inverse + up(over_g2) * inverse * inverse
        aerosol_bar = over_g2 * slope
    g_ref[part] = mass_bar * 0.5 * (1.0 + x / root)


def chemistry_step(filtered, seed_aerosol, volatility, cotangent):
    rows, cols, channels = filtered.shape
    levels = seed_aerosol.shape[-1]
    species = volatility.shape[0]
    group_m = level_table(levels, species)
    spread_m = group_m.T
    sat = jnp.tile(volatility, levels)[None, :]
    big = pl.BlockSpec((POLAR, cols, channels), lambda i: (i, 0, 0))
    small = pl.BlockSpec((POLAR, cols, levels), lambda i: (i, 0, 0))
    return pl.pallas_call(
        chem_kernel,
        grid=(rows // POLAR,),
        in_specs=[
            big,
            small,
            big,
            pl.BlockSpec((1, channels), lambda i: (0, 0)),
            pl.BlockSpec((levels, channels), lambda i: (0, 0)),
            pl.BlockSpec((channels, levels), lambda i: (0, 0)),
        ],
        out_specs=[big, big],
        out_shape=[
            jax.ShapeDtypeStruct(filtered.shape, jnp.float32),
            jax.ShapeDtypeStruct(filtered.shape, jnp.float32),
        ],
    )(filtered, seed_aerosol, cotangent, sat, spread_m, group_m)


def local(
    tracer,
    east_courant,
    north_courant,
    east_limiter,
    north_limiter,
    filter_keep,
    seed_aerosol,
    volatility,
    cotangent,
):
    row_count = tracer.shape[0]
    channels = tracer.shape[2]
    levels = east_courant.shape[2]
    species = volatility.shape[0]
    first_row = lax.axis_index("lat") * row_count
    packed = jnp.concatenate([tracer, east_courant, east_limiter.astype(jnp.float32)], axis=2)
    widened = east_west(packed)
    east_speed = widened[:, :, channels : channels + levels]
    east_choice = widened[:, :, channels + levels :].astype(jnp.int32)

    def zonal_only(window):
        return zonal_window(window, east_speed, east_choice, species)

    after_east, east_back = jax.vjp(zonal_only, widened[:, :, :channels])
    stacked = jnp.concatenate(
        [after_east, north_courant, north_limiter.astype(jnp.float32)], axis=2
    )
    tall_window = north_south(stacked)
    north_speed = tall_window[:, :, channels : channels + levels]
    north_choice = tall_window[:, :, channels + levels :].astype(jnp.int32)

    def meridional_only(window):
        return meridional_window(window, north_speed, north_choice, first_row, species)

    after_north, north_back = jax.vjp(meridional_only, tall_window[:, :, :channels])
    particle, chem_grad = chemistry_step(after_north, seed_aerosol, volatility, cotangent)
    particle, adjoint_filtered = polar_step(
        after_north, seed_aerosol, volatility, cotangent, filter_keep, particle, chem_grad
    )
    return (particle, fold_columns(east_back(fold_rows(north_back(adjoint_filtered)[0]))[0]))


def solution(mesh):
    in_specs = (
        P("lat", "lon", None),
        P("lat", "lon", None),
        P("lat", "lon", None),
        P("lat", "lon", None),
        P("lat", "lon", None),
        P("lat"),
        P("lat", "lon", None),
        P(),
        P("lat", "lon", None),
    )
    out_specs = (P("lat", "lon", None), P("lat", "lon", None))
    return jax.shard_map(local, mesh=mesh, in_specs=in_specs, out_specs=out_specs, check_vma=False)
```
